32 devices in a mesh: batch: 4 (over x, core), seq: 8 (over z, y).
Axes of the slice: x: 2, y: 2, z: 4, core: 2. Of those that a mesh axis runs over, the one named last changes fastest.
Arguments:
- tokens: bfloat16 [4, 4096, 1024], P('batch', 'seq'), may hold values from -6 to 6
- lengths: int32 [4, 4], P('batch'), may hold values from 1 to 2048, 4096 in all within a row
- key_mask: int32 [4, 4096], P('batch'), may hold values 0 or 1
- cotangent: bfloat16 [4, 4096, 1024], P('batch', 'seq'), may hold values from -6 to 6
- w_qkv: bfloat16 [1024, 3072], P('seq'), may hold values from -0.1875 to 0.1875
- w_out: bfloat16 [1024, 1024], P('seq'), may hold values from -1 to 1
- w_up: bfloat16 [1024, 4096], P('seq'), may hold values from -0.1875 to 0.1875
- w_down: bfloat16 [4096, 1024], P('seq'), may hold values from -0.09375 to 0.09375
- ln1_gain: bfloat16 [1024], P('seq'), may hold values from 0.5 to 1.5
- ln1_bias: bfloat16 [1024], P('seq'), may hold values from -1 to 1
- ln2_gain: bfloat16 [1024], P('seq'), may hold values from 0.5 to 1.5
- ln2_bias: bfloat16 [1024], P('seq'), may hold values from -1 to 1
- out_bias: bfloat16 [1024], P('seq'), may hold values from -3 to 3
- up_bias: bfloat16 [4096], P('seq'), may hold values from -3 to 3
- down_bias: bfloat16 [1024], P('seq'), may hold values from -3 to 3
Outputs:
- output: bfloat16 [4, 4096, 1024], P('batch', 'seq')
- input_grad: bfloat16 [4, 4096, 1024], P('batch', 'seq')
- grad_qkv_w: float32 [1024, 3072], P('seq')
- grad_out_w: float32 [1024, 1024], P('seq')
- grad_up_w: float32 [1024, 4096], P('seq')
- grad_down_w: float32 [4096, 1024], P('seq')
- grad_ln1_gain: float32 [1024], P('seq')
- grad_ln1_bias: float32 [1024], P('seq')
- grad_ln2_gain: float32 [1024], P('seq')
- grad_ln2_bias: float32 [1024], P('seq')
- grad_out_bias: float32 [1024], P('seq')
- grad_up_bias: float32 [4096], P('seq')
- grad_down_bias: float32 [1024], P('seq')
The draws below stay inside these ranges and needn't reach their ends.
Inputs may be any that keep to these rules, and one draw needn't show every extreme that they name: Each row of lengths sums to 4096, and its longest utterance has exactly 2048 frames.
All inputs are finite; a program needn't handle non-finite values. No bound on the sum of `key_mask` on one device may be relied on, other than what follows from the above.
Results may differ from the reference program's by a relative error of at most 0.019.
Values may be sent and summed in bfloat16 or wider, within the bound.
No kernel may reach another device: no remote copies, remote signals or barrier semaphores. Data moves between devices by JAX's collectives and lax.ppermute only.
A program may use at most 256 MiB of HBM per device.

```python
import math
import jax
import jax.numpy as jnp
import numpy as np
from jax import lax

D = 1024
HEAD_COUNT = 16
HEAD_DIM = 64
FF = 4096
BUCKETS = 4
GROUP_TOK = 4096
MAXLEN = 2048
UTTS = 4


def set_ends(entries, key, least, high):
    extent = entries.shape
    index_at = [jax.random.randint(jax.random.fold_in(key, axis), (), 0, extent[axis]) for axis in range(len(extent))]
    entries = entries.at[tuple(index_at)].set(least)
    longest = extent.index(max(extent))
    index_at[longest] = (index_at[longest] + 1) % extent[longest]
    return entries.at[tuple(index_at)].set(high)


def block_levels(key, extent, split, low, high):
    level, own = 1.0, jax.random.fold_in(key, 6)
    for axis_at, parts in split:
        steps = jnp.exp(jax.random.uniform(jax.random.fold_in(own, axis_at), (parts,), jnp.float32, low / len(split), high / len(split)))
        level = level * jnp.repeat(steps, extent[axis_at] // parts).reshape([-1 if axis == axis_at else 1 for axis in range(len(extent))])
    return level


def split_up(count, total, bound, skew):
    loads = [(1 << 20) // math.isqrt(rank ** skew) + 1 for rank in range(2, count + 1)]
    surplus, counts = total - bound - (count - 1), [1] * (count - 1)
    while surplus > 0:
        movable = [i for i in range(count - 1) if counts[i] < bound]
        whole, budget = sum([loads[i] for i in movable]), surplus
        for i in movable:
            more = min(bound - counts[i], max(1, budget * loads[i] // whole), surplus)
            counts[i] = counts[i] + more
            surplus = surplus - more
    return np.array([bound] + counts)


def uneven_parts(own_key, amount, total, reach, skew):
    if amount == 2:
        one = jax.random.randint(own_key, (), max(1, total - reach), min(reach, total - 1) + 1)
        return jnp.stack([one, total - one])
    sizes = jnp.asarray(split_up(amount, total, reach, skew), jnp.int32)
    couples = (amount - 1) // 2
    giver, sink = sizes[1:1 + 2 * couples:2], sizes[2:2 + 2 * couples:2]
    slack = jnp.minimum(giver - 1, reach - sink)
    shifted = jax.random.randint(jax.random.fold_in(own_key, 1), (couples,), 0, 1 << 20) % (slack + 1)
    sizes = sizes.at[1:1 + 2 * couples:2].set(giver - shifted).at[2:2 + 2 * couples:2].set(sink + shifted)
    return sizes[jax.random.permutation(jax.random.fold_in(own_key, 2), amount)]


def noise(key, extent, scale, reach, cuts=(), kind=jnp.bfloat16):
    values = jax.random.normal(key, extent, jnp.float32) * scale
    if len(cuts) > 0:
        values = block_levels(key, extent, cuts, -0.22, 0.18) * values
    return jnp.clip(values, min=-reach, max=reach).astype(kind)


def setup_inputs(seed: int = 0) -> dict:
    key_of = jax.random.split(jax.random.key(seed), 16)
    tokens = noise(key_of[0], (BUCKETS, GROUP_TOK, D), 1.0, 6.0, ((0, 4), (1, 8)))
    lengths = jax.vmap(lambda own: uneven_parts(own, UTTS, GROUP_TOK, MAXLEN, 1))(jax.random.split(key_of[1], BUCKETS)).reshape((BUCKETS, UTTS)).astype(jnp.int32)
    key_mask = set_ends((jax.random.randint(key_of[2], (BUCKETS, GROUP_TOK), 0, 8) < 7).astype(jnp.int32), jax.random.fold_in(key_of[2], 1), 0, 1)
    cotangent = noise(key_of[3], (BUCKETS, GROUP_TOK, D), 1.0, 6.0, ((0, 4), (1, 8)))
    w_qkv = noise(key_of[4], (D, 3 * D), D ** -0.5, 0.1875, ((0, 8),))
    w_out = noise(key_of[5], (D, D), 32 ** -0.5, 1.0, ((0, 8),))
    w_up = noise(key_of[6], (D, FF), D ** -0.5, 0.1875, ((0, 8),))
    w_down = noise(key_of[7], (FF, D), FF ** -0.5, 0.09375, ((0, 8),))
    ln1_gain = jnp.clip(1.0 + 0.1 * jax.random.normal(key_of[8], (D,), jnp.float32), 0.5, 1.5).astype(jnp.bfloat16)
    ln1_bias = noise(key_of[9], (D,), 0.2, 1.0, ((0, 8),))
    ln2_gain = jnp.clip(1.0 + 0.1 * jax.random.normal(key_of[10], (D,), jnp.float32), 0.5, 1.5).astype(jnp.bfloat16)
    ln2_bias = noise(key_of[11], (D,), 0.2, 1.0, ((0, 8),))
    out_bias = noise(key_of[12], (D,), 0.5, 3.0, ((0, 8),))
    up_bias = noise(key_of[13], (FF,), 0.5, 3.0, ((0, 8),))
    down_bias = noise(key_of[14], (D,), 0.5, 3.0, ((0, 8),))
    return dict(tokens=tokens, lengths=lengths, key_mask=key_mask, cotangent=cotangent, w_qkv=w_qkv, w_out=w_out, w_up=w_up, w_down=w_down, ln1_gain=ln1_gain, ln1_bias=ln1_bias, ln2_gain=ln2_gain, ln2_bias=ln2_bias, out_bias=out_bias, up_bias=up_bias, down_bias=down_bias)


@jax.custom_vjp
def low(v):
    return lax.optimization_barrier(v.astype(jnp.bfloat16)).astype(jnp.float32)

@jax.custom_vjp
def low_back(v):
    return v

def low_keep(v):
    return (low(v), None)

def low_pass(kept, grad):
    return (grad,)

def back_keep(v):
    return (v, None)

def back_low(kept, grad):
    return (low(grad),)
low.defvjp(low_keep, low_pass)
low_back.defvjp(back_keep, back_low)
NEGATIVE = -1e+30
EPSILON = 1e-05

def norm_rows(values, gain, shift):
    centre = lax.optimization_barrier(jnp.mean(values, axis=-1, keepdims=True))
    centred = values - centre
    spread = lax.optimization_barrier(jnp.mean(centred * centred, axis=-1, keepdims=True))
    return centred * lax.rsqrt(spread + EPSILON) * gain + shift

def segment_ids(lengths_row, total):
    ends = jnp.cumsum(lengths_row).astype(jnp.int32)
    places = jnp.arange(total, dtype=jnp.int32)
    return lax.optimization_barrier(jnp.sum((places[:, None] >= ends[None, :]).astype(jnp.int32), axis=1))

def attend(qkv, seg, key_on):
    total = qkv.shape[0]
    block = min(1024, total)
    score_scale = HEAD_DIM ** (-0.5)
    highest = lax.Precision.HIGHEST
    keys_padded = jnp.concatenate([jnp.zeros((MAXLEN, 2 * D), jnp.float32), qkv[:, D:]], axis=0)
    seg_padded = jnp.concatenate([jnp.full((MAXLEN,), -1, jnp.int32), seg.astype(jnp.int32)])
    live_padded = jnp.concatenate([jnp.zeros((MAXLEN,), jnp.int32), key_on.astype(jnp.int32)])
    queries_all = qkv[:, :D]

    def one_block(start):
        queries = lax.dynamic_slice_in_dim(queries_all, start, block, 0).reshape(block, HEAD_COUNT, HEAD_DIM)
        window = lax.dynamic_slice_in_dim(keys_padded, start, block + MAXLEN, 0)
        keys = window[:, :D].reshape(block + MAXLEN, HEAD_COUNT, HEAD_DIM)
        values = window[:, D:].reshape(block + MAXLEN, HEAD_COUNT, HEAD_DIM)
        query_seg = lax.dynamic_slice_in_dim(seg.astype(jnp.int32), start, block)
        key_seg = lax.dynamic_slice_in_dim(seg_padded, start, block + MAXLEN)
        key_live = lax.dynamic_slice_in_dim(live_padded, start, block + MAXLEN)
        query_pos = start + jnp.arange(block, dtype=jnp.int32)
        key_pos = start - MAXLEN + jnp.arange(block + MAXLEN, dtype=jnp.int32)
        same = key_seg[None, :] == query_seg[:, None]
        causal = key_pos[None, :] <= query_pos[:, None]
        usable = (key_live[None, :] == 1) | (key_pos[None, :] == query_pos[:, None])
        allowed = same & causal & usable
        scores = low_back(jnp.einsum('qhd,khd->hqk', queries, keys, precision=highest)) * score_scale
        scores = jnp.where(allowed[None], scores, NEGATIVE)
        row_max = lax.optimization_barrier(jnp.max(scores, axis=2, keepdims=True))
        expo = jnp.exp(scores - row_max)
        probs = expo / lax.optimization_barrier(jnp.sum(expo, axis=2, keepdims=True))
        attended = jnp.einsum('hqk,khd->qhd', low(probs), values, precision=highest)
        return low_back(low(attended.reshape(block, D)))
    starts = jnp.arange(total // block, dtype=jnp.int32) * block
    return lax.map(jax.checkpoint(one_block), starts).reshape(total, D)

def group_forward(inputs, seg, key_on, weights):
    w_qkv, w_out, w_up, w_down, gain_one, shift_one, gain_two, shift_two, out_shift, up_shift, down_shift = weights
    highest = lax.Precision.HIGHEST
    normed_one = low(norm_rows(inputs, gain_one, shift_one))
    qkv = low_back(low(jnp.dot(normed_one, w_qkv, precision=highest)))
    attended = attend(qkv, seg, key_on)
    branch = low_back(jnp.dot(attended, w_out, precision=highest) + out_shift)
    middle = inputs + branch
    normed_two = low(norm_rows(middle, gain_two, shift_two))
    up_value = low_back(jnp.dot(normed_two, w_up, precision=highest) + up_shift)
    activated = low(jax.nn.gelu(up_value, approximate=False))
    return middle + jnp.dot(activated, w_down, precision=highest) + down_shift

def reference(tokens, lengths, key_mask, cotangent, w_qkv, w_out, w_up, w_down, ln1_gain, ln1_bias, ln2_gain, ln2_bias, out_bias, up_bias, down_bias):
    weights = tuple((member.astype(jnp.float32) for member in (w_qkv, w_out, w_up, w_down, ln1_gain, ln1_bias, ln2_gain, ln2_bias, out_bias, up_bias, down_bias)))
    segments = jax.vmap(lambda lengths_row: segment_ids(lengths_row, GROUP_TOK))(lengths)

    def whole(inputs, params):

        def one_group(packed):
            return group_forward(packed[0], packed[1], packed[2], params)
        return lax.map(jax.checkpoint(one_group), (inputs, segments, key_mask))
    result, pull = jax.vjp(whole, tokens.astype(jnp.float32), weights)
    grad_inputs, grads = pull(cotangent.astype(jnp.float32))
    return (result.astype(jnp.bfloat16), grad_inputs.astype(jnp.bfloat16), grads[0], grads[1], grads[2], grads[3], grads[4], grads[5], grads[6], grads[7], grads[8], grads[9], grads[10])
```

```python
import jax
import jax.numpy as jnp
from jax import lax
from jax.experimental import pallas as pl
from jax.experimental.pallas import tpu as pltpu
from jax.sharding import PartitionSpec as P

HEAD_COUNT = 16
HEAD_DIM = 64
MAXCAP = 2048


NEGATIVE = -1e30
EPSILON = 1e-05


def shifted(block, axis, distance):
    devices = range(lax.axis_size(axis))
    route = [(i - distance, i) for i in devices if i - distance in devices]
    return lax.ppermute(block, axis, route)


def norm_rows(values, gain, shift):
    centre = jnp.mean(values, axis=-1, keepdims=True)
    centred = values - centre
    spread = jnp.mean(centred * centred, axis=-1, keepdims=True)
    return centred * lax.rsqrt(spread + EPSILON) * gain + shift


def gelu_exact(values):
    return jax.nn.gelu(values, approximate=False)


def segment_ids(lengths_row, total):
    ends = jnp.cumsum(lengths_row)
    places = jnp.arange(total, dtype=jnp.int32)
    return jnp.sum((places[:, None] >= ends[None, :]).astype(jnp.int32), axis=1)


def times_trans(left, right):
    return lax.dot_general(
        left, right, (((1,), (1,)), ((), ())), preferred_element_type=jnp.float32
    )


def trans_times(left, right):
    return lax.dot_general(
        left, right, (((0,), (0,)), ((), ())), preferred_element_type=jnp.float32
    )


def head_split(matrix):
    return matrix.reshape(matrix.shape[0], HEAD_COUNT, HEAD_DIM)


def keep_same(carry):
    return carry


def block_allowed(my_index, offset, frames, seg_all, key_on, query_seg, query_pos):
    source = my_index - offset
    start = jnp.maximum(source, 0) * frames
    key_pos = source * frames + jnp.arange(frames, dtype=jnp.int32)
    key_seg = lax.dynamic_slice_in_dim(seg_all, start, frames)
    key_live = lax.dynamic_slice_in_dim(key_on, start, frames)
    same = key_seg[None, :] == query_seg[:, None]
    causal = (key_pos[None, :] <= query_pos[:, None]) & (key_pos[None, :] >= 0)
    usable = (key_live[None, :] == 1) | (key_pos[None, :] == query_pos[:, None])
    return same & causal & usable


def block_scores(queries, keys, allowed, score_scale):
    scores = (
        jnp.einsum(
            "qhd,khd->hqk",
            head_split(queries),
            head_split(keys),
            preferred_element_type=jnp.float32,
        )
        * score_scale
    )
    return jnp.where(allowed[None], scores, NEGATIVE)


def block_probs(queries, block, allowed, row_max, row_sum, score_scale):
    scores = block_scores(queries, block[:, : queries.shape[1]], allowed, score_scale)
    return jnp.exp(scores - row_max[:, :, None]) / row_sum[:, :, None]


def forward_chain(kv_own, reach):
    blocks = [kv_own]
    moving = kv_own
    for offset in range(reach):
        moving = shifted(moving, "seq", 1)
        blocks.append(moving)
    return blocks


def again_chain(kv_own, reach):
    blocks = [kv_own]
    moving = kv_own
    for offset in range(reach):
        moving = shifted(moving, "seq", 1)
        blocks.append(moving)
    return blocks


def softmax_stats(queries, blocks, allowed_list, live_list, score_scale):
    frames, model_width = queries.shape
    row_max = jnp.full((HEAD_COUNT, frames), NEGATIVE, jnp.float32)
    row_sum = jnp.zeros((HEAD_COUNT, frames), jnp.float32)
    for offset in range(len(blocks)):

        def softmax_update(carry, block=blocks[offset], allowed=allowed_list[offset]):
            old_max, old_sum = carry
            scores = block_scores(queries, block[:, :model_width], allowed, score_scale)
            new_max = jnp.maximum(old_max, jnp.max(scores, axis=2))
            new_sum = old_sum * jnp.exp(old_max - new_max) + jnp.sum(
                jnp.exp(scores - new_max[:, :, None]), axis=2
            )
            return (new_max, new_sum)

        row_max, row_sum = lax.cond(
            live_list[offset], softmax_update, keep_same, (row_max, row_sum)
        )
    return (row_max, row_sum)


def attend_values(queries, blocks, allowed_list, live_list, row_max, row_sum, score_scale):
    frames, model_width = queries.shape
    total = jnp.zeros((frames, HEAD_COUNT, HEAD_DIM), jnp.float32)
    for offset in range(len(blocks)):

        def attend_update(carry, block=blocks[offset], allowed=allowed_list[offset]):
            probs = block_probs(queries, block, allowed, row_max, row_sum, score_scale).astype(
                jnp.bfloat16
            )
            return carry + jnp.einsum(
                "hqk,khd->qhd",
                probs,
                head_split(block[:, model_width:]),
                preferred_element_type=jnp.float32,
            )

        total = lax.cond(live_list[offset], attend_update, keep_same, total)
    return total.reshape(frames, model_width).astype(jnp.bfloat16)


def attention_grads(
    queries, grad_attended, blocks, allowed_list, live_list, row_max, row_sum, score_scale
):
    frames, model_width = queries.shape
    grad_heads = head_split(grad_attended)
    query_heads = head_split(queries)
    delta = jnp.zeros((HEAD_COUNT, frames), jnp.float32)
    for offset in range(len(blocks)):

        def attention_update(carry, block=blocks[offset], allowed=allowed_list[offset]):
            probs = block_probs(queries, block, allowed, row_max, row_sum, score_scale)
            dprobs = jnp.einsum(
                "qhd,khd->hqk",
                grad_heads,
                head_split(block[:, model_width:]),
                preferred_element_type=jnp.float32,
            )
            return carry + jnp.sum(probs * dprobs, axis=2)

        delta = lax.cond(live_list[offset], attention_update, keep_same, delta)
    grad_queries = jnp.zeros((frames, HEAD_COUNT, HEAD_DIM), jnp.float32)
    contributions = []
    for offset in range(len(blocks)):

        def block_grads(block=blocks[offset], allowed=allowed_list[offset]):
            probs = block_probs(queries, block, allowed, row_max, row_sum, score_scale)
            value_heads = head_split(block[:, model_width:])
            dprobs = jnp.einsum(
                "qhd,khd->hqk", grad_heads, value_heads, preferred_element_type=jnp.float32
            )
            dscores = (probs * (dprobs - delta[:, :, None]) * score_scale).astype(jnp.bfloat16)
            query_part = jnp.einsum(
                "hqk,khd->qhd",
                dscores,
                head_split(block[:, :model_width]),
                preferred_element_type=jnp.float32,
            )
            key_part = jnp.einsum(
                "hqk,qhd->khd", dscores, query_heads, preferred_element_type=jnp.float32
            )
            value_part = jnp.einsum(
                "hqk,qhd->khd",
                probs.astype(jnp.bfloat16),
                grad_heads,
                preferred_element_type=jnp.float32,
            )
            joined = jnp.concatenate(
                [key_part.reshape(frames, model_width), value_part.reshape(frames, model_width)],
                axis=1,
            )
            return (query_part, joined)

        def no_grads():
            return (
                jnp.zeros((frames, HEAD_COUNT, HEAD_DIM), jnp.float32),
                jnp.zeros((frames, 2 * model_width), jnp.float32),
            )

        query_part, joined = lax.cond(live_list[offset], block_grads, no_grads)
        grad_queries = grad_queries + query_part
        contributions.append(joined)
    return (grad_queries.reshape(frames, model_width), contributions)


def shards(
    tokens,
    lengths,
    key_mask,
    cotangent,
    w_qkv,
    w_out,
    w_up,
    w_down,
    ln1_gain,
    ln1_bias,
    ln2_gain,
    ln2_bias,
    out_bias,
    up_bias,
    down_bias,
):
    gathered = (
        lax.all_gather(w_qkv, "seq", axis=0, tiled=True),
        lax.all_gather(w_out, "seq", axis=0, tiled=True),
        lax.all_gather(w_up, "seq", axis=0, tiled=True),
        lax.all_gather(w_down, "seq", axis=0, tiled=True),
        lax.all_gather(ln1_gain, "seq", axis=0, tiled=True),
        lax.all_gather(ln1_bias, "seq", axis=0, tiled=True),
        lax.all_gather(ln2_gain, "seq", axis=0, tiled=True),
        lax.all_gather(ln2_bias, "seq", axis=0, tiled=True),
        lax.all_gather(out_bias, "seq", axis=0, tiled=True),
        lax.all_gather(up_bias, "seq", axis=0, tiled=True),
        lax.all_gather(down_bias, "seq", axis=0, tiled=True),
    )
    qkv_full, out_full, up_full, down_full = (gathered[0], gathered[1], gathered[2], gathered[3])
    gain_one, shift_one, gain_two, shift_two, out_shift, up_shift, down_shift = tuple(
        (member.astype(jnp.float32) for member in gathered[4:])
    )
    frames = tokens.shape[1]
    model_width = tokens.shape[2]
    cycle_size = lax.axis_size("seq")
    group_frames = frames * cycle_size
    longest = min(MAXCAP, group_frames // 2)
    reach = longest // frames
    my_index = lax.axis_index("seq")
    score_scale = HEAD_DIM ** (-0.5)
    seg_all = segment_ids(lengths[0], group_frames)
    key_on = key_mask[0]
    query_pos = my_index * frames + jnp.arange(frames, dtype=jnp.int32)
    query_seg = lax.dynamic_slice_in_dim(seg_all, my_index * frames, frames)
    allowed_list = [
        block_allowed(my_index, offset, frames, seg_all, key_on, query_seg, query_pos)
        for offset in range(reach + 1)
    ]
    live_list = [jnp.any(allowed) for allowed in allowed_list]
    inputs = tokens[0].astype(jnp.float32)
    normed_one = norm_rows(inputs, gain_one, shift_one).astype(jnp.bfloat16)
    qkv_low = jnp.dot(normed_one, qkv_full, preferred_element_type=jnp.float32).astype(jnp.bfloat16)
    queries = qkv_low[:, :model_width]
    kv_own = qkv_low[:, model_width:]
    blocks = forward_chain(kv_own, reach)
    row_max, row_sum = softmax_stats(queries, blocks, allowed_list, live_list, score_scale)
    attended = attend_values(
        queries, blocks, allowed_list, live_list, row_max, row_sum, score_scale
    )
    branch = jnp.dot(attended, out_full, preferred_element_type=jnp.float32) + out_shift
    middle = inputs + branch
    normed_two = norm_rows(middle, gain_two, shift_two).astype(jnp.bfloat16)
    up_value = jnp.dot(normed_two, up_full, preferred_element_type=jnp.float32) + up_shift
    activated = gelu_exact(up_value).astype(jnp.bfloat16)
    result = middle + jnp.dot(activated, down_full, preferred_element_type=jnp.float32) + down_shift
    grad_result = cotangent[0]
    grad_down_w = trans_times(activated, grad_result)
    grad_down_b = jnp.sum(grad_result.astype(jnp.float32), axis=0)
    grad_act = times_trans(grad_result, down_full)
    grad_up = jax.vjp(gelu_exact, up_value)[1](grad_act)[0].astype(jnp.bfloat16)
    grad_up_w = trans_times(normed_two, grad_up)
    grad_up_b = jnp.sum(grad_up.astype(jnp.float32), axis=0)
    grad_normed_two = times_trans(grad_up, up_full)
    pull_two = jax.vjp(norm_rows, middle, gain_two, shift_two)[1]
    grad_mid_norm, grad_gain_two, grad_shift_two = pull_two(grad_normed_two)
    grad_middle = grad_result.astype(jnp.float32) + grad_mid_norm
    grad_branch = grad_middle.astype(jnp.bfloat16)
    grad_out_w = trans_times(attended, grad_branch)
    grad_out_b = jnp.sum(grad_branch.astype(jnp.float32), axis=0)
    grad_attended = times_trans(grad_branch, out_full).astype(jnp.bfloat16)
    back_blocks = again_chain(kv_own, reach)
    grad_queries, contributions = attention_grads(
        queries, grad_attended, back_blocks, allowed_list, live_list, row_max, row_sum, score_scale
    )
    flowing = contributions[reach]
    for offset in range(reach - 1, -1, -1):
        flowing = (
            shifted(flowing.astype(jnp.bfloat16), "seq", -1).astype(flowing.dtype)
            + contributions[offset]
        )
    grad_qkv = jnp.concatenate([grad_queries, flowing], axis=1).astype(jnp.bfloat16)
    grad_qkv_w = trans_times(normed_one, grad_qkv)
    grad_normed_one = times_trans(grad_qkv, qkv_full)
    pull_one = jax.vjp(norm_rows, inputs, gain_one, shift_one)[1]
    grad_in_norm, grad_gain_one, grad_shift_one = pull_one(grad_normed_one)
    grad_inputs = (grad_middle + grad_in_norm).astype(jnp.bfloat16)
    shares = (
        lax.psum_scatter(
            grad_qkv_w.astype(jnp.bfloat16), "seq", scatter_dimension=0, tiled=True
        ).astype(jnp.float32),
        lax.psum_scatter(
            grad_out_w.astype(jnp.bfloat16), "seq", scatter_dimension=0, tiled=True
        ).astype(jnp.float32),
        lax.psum_scatter(
            grad_up_w.astype(jnp.bfloat16), "seq", scatter_dimension=0, tiled=True
        ).astype(jnp.float32),
        lax.psum_scatter(
            grad_down_w.astype(jnp.bfloat16), "seq", scatter_dimension=0, tiled=True
        ).astype(jnp.float32),
        lax.psum_scatter(
            grad_gain_one.astype(jnp.bfloat16), "seq", scatter_dimension=0, tiled=True
        ).astype(jnp.float32),
        lax.psum_scatter(
            grad_shift_one.astype(jnp.bfloat16), "seq", scatter_dimension=0, tiled=True
        ).astype(jnp.float32),
        lax.psum_scatter(
            grad_gain_two.astype(jnp.bfloat16), "seq", scatter_dimension=0, tiled=True
        ).astype(jnp.float32),
        lax.psum_scatter(
            grad_shift_two.astype(jnp.bfloat16), "seq", scatter_dimension=0, tiled=True
        ).astype(jnp.float32),
        lax.psum_scatter(
            grad_out_b.astype(jnp.bfloat16), "seq", scatter_dimension=0, tiled=True
        ).astype(jnp.float32),
        lax.psum_scatter(
            grad_up_b.astype(jnp.bfloat16), "seq", scatter_dimension=0, tiled=True
        ).astype(jnp.float32),
        lax.psum_scatter(
            grad_down_b.astype(jnp.bfloat16), "seq", scatter_dimension=0, tiled=True
        ).astype(jnp.float32),
    )
    reduced = (
        lax.psum(shares[0].astype(jnp.bfloat16), "batch").astype(jnp.float32),
        lax.psum(shares[1].astype(jnp.bfloat16), "batch").astype(jnp.float32),
        lax.psum(shares[2].astype(jnp.bfloat16), "batch").astype(jnp.float32),
        lax.psum(shares[3].astype(jnp.bfloat16), "batch").astype(jnp.float32),
        lax.psum(shares[4].astype(jnp.bfloat16), "batch").astype(jnp.float32),
        lax.psum(shares[5].astype(jnp.bfloat16), "batch").astype(jnp.float32),
        lax.psum(shares[6].astype(jnp.bfloat16), "batch").astype(jnp.float32),
        lax.psum(shares[7].astype(jnp.bfloat16), "batch").astype(jnp.float32),
        lax.psum(shares[8].astype(jnp.bfloat16), "batch").astype(jnp.float32),
        lax.psum(shares[9].astype(jnp.bfloat16), "batch").astype(jnp.float32),
        lax.psum(shares[10].astype(jnp.bfloat16), "batch").astype(jnp.float32),
    )
    return (
        result.astype(jnp.bfloat16)[None],
        grad_inputs[None],
        reduced[0],
        reduced[1],
        reduced[2],
        reduced[3],
        reduced[4],
        reduced[5],
        reduced[6],
        reduced[7],
        reduced[8],
        reduced[9],
        reduced[10],
    )


LANES = 128
TILE = 512
UTTERANCES = 4
SHRINK = 1
PARAMS = pltpu.CompilerParams(dimension_semantics=("arbitrary",), vmem_limit_bytes=56 << 20)


def dot_nt(left, right):
    return lax.dot_general(
        left, right, (((1,), (1,)), ((), ())), preferred_element_type=jnp.float32
    )


def dot_nn(left, right):
    return lax.dot_general(
        left, right, (((1,), (0,)), ((), ())), preferred_element_type=jnp.float32
    )


def dot_tn(left, right):
    return lax.dot_general(
        left, right, (((0,), (0,)), ((), ())), preferred_element_type=jnp.float32
    )


def norm_stats(values):
    centre = jnp.mean(values, axis=-1, keepdims=True)
    centred = values - centre
    spread = jnp.mean(centred * centred, axis=-1, keepdims=True)
    inverse = lax.rsqrt(spread + EPSILON)
    return centred * inverse, inverse


def norm_back(grad, normed, inverse, gain):
    g = grad * gain
    return inverse * (
        g
        - jnp.mean(g, axis=-1, keepdims=True)
        - normed * jnp.mean(g * normed, axis=-1, keepdims=True)
    )


def whole(*shape):
    return pl.BlockSpec(shape, lambda *_: (0,) * len(shape))


def like(shape, kind):
    return jax.ShapeDtypeStruct(shape, kind)


def call(kernel, name, grid, in_specs, out_specs, out_shape, scratch=(), flops=0):
    def run(ids, *args):
        bytes_accessed = sum(a.size * a.dtype.itemsize for a in args)
        return pl.pallas_call(
            kernel,
            out_shape=out_shape,
            grid_spec=pltpu.PrefetchScalarGridSpec(
                num_scalar_prefetch=1,
                grid=(grid,),
                in_specs=in_specs,
                out_specs=out_specs,
                scratch_shapes=list(scratch),
            ),
            compiler_params=PARAMS,
            cost_estimate=pl.CostEstimate(
                flops=flops // SHRINK,
                bytes_accessed=2 * bytes_accessed // SHRINK,
                transcendentals=0,
            ),
            name=name,
        )(ids, *args)

    return run


CORE, CHIP_X, SQUARE, Y_BIT = 0, 1, 2, 3


def norm_kernel(ids, tokens, vectors, out):
    normed, _ = norm_stats(tokens[...].astype(jnp.float32))
    out[...] = (normed * vectors[0:1, :] + vectors[1:2, :]).astype(jnp.bfloat16)


def project_kernel(ids, own, y_one, z_one, top, bottom, w_own, w_other, out, leaving, natural):
    square = ids[SQUARE]
    width = own.shape[1]
    part = width // 8
    weights = [w[:, 0:part, :].reshape(width, 3 * LANES) for w in (w_own, w_other)]
    corner = jnp.where(pl.program_id(0) < 2, top[...], bottom[...])
    for j, rows in enumerate((own[...], y_one[...], z_one[...], corner)):
        at = pl.ds(square ^ j, 1)
        natural[at] = rows[None]
        out[at] = dot_nn(rows, weights[0]).astype(jnp.bfloat16)[None]
        leaving[at] = dot_nn(rows, weights[1]).astype(jnp.bfloat16)[None]


def head_lanes(block, head):
    lane = lax.broadcasted_iota(jnp.int32, block.shape, 1)
    keep = (lane < HEAD_DIM) if head == 0 else (lane >= HEAD_DIM)
    return jnp.where(keep, block, jnp.zeros_like(block))


def join_heads(ids, own, came, qkv):
    half = own.shape[0]
    for rows, side in ((own, ids[CORE]), (came, 1 - ids[CORE])):
        at = pl.ds(pl.multiple_of(side * half, half), half)
        qkv[at, 0:LANES] = rows[:, 0:LANES] * jnp.bfloat16(HEAD_DIM ** (-0.5))
        qkv[at, LANES : 3 * LANES] = rows[:, LANES : 3 * LANES]


def first_frames(bounds, positions):
    start = jnp.zeros_like(positions)
    for u in range(1, UTTERANCES):
        start = jnp.where(positions >= bounds[4, u], bounds[4, u], start)
    return start


def attend_kernel(ids, bounds, own, came, bias_row, out, lse, qkv, top, total, acc):
    tile = pl.program_id(0)
    base = pl.multiple_of(tile * TILE, TILE)

    @pl.when(tile == 0)
    def _():
        join_heads(ids, own, came, qkv)

    queries = [head_lanes(qkv[pl.ds(base, TILE), 0:LANES], head) for head in range(2)]
    top[...] = jnp.full_like(top, NEGATIVE)
    total[...] = jnp.zeros_like(total)
    acc[...] = jnp.zeros_like(acc)

    def step(j, masked):
        at = pl.multiple_of(j * TILE, TILE)
        keys = qkv[pl.ds(at, TILE), LANES : 2 * LANES]
        values = qkv[pl.ds(at, TILE), 2 * LANES : 3 * LANES]
        bias = bias_row[:, pl.ds(at, TILE)]
        if masked:
            key_pos = at + lax.broadcasted_iota(jnp.int32, (TILE, TILE), 1)
            query_pos = base + lax.broadcasted_iota(jnp.int32, (TILE, TILE), 0)
            column = base + lax.broadcasted_iota(jnp.int32, (TILE, 1), 0)
            allowed = (
                (key_pos >= first_frames(bounds, column))
                & (key_pos <= query_pos)
                & ((bias == 0.0) | (key_pos == query_pos))
            )
        for head in range(2):
            scores = dot_nt(queries[head], keys)
            if masked:
                scores = jnp.where(allowed, scores, NEGATIVE)
            else:
                scores = scores + bias
            old = top[head]
            new = jnp.maximum(old, jnp.max(scores, axis=1, keepdims=True))
            probs = jnp.exp(scores - new[:, 0:1])
            shrink = jnp.exp(old - new)
            total[head] = total[head] * shrink + jnp.sum(probs, axis=1, keepdims=True)
            acc[head] = acc[head] * shrink + dot_nn(probs.astype(jnp.bfloat16), values)
            top[head] = new

    def masked_step(j, carry):
        step(j, True)
        return carry

    def free_step(j, carry):
        step(j, False)
        return carry

    lax.fori_loop(bounds[0, tile], bounds[1, tile], masked_step, 0)
    lax.fori_loop(bounds[1, tile], tile, free_step, 0)
    step(tile, True)
    lane = lax.broadcasted_iota(jnp.int32, (TILE, LANES), 1)
    out[0] = jnp.where(lane < HEAD_DIM, acc[0] / total[0], acc[1] / total[1]).astype(jnp.bfloat16)
    for head in range(2):
        column = top[head] + jnp.log(total[head])
        lse[head : head + 1, pl.ds(base, TILE)] = jnp.transpose(column)[0:1, :]


def block_order(i):
    return 2 * (i % 4) + i // 4


def attend(ids, bounds, own, came, bias_row):
    rows = 2 * own.shape[0]
    return pl.pallas_call(
        attend_kernel,
        out_shape=(like((8, TILE, LANES), jnp.bfloat16), like((2, rows), jnp.float32)),
        grid_spec=pltpu.PrefetchScalarGridSpec(
            num_scalar_prefetch=2,
            grid=(rows // TILE,),
            in_specs=[
                whole(*own.shape),
                whole(*came.shape),
                whole(1, rows),
            ],
            out_specs=[
                pl.BlockSpec((1, TILE, LANES), lambda i, *_: (block_order(i), 0, 0)),
                whole(2, rows),
            ],
            scratch_shapes=[pltpu.VMEM((rows, 3 * LANES), jnp.bfloat16)]
            + [pltpu.VMEM((2, TILE, LANES), jnp.float32)] * 3,
        ),
        compiler_params=PARAMS,
        cost_estimate=pl.CostEstimate(
            flops=rows * rows * 256 // SHRINK, bytes_accessed=rows * 2400, transcendentals=rows * rows
        ),
        name="attend",
    )(ids, bounds, own, came, bias_row)


def attend_back_kernel(
    ids,
    bounds,
    own,
    came,
    grad_own,
    grad_came,
    attended,
    bias_row,
    lse,
    out,
    leaving,
    qkv,
    grad,
    delta,
    grad_queries,
    grad_kv,
):
    tile = pl.program_id(0)
    base = pl.multiple_of(tile * TILE, TILE)
    core = ids[CORE]

    @pl.when(tile == 0)
    def _():
        join_heads(ids, own, came, qkv)
        grad_queries[...] = jnp.zeros_like(grad_queries)
        for j in range(4):
            for rows, side in ((grad_own, core), (grad_came, 1 - core)):
                at = pl.multiple_of((4 * side + j) * TILE, TILE)
                block = rows[pl.ds(2 * j + core, 1)].reshape(TILE, LANES)
                grad[pl.ds(at, TILE), :] = block
                product = block.astype(jnp.float32) * attended[
                    pl.ds(2 * j + side, 1)
                ].reshape(TILE, LANES).astype(jnp.float32)
                turned = jnp.transpose(product)
                delta[0:1, pl.ds(at, TILE)] = jnp.sum(turned[:HEAD_DIM], axis=0, keepdims=True)
                delta[1:2, pl.ds(at, TILE)] = jnp.sum(turned[HEAD_DIM:], axis=0, keepdims=True)

    keys = qkv[pl.ds(base, TILE), LANES : 2 * LANES]
    values = qkv[pl.ds(base, TILE), 2 * LANES : 3 * LANES]
    head_keys = [head_lanes(keys, head) for head in range(2)]
    bias = jnp.broadcast_to(bias_row[:, pl.ds(base, TILE)], (LANES, TILE))
    bias = jnp.transpose(bias)[:, 0:1]
    grad_kv[...] = jnp.zeros_like(grad_kv)

    def step(i, masked):
        at = pl.multiple_of(i * TILE, TILE)
        scaled = qkv[pl.ds(at, TILE), 0:LANES]
        grads = grad[pl.ds(at, TILE), :]
        if masked:
            key_pos = base + lax.broadcasted_iota(jnp.int32, (TILE, TILE), 0)
            query_pos = at + lax.broadcasted_iota(jnp.int32, (TILE, TILE), 1)
            row = at + lax.broadcasted_iota(jnp.int32, (1, TILE), 1)
            allowed = (
                (key_pos >= first_frames(bounds, row))
                & (key_pos <= query_pos)
                & ((bias == 0.0) | (key_pos == query_pos))
            )
        query_part = jnp.zeros((TILE, LANES), jnp.float32)
        key_part = grad_kv[0]
        value_part = grad_kv[1]
        for head in range(2):
            queries = head_lanes(scaled, head)
            head_grads = head_lanes(grads, head)
            scores = dot_nt(keys, queries)
            if masked:
                scores = jnp.where(allowed, scores, NEGATIVE)
            else:
                scores = scores + bias
            probs = jnp.exp(scores - lse[head : head + 1, pl.ds(at, TILE)])
            dprobs = dot_nt(values, head_grads)
            dscores = (probs * (dprobs - delta[head : head + 1, pl.ds(at, TILE)])).astype(
                jnp.bfloat16
            )
            value_part = value_part + dot_nn(probs.astype(jnp.bfloat16), head_grads)
            key_part = key_part + dot_nn(dscores, queries)
            query_part = query_part + dot_tn(dscores, head_keys[head])
        grad_kv[0] = key_part
        grad_kv[1] = value_part
        grad_queries[pl.ds(at, TILE), :] += query_part

    def masked_step(i, carry):
        step(i, True)
        return carry

    def free_step(i, carry):
        step(i, False)
        return carry

    step(tile, True)
    lax.fori_loop(tile + 1, bounds[2, tile], free_step, 0)
    lax.fori_loop(bounds[2, tile], bounds[3, tile], masked_step, 0)

    def store(target):
        at = pl.ds(pl.multiple_of((tile % 4) * TILE, TILE), TILE)
        target[at, 0:LANES] = (
            grad_queries[pl.ds(base, TILE), :] * HEAD_DIM ** (-0.5)
        ).astype(jnp.bfloat16)
        target[at, LANES : 2 * LANES] = grad_kv[0].astype(jnp.bfloat16)
        target[at, 2 * LANES : 3 * LANES] = grad_kv[1].astype(jnp.bfloat16)

    @pl.when(tile // 4 == core)
    def _():
        store(out)

    @pl.when(tile // 4 != core)
    def _():
        store(leaving)


def attend_back(ids, bounds, own, came, grad_own, grad_came, attended, bias_row, lse):
    half = own.shape[0]
    rows = 2 * half
    return pl.pallas_call(
        attend_back_kernel,
        out_shape=(like(own.shape, jnp.bfloat16), like(own.shape, jnp.bfloat16)),
        grid_spec=pltpu.PrefetchScalarGridSpec(
            num_scalar_prefetch=2,
            grid=(rows // TILE,),
            in_specs=[
                whole(*own.shape),
                whole(*came.shape),
                whole(*grad_own.shape),
                whole(*grad_came.shape),
                whole(*attended.shape),
                whole(1, rows),
                whole(2, rows),
            ],
            out_specs=[whole(*own.shape), whole(*own.shape)],
            scratch_shapes=[
                pltpu.VMEM((rows, 3 * LANES), jnp.bfloat16),
                pltpu.VMEM((rows, LANES), jnp.bfloat16),
                pltpu.VMEM((2, rows), jnp.float32),
                pltpu.VMEM((rows, LANES), jnp.float32),
                pltpu.VMEM((2, TILE, LANES), jnp.float32),
            ],
        ),
        compiler_params=PARAMS,
        cost_estimate=pl.CostEstimate(
            flops=rows * rows * 640 // SHRINK, bytes_accessed=rows * 2400, transcendentals=rows * rows
        ),
        name="attend_back",
    )(ids, bounds, own, came, grad_own, grad_came, attended, bias_row, lse)


def attend_bounds(start, starts, rows):
    tiles = rows // TILE
    index = jnp.arange(tiles, dtype=jnp.int32)
    first = start[:: TILE]
    last = start[TILE - 1 :: TILE]
    low = first // TILE
    middle = jnp.clip((last + TILE - 1) // TILE, low, index)
    key_first = index * TILE
    free_end = jnp.sum((last[None, :] <= key_first[:, None]).astype(jnp.int32), axis=1)
    free_end = jnp.maximum(free_end, index + 1)
    far_end = jnp.sum(
        (first[None, :] <= key_first[:, None] + TILE - 1).astype(jnp.int32), axis=1
    )
    starts = jnp.pad(starts, (0, tiles - starts.shape[0]))
    return jnp.stack([low, middle, free_end, far_end, starts]).astype(jnp.int32)


def out_kernel(ids, own, came, tokens, w_out, vectors, attended, middle, normed):
    core = ids[CORE]
    rows, width = tokens.shape
    mine, other = [], []
    for j in range(4):
        mine.append(own[pl.ds(2 * j + core, 1)].reshape(rows, LANES))
        other.append(came[pl.ds(2 * j + core, 1)].reshape(rows, LANES))
    mine, other = jnp.concatenate(mine, axis=1), jnp.concatenate(other, axis=1)
    first = jnp.where(core == 0, mine, other)
    second = jnp.where(core == 0, other, mine)
    joined = jnp.concatenate([first, second], axis=1)
    attended[...] = joined
    branch = dot_nn(joined, w_out[...].reshape(width, width)) + vectors[4:5, :]
    value = tokens[...].astype(jnp.float32) + branch
    middle[...] = value
    xhat, _ = norm_stats(value)
    normed[...] = (xhat * vectors[2:3, :] + vectors[3:4, :]).astype(jnp.bfloat16)


def forward_kernel(
    ids,
    normed_own,
    normed_came,
    grad_own,
    grad_came,
    up_a,
    up_b,
    down_a,
    down_b,
    vectors,
    act,
    grad_up,
    up_bias,
    result_own,
    result_came,
    back_own,
    back_came,
    result,
    back,
):
    step = pl.program_id(0)
    core = ids[CORE]
    frames, width = normed_own.shape

    @pl.when(step == 0)
    def _():
        result[...] = jnp.zeros_like(result)
        back[...] = jnp.zeros_like(back)

    w_up = jnp.concatenate(
        [up_a[...].reshape(width, LANES), up_b[...].reshape(width, LANES)], axis=1
    )
    w_down = jnp.concatenate(
        [down_a[...].reshape(LANES, width), down_b[...].reshape(LANES, width)], axis=0
    )
    shift = jnp.where(
        core == 0,
        jnp.concatenate([vectors[6:7, :], vectors[7:8, :]], axis=1),
        jnp.concatenate([vectors[8:9, :], vectors[9:10, :]], axis=1),
    )
    bias = jnp.zeros((1, 2 * LANES), jnp.float32)
    for side, (normed, grad) in enumerate(((normed_own, grad_own), (normed_came, grad_came))):
        value = dot_nn(normed[...], w_up) + shift
        half = 0.5 + 0.5 * lax.erf(value * 0.7071067811865476)
        bell = jnp.exp(-0.5 * value * value) * 0.3989422804014327
        activated = (value * half).astype(jnp.bfloat16)
        act[side] = activated
        change = dot_nt(grad[...], w_down) * (half + value * bell)
        bias = bias + jnp.sum(change.astype(jnp.bfloat16).astype(jnp.float32), axis=0, keepdims=True)
        change = change.astype(jnp.bfloat16)
        grad_up[side] = change
        result[side] += dot_nn(activated, w_down)
        back[side] += dot_nt(change, w_up)
    up_bias[0:1, :] = bias[:, 0:LANES]
    up_bias[1:2, :] = bias[:, LANES:]

    @pl.when(step == 7)
    def _():
        result_own[...] = result[0]
        result_came[...] = result[1].astype(jnp.bfloat16)
        back_own[...] = back[0]
        back_came[...] = back[1].astype(jnp.bfloat16)


def middle_kernel(
    ids, back_own, back_came, middle, cotangent, w_out, vectors, grad_middle, grad_branch, out, sums
):
    step = pl.program_id(0)
    xhat, inverse = norm_stats(middle[...])
    grad = back_own[...] + back_came[...].astype(jnp.float32)
    value = cotangent[...].astype(jnp.float32) + norm_back(grad, xhat, inverse, vectors[2:3, :])
    grad_middle[...] = value
    low = value.astype(jnp.bfloat16)
    grad_branch[...] = low

    @pl.when(step == 0)
    def _():
        sums[...] = jnp.zeros_like(sums)

    sums[0:1, :] += jnp.sum(grad * xhat, axis=0, keepdims=True)
    sums[1:2, :] += jnp.sum(grad, axis=0, keepdims=True)
    sums[2:3, :] += jnp.sum(low.astype(jnp.float32), axis=0, keepdims=True)
    sums[3:4, :] += jnp.sum(cotangent[...].astype(jnp.float32), axis=0, keepdims=True)
    width = w_out.shape[-1]
    spread = dot_nt(low, w_out[...].reshape(width, width)).astype(jnp.bfloat16)
    for group in range(8):
        out[block_order(group)] = spread[:, group * LANES : (group + 1) * LANES]


def grad_out_kernel(ids, attended, grad_branch, kept, leaving):
    core = ids[CORE]
    grad = dot_tn(attended[...], grad_branch[...]).astype(jnp.bfloat16)
    half = grad.shape[1] // 2
    shape = kept.shape
    kept[...] = jnp.where(core == 0, grad[:, :half], grad[:, half:]).reshape(shape)
    leaving[...] = jnp.where(core == 0, grad[:, half:], grad[:, :half]).reshape(shape)


def grad_down_kernel(ids, act, grad_own, grad_came, out):
    grad = dot_tn(act[0], grad_own[...]) + dot_tn(act[1], grad_came[...])
    out[...] = grad.astype(jnp.bfloat16)


def grad_up_kernel(ids, normed_own, normed_came, grad_up, out_own, out_came, kept, leaving):
    chip_x = ids[CHIP_X]
    grad = (dot_tn(normed_own[...], grad_up[0]) + dot_tn(normed_came[...], grad_up[1])).astype(
        jnp.bfloat16
    )
    half = grad.shape[1] // 2
    shape = kept.shape[:2] + (half,)
    kept[:, :, :half] = jnp.where(chip_x == 0, grad[:, :half], grad[:, half:]).reshape(shape)
    leaving[:, :, :half] = jnp.where(chip_x == 0, grad[:, half:], grad[:, :half]).reshape(shape)
    more = (out_own[...].astype(jnp.float32) + out_came[...].astype(jnp.float32)).astype(
        jnp.bfloat16
    )
    cut = more.shape[2] // 2
    kept[:, :, half:] = jnp.where(chip_x == 0, more[:, :, :cut], more[:, :, cut:])
    leaving[:, :, half:] = jnp.where(chip_x == 0, more[:, :, cut:], more[:, :, :cut])


def back_project_kernel(ids, own, came, w_own, w_other, first, y_out, z_out, keep_left, keep_right):
    square = ids[SQUARE]
    width = first.shape[1]
    part = width // 8
    half = width // 2
    weights = [w[:, 0:part, :].reshape(width, 3 * LANES) for w in (w_own, w_other)]
    for j in range(4):
        at = square ^ j
        value = dot_nt(own[at], weights[0]) + dot_nt(came[at], weights[1])
        if j == 0:
            first[...] = value
        if j == 1:
            y_out[0] = value[:, :half].astype(jnp.bfloat16)
            keep_right[...] = value[:, half:]
        if j == 2:
            z_out[0] = value[:, half:].astype(jnp.bfloat16)
            keep_left[...] = value[:, :half]
        if j == 3:
            y_out[1] = value[:, :half].astype(jnp.bfloat16)
            z_out[1] = value[:, half:].astype(jnp.bfloat16)


def second_kernel(ids, keep_left, keep_right, y_came, z_came, z_out, y_out):
    z_out[...] = (keep_left[...] + y_came[1].astype(jnp.float32)).astype(jnp.bfloat16)
    y_out[...] = (keep_right[...] + z_came[1].astype(jnp.float32)).astype(jnp.bfloat16)


def last_kernel(
    ids, first, y_came, z_came, z_second, y_second, tokens, grad_middle, vectors, out, sums
):
    step = pl.program_id(0)
    wide = jnp.float32
    left = y_came[0].astype(wide) + z_second[...].astype(wide)
    right = z_came[0].astype(wide) + y_second[...].astype(wide)
    grad = first[...] + jnp.concatenate([left, right], axis=1)
    xhat, inverse = norm_stats(tokens[...].astype(wide))
    out[...] = (grad_middle[...] + norm_back(grad, xhat, inverse, vectors[0:1, :])).astype(
        jnp.bfloat16
    )

    @pl.when(step == 0)
    def _():
        sums[...] = jnp.zeros_like(sums)

    sums[0:1, :] += jnp.sum(grad * xhat, axis=0, keepdims=True)
    sums[1:2, :] += jnp.sum(grad, axis=0, keepdims=True)


def grad_heads_kernel(ids, normed, own, came, out, leaving):
    out[...] = dot_tn(normed[...], own[...]).astype(jnp.bfloat16)
    leaving[...] = dot_tn(normed[...], came[...]).astype(jnp.bfloat16)


def hop_batch(block, bit):
    size = lax.axis_size("batch")
    return lax.ppermute(block, "batch", [(i, i ^ bit) for i in range(size)])


def hop_seq(block, bits):
    size = lax.axis_size("seq")
    return lax.ppermute(block, "seq", [(i, i ^ bits) for i in range(size)])


def swap_halves(block):
    batches, seqs = lax.axis_size("batch"), lax.axis_size("seq")
    route = []
    for b in range(batches):
        for s in range(seqs):
            target = ((b & ~1) | (s >> 2)) * seqs + ((s & 3) | ((b & 1) << 2))
            route.append((b * seqs + s, target))
    return lax.ppermute(block, ("batch", "seq"), route)


def after(value, *anchors):
    return lax.optimization_barrier((value,) + anchors)[0]


def trade(block, groups):
    return lax.all_to_all(block, "seq", 0, 0, tiled=True, axis_index_groups=groups)


IN_SQUARE = [[0, 1, 2, 3], [4, 5, 6, 7]]
ALONG_Z = [[0, 2, 4, 6], [1, 3, 5, 7]]


def by_side(side, own, other, axis):
    return jnp.where(
        side == 0,
        jnp.concatenate([own, other], axis=axis),
        jnp.concatenate([other, own], axis=axis),
    )


def square_shards(
    tokens,
    lengths,
    key_mask,
    cotangent,
    w_qkv,
    w_out,
    w_up,
    w_down,
    ln1_gain,
    ln1_bias,
    ln2_gain,
    ln2_bias,
    out_bias,
    up_bias,
    down_bias,
):
    low, wide = jnp.bfloat16, jnp.float32
    batch_index = lax.axis_index("batch")
    seq_index = lax.axis_index("seq")
    core = batch_index & 1
    chip_x = batch_index >> 1
    square = seq_index & 3
    y_bit = seq_index & 1
    ids = jnp.stack([core, chip_x, square, y_bit]).astype(jnp.int32)
    frames, width = tokens.shape[1], tokens.shape[2]
    rows = 8 * frames
    part = width // 8
    quarter = 2 * core + chip_x

    up_piece = lax.dynamic_index_in_dim(w_up.reshape(part, 8, 4, LANES), quarter, 2, False)
    down_piece = lax.dynamic_slice_in_dim(w_down, quarter * part, part, 0)
    out_piece = lax.dynamic_slice_in_dim(w_out, batch_index * (part // 4), part // 4, 0)
    bundle = jnp.concatenate([down_piece, up_piece.reshape(part, width), out_piece], axis=0)
    deep = bundle.shape[0]

    tokens_here = swap_halves(tokens[0])
    heads = lax.dynamic_slice_in_dim(w_qkv.reshape(part, 3, 8, LANES), 4 * core, 4, 2)
    heads = heads.transpose(2, 0, 1, 3).reshape(4, part, 3 * LANES)
    small = jnp.concatenate(
        [
            jnp.stack([ln1_gain, ln1_bias, ln2_gain, ln2_bias, out_bias, down_bias]),
            up_bias.reshape(4, part),
            jnp.zeros((6, part), low),
        ],
        axis=0,
    )
    small = jnp.broadcast_to(jnp.pad(small, ((0, 0), (0, 2 * part)))[None], (4, 16, 3 * part))
    heads = jnp.concatenate([heads, small], axis=1)
    w_heads = lax.all_to_all(
        jnp.concatenate([heads, heads], axis=0), "seq", 0, 0, tiled=True
    )
    tokens_here, w_heads, bundle = lax.optimization_barrier((tokens_here, w_heads, bundle))
    bundle = lax.all_gather(bundle, ("seq", "batch"), axis=0, tiled=True)
    bundle = bundle.reshape(8, 4, deep, width)
    vectors = w_heads[:, part:, :part].astype(wide).transpose(1, 0, 2).reshape(16, width)
    w_other = hop_batch(w_heads, 1)

    meta = jnp.concatenate([key_mask[0], jnp.pad(lengths[0], (0, LANES - lengths.shape[1]))])
    meta = meta.reshape(-1, LANES)
    meta = jnp.where(core == (seq_index >> 2), meta, hop_batch(meta, 1)).reshape(-1)
    ends = jnp.cumsum(meta[rows : rows + lengths.shape[1]])
    starts = ends - meta[rows : rows + lengths.shape[1]]
    positions = jnp.arange(rows, dtype=jnp.int32)
    start = jnp.max(
        jnp.where(starts[None, :] <= positions[:, None], starts[None, :], 0), axis=1
    ).astype(jnp.int32)
    bounds = attend_bounds(start, starts, rows)
    bias = jnp.where(meta[:rows] == 1, 0.0, NEGATIVE).astype(wide)[None, :]

    fourth = frames // 4
    slab = pl.BlockSpec((fourth, width), lambda i, *_: (i, 0))
    normed_one = call(
        norm_kernel, "norm", 4, [slab, whole(16, width)], slab, like((frames, width), low)
    )(ids, tokens_here, vectors)
    y_one = hop_seq(normed_one, 1)
    z_one = hop_seq(normed_one, 2)
    half = frames // 2
    top, bottom = hop_seq(y_one[:half], 2), hop_seq(z_one[half:], 1)
    heads_shape = (4, frames, 3 * LANES)
    top_slab = pl.BlockSpec((fourth, width), lambda i, *_: (jnp.minimum(i, 1), 0))
    bottom_slab = pl.BlockSpec((fourth, width), lambda i, *_: (jnp.maximum(i, 2) - 2, 0))
    heads_slab = pl.BlockSpec((4, fourth, 3 * LANES), lambda i, *_: (0, i, 0))
    natural_slab = pl.BlockSpec((4, fourth, width), lambda i, *_: (0, i, 0))
    heads_like = like(heads_shape, low)
    qkv_own, leaving, natural = call(
        project_kernel,
        "project",
        4,
        [slab] * 3 + [top_slab, bottom_slab] + [whole(*w_heads.shape)] * 2,
        [heads_slab, heads_slab, natural_slab],
        (heads_like, heads_like, like((4, frames, width), low)),
        flops=2 * 4 * frames * width * 6 * LANES,
    )(ids, normed_one, y_one, z_one, top, bottom, w_heads, w_other)
    qkv_came = hop_batch(leaving, 1).reshape(4 * frames, 3 * LANES)
    qkv_own = qkv_own.reshape(4 * frames, 3 * LANES)
    natural = natural.reshape(4 * frames, width)
    cotangent_own = swap_halves(after(cotangent[0], leaving))

    attended_heads, lse = attend(ids, bounds, qkv_own, qkv_came, bias)
    cotangent_came = hop_batch(cotangent_own, 1)

    mine = trade(attended_heads, IN_SQUARE)
    mine_came = hop_batch(mine, 1)
    blocks = pl.BlockSpec((8, fourth, LANES), lambda i, *_: (0, i, 0))
    w_out_spec = pl.BlockSpec(
        (8, 4, part // 4, width), lambda *_: (0, 0, (deep * 4) // part - 1, 0)
    )
    attended, middle, normed_two = call(
        out_kernel,
        "out_project",
        4,
        [blocks, blocks, slab, w_out_spec, whole(16, width)],
        [slab] * 3,
        (like((frames, width), low), like((frames, width), wide), like((frames, width), low)),
        flops=2 * frames * width * width,
    )(ids, mine, mine_came, tokens_here, bundle, vectors)
    normed_two_came = hop_batch(normed_two, 1)

    up_specs = [
        pl.BlockSpec((8, 1, part, LANES), lambda s, ids, k=k: (0, 2 * k + ids[CORE], 1, s))
        for k in range(2)
    ]
    down_specs = [
        pl.BlockSpec((1, 1, part, width), lambda s, ids, k=k: (s, 2 * k + ids[CORE], 0, 0))
        for k in range(2)
    ]
    hidden = pl.BlockSpec((2, frames, 2 * LANES), lambda s, *_: (0, 0, s))
    act, grad_up, up_sums, result_own, result_leaving, back_own, back_leaving = call(
        forward_kernel,
        "feed_forward",
        8,
        [whole(frames, width)] * 4
        + up_specs
        + down_specs
        + [pl.BlockSpec((16, LANES), lambda s, *_: (0, s))],
        [hidden, hidden, pl.BlockSpec((8, LANES), lambda s, *_: (0, s))]
        + [whole(frames, width)] * 4,
        (
            like((2, frames, 2 * width), low),
            like((2, frames, 2 * width), low),
            like((8, width), wide),
            like((frames, width), wide),
            like((frames, width), low),
            like((frames, width), wide),
            like((frames, width), low),
        ),
        scratch=[pltpu.VMEM((2, frames, width), wide)] * 2,
        flops=2 * 4 * 2 * frames * width * 2 * width,
    )(
        ids,
        normed_two,
        normed_two_came,
        cotangent_own,
        cotangent_came,
        bundle,
        bundle,
        bundle,
        bundle,
        vectors,
    )
    back_came = hop_batch(back_leaving, 1)

    hidden_pair = pl.BlockSpec((2, frames, 4 * LANES), lambda s, *_: (0, 0, s))
    down = call(
        grad_down_kernel,
        "grad_down",
        4,
        [hidden_pair, whole(frames, width), whole(frames, width)],
        pl.BlockSpec((4 * LANES, width), lambda s, *_: (s, 0)),
        like((2 * width, width), low),
        flops=2 * 2 * frames * width * 2 * width,
    )(ids, act, cotangent_own, cotangent_came)
    back_own = after(back_own, down)
    down = lax.psum_scatter(down, "seq", scatter_dimension=0, tiled=True)
    grad_middle, grad_branch, spread, middle_sums = call(
        middle_kernel,
        "middle_back",
        4,
        [slab] * 4 + [w_out_spec, whole(16, width)],
        [slab, slab, blocks, whole(8, width)],
        (
            like((frames, width), wide),
            like((frames, width), low),
            like((8, frames, LANES), low),
            like((8, width), wide),
        ),
        flops=2 * frames * width * width,
    )(ids, back_own, back_came, middle, cotangent_own, bundle, vectors)
    grad_mine = trade(spread, IN_SQUARE)
    grad_mine_came = hop_batch(grad_mine, 1)

    split = like((8, part, width // 2), low)
    split_spec = pl.BlockSpec((4,) + split.shape[1:], lambda s, *_: (s, 0, 0))
    column = pl.BlockSpec((frames, 4 * part), lambda s, *_: (0, s))
    out_kept, out_leaving = call(
        grad_out_kernel,
        "grad_out",
        2,
        [column, whole(frames, width)],
        [split_spec, split_spec],
        (split, split),
        flops=2 * frames * width * width,
    )(ids, attended, grad_branch)
    out_came = hop_batch(out_leaving, 1)
    broad = like((8, part, width + width // 4), low)
    broad_spec = pl.BlockSpec((4,) + broad.shape[1:], lambda s, *_: (s, 0, 0))
    up_kept, up_leaving = call(
        grad_up_kernel,
        "grad_up",
        2,
        [column, column, whole(2, frames, 2 * width), split_spec, split_spec],
        [broad_spec, broad_spec],
        (broad, broad),
        flops=2 * 2 * frames * width * 2 * width,
    )(ids, normed_two, normed_two_came, grad_up, out_kept, out_came)
    up_came = hop_batch(up_leaving, 2)

    result = (
        middle
        + result_own
        + hop_batch(result_leaving, 1).astype(wide)
        + vectors[5:6]
    ).astype(low)
    result_home = swap_halves(result)

    ups = jnp.zeros((4, width), wide)
    ups = lax.dynamic_update_slice(ups, up_sums[:2], (2 * core, 0))
    sums = jnp.concatenate([middle_sums[:4], ups])
    sums = sums.reshape(8, 8, 1, part).transpose(1, 2, 0, 3)
    early = jnp.broadcast_to(sums, (8, 4, 8, part)).reshape(32, 8, part)

    early = lax.all_to_all(early, ("seq", "batch"), 0, 0, tiled=True)

    grad_mine = after(grad_mine, result, up_leaving)
    grad_qkv, grad_leaving = attend_back(
        ids,
        bounds,
        qkv_own,
        qkv_came,
        grad_mine,
        grad_mine_came,
        attended_heads,
        bias,
        lse,
    )
    grad_leaving = after(grad_leaving, up_came, result_home, early)
    sums = jnp.sum(early, axis=0)
    mixed = (up_kept.astype(wide) + after(up_came, grad_leaving).astype(wide)).astype(low)
    mixed = lax.psum_scatter(
        mixed.reshape(width, width + width // 4), "seq", scatter_dimension=0, tiled=True
    )
    grad_qkv_came = hop_batch(grad_leaving, 1)

    pair = (2, frames, width // 2)
    half_spec = pl.BlockSpec((fourth, width // 2), lambda i, *_: (i, 0))
    pair_spec = pl.BlockSpec((2, fourth, width // 2), lambda i, *_: (0, i, 0))
    first, y_out, z_out, keep_left, keep_right = call(
        back_project_kernel,
        "back_project",
        4,
        [heads_slab] * 2 + [whole(*w_heads.shape)] * 2,
        [slab, pair_spec, pair_spec, half_spec, half_spec],
        (
            like((frames, width), wide),
            like(pair, low),
            like(pair, low),
            like(pair[1:], wide),
            like(pair[1:], wide),
        ),
        flops=2 * 4 * frames * width * 6 * LANES,
    )(
        ids,
        grad_qkv.reshape(heads_shape),
        grad_qkv_came.reshape(heads_shape),
        w_heads,
        w_other,
    )
    y_came, z_came = hop_seq(y_out, 1), hop_seq(z_out, 2)

    z_second, y_second = call(
        second_kernel,
        "second",
        4,
        [half_spec, half_spec, pair_spec, pair_spec],
        [half_spec, half_spec],
        (like(pair[1:], low), like(pair[1:], low)),
    )(ids, keep_left, keep_right, y_came, z_came)
    z_second, y_second = hop_seq(z_second, 2), hop_seq(y_second, 1)
    heads_out = like((width, 3 * LANES), low)
    heads_kept, heads_leaving = call(
        grad_heads_kernel,
        "grad_heads",
        2,
        [pl.BlockSpec((4 * frames, 4 * part), lambda i, *_: (0, i))]
        + [whole(4 * frames, 3 * LANES)] * 2,
        [pl.BlockSpec((4 * part, 3 * LANES), lambda i, *_: (i, 0))] * 2,
        (heads_out, heads_out),
        flops=2 * 4 * frames * width * 6 * LANES,
    )(ids, after(natural, z_out), grad_qkv, grad_qkv_came)
    heads_came = hop_batch(heads_leaving, 1)

    grad_inputs, last_sums = call(
        last_kernel,
        "last",
        4,
        [slab, pair_spec, pair_spec, half_spec, half_spec, slab, slab, whole(16, width)],
        [slab, whole(8, width)],
        (like((frames, width), low), like((8, width), wide)),
    )(ids, first, y_came, z_came, z_second, y_second, tokens_here, grad_middle, vectors)
    grad_inputs = swap_halves(grad_inputs)

    heads_sum = (heads_kept.astype(wide) + heads_came.astype(wide)).astype(low)
    heads_sum = lax.all_to_all(
        heads_sum.reshape(8, part, 3 * LANES), "seq", 0, 0, tiled=True
    ).astype(wide)
    heads_sum = (heads_sum[:4] + heads_sum[4:]).astype(low)
    heads_sum = (heads_sum.astype(wide) + hop_batch(heads_sum, 2).astype(wide)).astype(low)
    grad_qkv_w = by_side(core, heads_sum, hop_batch(heads_sum, 1), 0).astype(wide)
    grad_qkv_w = (
        grad_qkv_w.reshape(8, part, 3, LANES).transpose(1, 2, 0, 3).reshape(part, 3 * width)
    )

    down = (down.astype(wide) + hop_batch(down, 2).astype(wide)).astype(low)
    grad_down_w = by_side(core, down, hop_batch(down, 1), 0).astype(wide)
    mixed = jnp.stack([mixed, hop_batch(mixed, 2)])
    mixed = by_side(chip_x, mixed[:1], mixed[1:], 0)
    mixed = by_side(core, mixed[None], hop_batch(mixed, 1)[None], 0).astype(wide)
    grad_up_w = mixed[..., :width].reshape(2, 2, part, 4, 2 * LANES)
    grad_up_w = grad_up_w.transpose(2, 1, 3, 0, 4).reshape(part, 4 * width)
    grad_out_w = mixed[..., width:].transpose(2, 0, 1, 3).reshape(part, width)

    late = last_sums[:2]
    late = late + hop_batch(late, 2)
    late = late + hop_batch(late, 1)
    for bits in (1, 2, 4):
        late = late + hop_seq(late, bits)
    late = lax.dynamic_slice_in_dim(late, seq_index * part, part, 1)
    return (
        result_home[None],
        grad_inputs[None],
        grad_qkv_w,
        grad_out_w,
        grad_up_w,
        grad_down_w,
        late[0],
        late[1],
        sums[0],
        sums[1],
        sums[2],
        sums[4:8].reshape(4 * LANES),
        sums[3],
    )


def solution(mesh):
    square = mesh.shape["seq"] == 8 and mesh.shape["batch"] == 4
    return jax.shard_map(
        square_shards if square else shards,
        mesh=mesh,
        in_specs=(
            P("batch", "seq", None),
            P("batch", None),
            P("batch", None),
            P("batch", "seq", None),
            P("seq", None),
            P("seq", None),
            P("seq", None),
            P("seq", None),
            P("seq"),
            P("seq"),
            P("seq"),
            P("seq"),
            P("seq"),
            P("seq"),
            P("seq"),
        ),
        out_specs=(
            P("batch", "seq", None),
            P("batch", "seq", None),
            P("seq", None),
            P("seq", None),
            P("seq", None),
            P("seq", None),
            P("seq"),
            P("seq"),
            P("seq"),
            P("seq"),
            P("seq"),
            P("seq"),
            P("seq"),
        ),
        check_vma=False,
    )
```

```python
import jax
import jax.numpy as jnp
from jax import lax
from jax.experimental import pallas as pl
from jax.experimental.pallas import tpu as pltpu
from jax.sharding import PartitionSpec as P

HEAD_COUNT = 16
HEAD_DIM = 64
MAXCAP = 2048


NEGATIVE = -1e30
EPSILON = 1e-05


def shifted(block, axis, distance):
    devices = range(lax.axis_size(axis))
    route = [(i - distance, i) for i in devices if i - distance in devices]
    return lax.ppermute(block, axis, route)


def norm_rows(values, gain, shift):
    centre = jnp.mean(values, axis=-1, keepdims=True)
    centred = values - centre
    spread = jnp.mean(centred * centred, axis=-1, keepdims=True)
    return centred * lax.rsqrt(spread + EPSILON) * gain + shift


def gelu_exact(values):
    return jax.nn.gelu(values, approximate=False)


def segment_ids(lengths_row, total):
    ends = jnp.cumsum(lengths_row)
    places = jnp.arange(total, dtype=jnp.int32)
    return jnp.sum((places[:, None] >= ends[None, :]).astype(jnp.int32), axis=1)


def times_trans(left, right):
    return lax.dot_general(
        left, right, (((1,), (1,)), ((), ())), preferred_element_type=jnp.float32
    )


def trans_times(left, right):
    return lax.dot_general(
        left, right, (((0,), (0,)), ((), ())), preferred_element_type=jnp.float32
    )


def head_split(matrix):
    return matrix.reshape(matrix.shape[0], HEAD_COUNT, HEAD_DIM)


def keep_same(carry):
    return carry


def block_allowed(my_index, offset, frames, seg_all, key_on, query_seg, query_pos):
    source = my_index - offset
    start = jnp.maximum(source, 0) * frames
    key_pos = source * frames + jnp.arange(frames, dtype=jnp.int32)
    key_seg = lax.dynamic_slice_in_dim(seg_all, start, frames)
    key_live = lax.dynamic_slice_in_dim(key_on, start, frames)
    same = key_seg[None, :] == query_seg[:, None]
    causal = (key_pos[None, :] <= query_pos[:, None]) & (key_pos[None, :] >= 0)
    usable = (key_live[None, :] == 1) | (key_pos[None, :] == query_pos[:, None])
    return same & causal & usable


def block_scores(queries, keys, allowed, score_scale):
    scores = (
        jnp.einsum(
            "qhd,khd->hqk",
            head_split(queries),
            head_split(keys),
            preferred_element_type=jnp.float32,
        )
        * score_scale
    )
    return jnp.where(allowed[None], scores, NEGATIVE)


def block_probs(queries, block, allowed, row_max, row_sum, score_scale):
    scores = block_scores(queries, block[:, : queries.shape[1]], allowed, score_scale)
    return jnp.exp(scores - row_max[:, :, None]) / row_sum[:, :, None]


def forward_chain(kv_own, reach):
    blocks = [kv_own]
    moving = kv_own
    for offset in range(reach):
        moving = shifted(moving, "seq", 1)
        blocks.append(moving)
    return blocks


def again_chain(kv_own, reach):
    blocks = [kv_own]
    moving = kv_own
    for offset in range(reach):
        moving = shifted(moving, "seq", 1)
        blocks.append(moving)
    return blocks


def softmax_stats(queries, blocks, allowed_list, live_list, score_scale):
    frames, model_width = queries.shape
    row_max = jnp.full((HEAD_COUNT, frames), NEGATIVE, jnp.float32)
    row_sum = jnp.zeros((HEAD_COUNT, frames), jnp.float32)
    for offset in range(len(blocks)):

        def softmax_update(carry, block=blocks[offset], allowed=allowed_list[offset]):
            old_max, old_sum = carry
            scores = block_scores(queries, block[:, :model_width], allowed, score_scale)
            new_max = jnp.maximum(old_max, jnp.max(scores, axis=2))
            new_sum = old_sum * jnp.exp(old_max - new_max) + jnp.sum(
                jnp.exp(scores - new_max[:, :, None]), axis=2
            )
            return (new_max, new_sum)

        row_max, row_sum = lax.cond(
            live_list[offset], softmax_update, keep_same, (row_max, row_sum)
        )
    return (row_max, row_sum)


def attend_values(queries, blocks, allowed_list, live_list, row_max, row_sum, score_scale):
    frames, model_width = queries.shape
    total = jnp.zeros((frames, HEAD_COUNT, HEAD_DIM), jnp.float32)
    for offset in range(len(blocks)):

        def attend_update(carry, block=blocks[offset], allowed=allowed_list[offset]):
            probs = block_probs(queries, block, allowed, row_max, row_sum, score_scale).astype(
                jnp.bfloat16
            )
            return carry + jnp.einsum(
                "hqk,khd->qhd",
                probs,
                head_split(block[:, model_width:]),
                preferred_element_type=jnp.float32,
            )

        total = lax.cond(live_list[offset], attend_update, keep_same, total)
    return total.reshape(frames, model_width).astype(jnp.bfloat16)


def attention_grads(
    queries, grad_attended, blocks, allowed_list, live_list, row_max, row_sum, score_scale
):
    frames, model_width = queries.shape
    grad_heads = head_split(grad_attended)
    query_heads = head_split(queries)
    delta = jnp.zeros((HEAD_COUNT, frames), jnp.float32)
    for offset in range(len(blocks)):

        def attention_update(carry, block=blocks[offset], allowed=allowed_list[offset]):
            probs = block_probs(queries, block, allowed, row_max, row_sum, score_scale)
            dprobs = jnp.einsum(
                "qhd,khd->hqk",
                grad_heads,
                head_split(block[:, model_width:]),
                preferred_element_type=jnp.float32,
            )
            return carry + jnp.sum(probs * dprobs, axis=2)

        delta = lax.cond(live_list[offset], attention_update, keep_same, delta)
    grad_queries = jnp.zeros((frames, HEAD_COUNT, HEAD_DIM), jnp.float32)
    contributions = []
    for offset in range(len(blocks)):

        def block_grads(block=blocks[offset], allowed=allowed_list[offset]):
            probs = block_probs(queries, block, allowed, row_max, row_sum, score_scale)
            value_heads = head_split(block[:, model_width:])
            dprobs = jnp.einsum(
                "qhd,khd->hqk", grad_heads, value_heads, preferred_element_type=jnp.float32
            )
            dscores = (probs * (dprobs - delta[:, :, None]) * score_scale).astype(jnp.bfloat16)
            query_part = jnp.einsum(
                "hqk,khd->qhd",
                dscores,
                head_split(block[:, :model_width]),
                preferred_element_type=jnp.float32,
            )
            key_part = jnp.einsum(
                "hqk,qhd->khd", dscores, query_heads, preferred_element_type=jnp.float32
            )
            value_part = jnp.einsum(
                "hqk,qhd->khd",
                probs.astype(jnp.bfloat16),
                grad_heads,
                preferred_element_type=jnp.float32,
            )
            joined = jnp.concatenate(
                [key_part.reshape(frames, model_width), value_part.reshape(frames, model_width)],
                axis=1,
            )
            return (query_part, joined)

        def no_grads():
            return (
                jnp.zeros((frames, HEAD_COUNT, HEAD_DIM), jnp.float32),
                jnp.zeros((frames, 2 * model_width), jnp.float32),
            )

        query_part, joined = lax.cond(live_list[offset], block_grads, no_grads)
        grad_queries = grad_queries + query_part
        contributions.append(joined)
    return (grad_queries.reshape(frames, model_width), contributions)


def shards(
    tokens,
    lengths,
    key_mask,
    cotangent,
    w_qkv,
    w_out,
    w_up,
    w_down,
    ln1_gain,
    ln1_bias,
    ln2_gain,
    ln2_bias,
    out_bias,
    up_bias,
    down_bias,
):
    gathered = (
        lax.all_gather(w_qkv, "seq", axis=0, tiled=True),
        lax.all_gather(w_out, "seq", axis=0, tiled=True),
        lax.all_gather(w_up, "seq", axis=0, tiled=True),
        lax.all_gather(w_down, "seq", axis=0, tiled=True),
        lax.all_gather(ln1_gain, "seq", axis=0, tiled=True),
        lax.all_gather(ln1_bias, "seq", axis=0, tiled=True),
        lax.all_gather(ln2_gain, "seq", axis=0, tiled=True),
        lax.all_gather(ln2_bias, "seq", axis=0, tiled=True),
        lax.all_gather(out_bias, "seq", axis=0, tiled=True),
        lax.all_gather(up_bias, "seq", axis=0, tiled=True),
        lax.all_gather(down_bias, "seq", axis=0, tiled=True),
    )
    qkv_full, out_full, up_full, down_full = (gathered[0], gathered[1], gathered[2], gathered[3])
    gain_one, shift_one, gain_two, shift_two, out_shift, up_shift, down_shift = tuple(
        (member.astype(jnp.float32) for member in gathered[4:])
    )
    frames = tokens.shape[1]
    model_width = tokens.shape[2]
    cycle_size = lax.axis_size("seq")
    group_frames = frames * cycle_size
    longest = min(MAXCAP, group_frames // 2)
    reach = longest // frames
    my_index = lax.axis_index("seq")
    score_scale = HEAD_DIM ** (-0.5)
    seg_all = segment_ids(lengths[0], group_frames)
    key_on = key_mask[0]
    query_pos = my_index * frames + jnp.arange(frames, dtype=jnp.int32)
    query_seg = lax.dynamic_slice_in_dim(seg_all, my_index * frames, frames)
    allowed_list = [
        block_allowed(my_index, offset, frames, seg_all, key_on, query_seg, query_pos)
        for offset in range(reach + 1)
    ]
    live_list = [jnp.any(allowed) for allowed in allowed_list]
    inputs = tokens[0].astype(jnp.float32)
    normed_one = norm_rows(inputs, gain_one, shift_one).astype(jnp.bfloat16)
    qkv_low = jnp.dot(normed_one, qkv_full, preferred_element_type=jnp.float32).astype(jnp.bfloat16)
    queries = qkv_low[:, :model_width]
    kv_own = qkv_low[:, model_width:]
    blocks = forward_chain(kv_own, reach)
    row_max, row_sum = softmax_stats(queries, blocks, allowed_list, live_list, score_scale)
    attended = attend_values(
        queries, blocks, allowed_list, live_list, row_max, row_sum, score_scale
    )
    branch = jnp.dot(attended, out_full, preferred_element_type=jnp.float32) + out_shift
    middle = inputs + branch
    normed_two = norm_rows(middle, gain_two, shift_two).astype(jnp.bfloat16)
    up_value = jnp.dot(normed_two, up_full, preferred_element_type=jnp.float32) + up_shift
    activated = gelu_exact(up_value).astype(jnp.bfloat16)
    result = middle + jnp.dot(activated, down_full, preferred_element_type=jnp.float32) + down_shift
    grad_result = cotangent[0]
    grad_down_w = trans_times(activated, grad_result)
    grad_down_b = jnp.sum(grad_result.astype(jnp.float32), axis=0)
    grad_act = times_trans(grad_result, down_full)
    grad_up = jax.vjp(gelu_exact, up_value)[1](grad_act)[0].astype(jnp.bfloat16)
    grad_up_w = trans_times(normed_two, grad_up)
    grad_up_b = jnp.sum(grad_up.astype(jnp.float32), axis=0)
    grad_normed_two = times_trans(grad_up, up_full)
    pull_two = jax.vjp(norm_rows, middle, gain_two, shift_two)[1]
    grad_mid_norm, grad_gain_two, grad_shift_two = pull_two(grad_normed_two)
    grad_middle = grad_result.astype(jnp.float32) + grad_mid_norm
    grad_branch = grad_middle.astype(jnp.bfloat16)
    grad_out_w = trans_times(attended, grad_branch)
    grad_out_b = jnp.sum(grad_branch.astype(jnp.float32), axis=0)
    grad_attended = times_trans(grad_branch, out_full).astype(jnp.bfloat16)
    back_blocks = again_chain(kv_own, reach)
    grad_queries, contributions = attention_grads(
        queries, grad_attended, back_blocks, allowed_list, live_list, row_max, row_sum, score_scale
    )
    flowing = contributions[reach]
    for offset in range(reach - 1, -1, -1):
        flowing = (
            shifted(flowing.astype(jnp.bfloat16), "seq", -1).astype(flowing.dtype)
            + contributions[offset]
        )
    grad_qkv = jnp.concatenate([grad_queries, flowing], axis=1).astype(jnp.bfloat16)
    grad_qkv_w = trans_times(normed_one, grad_qkv)
    grad_normed_one = times_trans(grad_qkv, qkv_full)
    pull_one = jax.vjp(norm_rows, inputs, gain_one, shift_one)[1]
    grad_in_norm, grad_gain_one, grad_shift_one = pull_one(grad_normed_one)
    grad_inputs = (grad_middle + grad_in_norm).astype(jnp.bfloat16)
    shares = (
        lax.psum_scatter(
            grad_qkv_w.astype(jnp.bfloat16), "seq", scatter_dimension=0, tiled=True
        ).astype(jnp.float32),
        lax.psum_scatter(
            grad_out_w.astype(jnp.bfloat16), "seq", scatter_dimension=0, tiled=True
        ).astype(jnp.float32),
        lax.psum_scatter(
            grad_up_w.astype(jnp.bfloat16), "seq", scatter_dimension=0, tiled=True
        ).astype(jnp.float32),
        lax.psum_scatter(
            grad_down_w.astype(jnp.bfloat16), "seq", scatter_dimension=0, tiled=True
        ).astype(jnp.float32),
        lax.psum_scatter(
            grad_gain_one.astype(jnp.bfloat16), "seq", scatter_dimension=0, tiled=True
        ).astype(jnp.float32),
        lax.psum_scatter(
            grad_shift_one.astype(jnp.bfloat16), "seq", scatter_dimension=0, tiled=True
        ).astype(jnp.float32),
        lax.psum_scatter(
            grad_gain_two.astype(jnp.bfloat16), "seq", scatter_dimension=0, tiled=True
        ).astype(jnp.float32),
        lax.psum_scatter(
            grad_shift_two.astype(jnp.bfloat16), "seq", scatter_dimension=0, tiled=True
        ).astype(jnp.float32),
        lax.psum_scatter(
            grad_out_b.astype(jnp.bfloat16), "seq", scatter_dimension=0, tiled=True
        ).astype(jnp.float32),
        lax.psum_scatter(
            grad_up_b.astype(jnp.bfloat16), "seq", scatter_dimension=0, tiled=True
        ).astype(jnp.float32),
        lax.psum_scatter(
            grad_down_b.astype(jnp.bfloat16), "seq", scatter_dimension=0, tiled=True
        ).astype(jnp.float32),
    )
    reduced = (
        lax.psum(shares[0].astype(jnp.bfloat16), "batch").astype(jnp.float32),
        lax.psum(shares[1].astype(jnp.bfloat16), "batch").astype(jnp.float32),
        lax.psum(shares[2].astype(jnp.bfloat16), "batch").astype(jnp.float32),
        lax.psum(shares[3].astype(jnp.bfloat16), "batch").astype(jnp.float32),
        lax.psum(shares[4].astype(jnp.bfloat16), "batch").astype(jnp.float32),
        lax.psum(shares[5].astype(jnp.bfloat16), "batch").astype(jnp.float32),
        lax.psum(shares[6].astype(jnp.bfloat16), "batch").astype(jnp.float32),
        lax.psum(shares[7].astype(jnp.bfloat16), "batch").astype(jnp.float32),
        lax.psum(shares[8].astype(jnp.bfloat16), "batch").astype(jnp.float32),
        lax.psum(shares[9].astype(jnp.bfloat16), "batch").astype(jnp.float32),
        lax.psum(shares[10].astype(jnp.bfloat16), "batch").astype(jnp.float32),
    )
    return (
        result.astype(jnp.bfloat16)[None],
        grad_inputs[None],
        reduced[0],
        reduced[1],
        reduced[2],
        reduced[3],
        reduced[4],
        reduced[5],
        reduced[6],
        reduced[7],
        reduced[8],
        reduced[9],
        reduced[10],
    )


LANES = 128
TILE = 512
UTTERANCES = 4
SHRINK = 1
PARAMS = pltpu.CompilerParams(dimension_semantics=("arbitrary",), vmem_limit_bytes=56 << 20)


def dot_nt(left, right):
    return lax.dot_general(
        left, right, (((1,), (1,)), ((), ())), preferred_element_type=jnp.float32
    )


def dot_nn(left, right):
    return lax.dot_general(
        left, right, (((1,), (0,)), ((), ())), preferred_element_type=jnp.float32
    )


def dot_tn(left, right):
    return lax.dot_general(
        left, right, (((0,), (0,)), ((), ())), preferred_element_type=jnp.float32
    )


def norm_stats(values):
    centre = jnp.mean(values, axis=-1, keepdims=True)
    centred = values - centre
    spread = jnp.mean(centred * centred, axis=-1, keepdims=True)
    inverse = lax.rsqrt(spread + EPSILON)
    return centred * inverse, inverse


def norm_back(grad, normed, inverse, gain):
    g = grad * gain
    return inverse * (
        g
        - jnp.mean(g, axis=-1, keepdims=True)
        - normed * jnp.mean(g * normed, axis=-1, keepdims=True)
    )


def whole(*shape):
    return pl.BlockSpec(shape, lambda *_: (0,) * len(shape))


def like(shape, kind):
    return jax.ShapeDtypeStruct(shape, kind)


def call(kernel, name, grid, in_specs, out_specs, out_shape, scratch=(), flops=0):
    def run(ids, *args):
        bytes_accessed = sum(a.size * a.dtype.itemsize for a in args)
        return pl.pallas_call(
            kernel,
            out_shape=out_shape,
            grid_spec=pltpu.PrefetchScalarGridSpec(
                num_scalar_prefetch=1,
                grid=(grid,),
                in_specs=in_specs,
                out_specs=out_specs,
                scratch_shapes=list(scratch),
            ),
            compiler_params=PARAMS,
            cost_estimate=pl.CostEstimate(
                flops=flops // SHRINK,
                bytes_accessed=2 * bytes_accessed // SHRINK,
                transcendentals=0,
            ),
            name=name,
        )(ids, *args)

    return run


CORE, CHIP_X, SQUARE, Y_BIT = 0, 1, 2, 3


def norm_kernel(ids, tokens, vectors, out):
    normed, _ = norm_stats(tokens[...].astype(jnp.float32))
    out[...] = (normed * vectors[0:1, :] + vectors[1:2, :]).astype(jnp.bfloat16)


def project_kernel(ids, own, y_one, z_one, top, bottom, w_own, w_other, out, leaving, natural):
    square = ids[SQUARE]
    corner = jnp.where(pl.program_id(0) < 2, top[...], bottom[...])
    pieces = (own[...], y_one[...], z_one[...], corner)
    rows = jnp.concatenate(pieces, axis=0)
    size = corner.shape[0]
    mine = dot_nn(rows, w_own[...]).astype(jnp.bfloat16)
    other = dot_nn(rows, w_other[...]).astype(jnp.bfloat16)
    for j in range(4):
        at = pl.ds(square ^ j, 1)
        natural[at] = pieces[j][None]
        out[at] = mine[None, j * size : (j + 1) * size]
        leaving[at] = other[None, j * size : (j + 1) * size]


def head_lanes(block, head):
    lane = lax.broadcasted_iota(jnp.int32, block.shape, 1)
    keep = (lane < HEAD_DIM) if head == 0 else (lane >= HEAD_DIM)
    return jnp.where(keep, block, jnp.zeros_like(block))


def join_heads(ids, own, came, qkv):
    half = own.shape[0]
    for rows, side in ((own, ids[CORE]), (came, 1 - ids[CORE])):
        at = pl.ds(pl.multiple_of(side * half, half), half)
        qkv[at, 0:LANES] = rows[:, 0:LANES] * jnp.bfloat16(HEAD_DIM ** (-0.5))
        qkv[at, LANES : 3 * LANES] = rows[:, LANES : 3 * LANES]


def first_frames(bounds, positions):
    start = jnp.zeros_like(positions)
    for u in range(1, UTTERANCES):
        start = jnp.where(positions >= bounds[2, u], bounds[2, u], start)
    return start


def spread_places(places_row, column):
    for j in range(places_row.shape[1] // TILE):
        row = places_row[:, j * TILE : (j + 1) * TILE]
        column[j * TILE : (j + 1) * TILE, :] = jnp.transpose(
            jnp.broadcast_to(row, (LANES, TILE))
        )


def allowed_keys(column, at, start, diagonal):
    places = jnp.concatenate([column[pl.ds(at, TILE), :]] * (TILE // LANES), axis=1)
    allowed = places >= start
    if diagonal:
        key = lax.broadcasted_iota(jnp.int32, (TILE, TILE), 0)
        query = lax.broadcasted_iota(jnp.int32, (TILE, TILE), 1)
        allowed = (allowed & (key < query)) | (key == query)
    return allowed


def row_starts(bounds, base):
    return first_frames(bounds, base + lax.broadcasted_iota(jnp.int32, (1, TILE), 1)).astype(
        jnp.float32
    )


def attend_kernel(
    ids, bounds, own, came, places_row, out, lse, qkv, turned, column, scores, top, total, acc
):
    tile = pl.program_id(0)
    base = pl.multiple_of(tile * TILE, TILE)

    @pl.when(tile == 0)
    def _():
        join_heads(ids, own, came, qkv)
        spread_places(places_row, column)
        for j in range(qkv.shape[0] // TILE):
            rows = slice(j * TILE, (j + 1) * TILE)
            turned[:, rows] = jnp.transpose(qkv[rows, 2 * LANES : 3 * LANES])

    queries = [head_lanes(qkv[pl.ds(base, TILE), 0:LANES], head) for head in range(2)]
    top[...] = jnp.full_like(top, NEGATIVE)
    total[...] = jnp.zeros_like(total)
    acc[...] = jnp.zeros_like(acc)

    start = row_starts(bounds, base)

    def step(j, diagonal):
        at = pl.multiple_of(j * TILE, TILE)
        keys = qkv[pl.ds(at, TILE), LANES : 2 * LANES]
        allowed = allowed_keys(column, at, start, diagonal)
        for head in range(2):
            value = jnp.where(allowed, dot_nt(keys, queries[head]), NEGATIVE)
            scores[head, j] = value
            top[head : head + 1, :] = jnp.maximum(
                top[head : head + 1, :], jnp.max(value, axis=0, keepdims=True)
            )

    def first_pass(j, carry):
        step(j, False)
        return carry

    def second_pass(j, carry):
        at = pl.multiple_of(j * TILE, TILE)
        for head in range(2):
            probs = jnp.exp(scores[head, j] - top[head : head + 1, :])
            total[head : head + 1, :] += jnp.sum(probs, axis=0, keepdims=True)
            values = turned[head * HEAD_DIM : (head + 1) * HEAD_DIM, pl.ds(at, TILE)]
            acc[head] += dot_nn(values, probs.astype(jnp.bfloat16))
        return carry

    lax.fori_loop(bounds[0, tile], tile, first_pass, 0)
    step(tile, True)
    lax.fori_loop(bounds[0, tile], tile + 1, second_pass, 0)
    both = jnp.concatenate([acc[0] / total[0:1, :], acc[1] / total[1:2, :]], axis=0)
    out[0] = jnp.transpose(both).astype(jnp.bfloat16)
    lse[:, pl.ds(base, TILE)] = top[...] + jnp.log(total[...])


def block_order(i):
    return 2 * (i % 4) + i // 4


def attend(ids, bounds, own, came, places):
    rows = 2 * own.shape[0]
    return pl.pallas_call(
        attend_kernel,
        out_shape=(like((8, TILE, LANES), jnp.bfloat16), like((2, rows), jnp.float32)),
        grid_spec=pltpu.PrefetchScalarGridSpec(
            num_scalar_prefetch=2,
            grid=(rows // TILE,),
            in_specs=[
                whole(*own.shape),
                whole(*came.shape),
                whole(1, rows),
            ],
            out_specs=[
                pl.BlockSpec((1, TILE, LANES), lambda i, *_: (block_order(i), 0, 0)),
                whole(2, rows),
            ],
            scratch_shapes=[
                pltpu.VMEM((rows, 3 * LANES), jnp.bfloat16),
                pltpu.VMEM((LANES, rows), jnp.bfloat16),
                pltpu.VMEM((rows, LANES), jnp.float32),
                pltpu.VMEM((2, rows // TILE, TILE, TILE), jnp.float32),
                pltpu.VMEM((2, TILE), jnp.float32),
                pltpu.VMEM((2, TILE), jnp.float32),
                pltpu.VMEM((2, HEAD_DIM, TILE), jnp.float32),
            ],
        ),
        compiler_params=PARAMS,
        cost_estimate=pl.CostEstimate(
            flops=rows * rows * 256 // SHRINK, bytes_accessed=rows * 2400, transcendentals=rows * rows
        ),
        name="attend",
    )(ids, bounds, own, came, places)


def attend_back_kernel(
    ids,
    bounds,
    own,
    came,
    grad_own,
    grad_came,
    attended,
    places_row,
    lse,
    out,
    leaving,
    qkv,
    grad,
    delta,
    grad_queries,
    grad_kv,
    column,
):
    tile = pl.program_id(0)
    base = pl.multiple_of(tile * TILE, TILE)
    core = ids[CORE]

    @pl.when(tile == 0)
    def _():
        join_heads(ids, own, came, qkv)
        spread_places(places_row, column)
        grad_queries[...] = jnp.zeros_like(grad_queries)
        for j in range(4):
            for rows, side in ((grad_own, core), (grad_came, 1 - core)):
                at = pl.multiple_of((4 * side + j) * TILE, TILE)
                block = rows[pl.ds(2 * j + core, 1)].reshape(TILE, LANES)
                grad[pl.ds(at, TILE), :] = block
                product = block.astype(jnp.float32) * attended[
                    pl.ds(2 * j + side, 1)
                ].reshape(TILE, LANES).astype(jnp.float32)
                turned = jnp.transpose(product)
                delta[0:1, pl.ds(at, TILE)] = jnp.sum(turned[:HEAD_DIM], axis=0, keepdims=True)
                delta[1:2, pl.ds(at, TILE)] = jnp.sum(turned[HEAD_DIM:], axis=0, keepdims=True)

    keys = qkv[pl.ds(base, TILE), LANES : 2 * LANES]
    values = qkv[pl.ds(base, TILE), 2 * LANES : 3 * LANES]
    head_keys = [head_lanes(keys, head) for head in range(2)]
    grad_kv[...] = jnp.zeros_like(grad_kv)

    def step(i, diagonal):
        at = pl.multiple_of(i * TILE, TILE)
        scaled = qkv[pl.ds(at, TILE), 0:LANES]
        grads = grad[pl.ds(at, TILE), :]
        allowed = allowed_keys(column, base, row_starts(bounds, at), diagonal)
        query_part = jnp.zeros((TILE, LANES), jnp.float32)
        key_part = grad_kv[0]
        value_part = grad_kv[1]
        for head in range(2):
            queries = head_lanes(scaled, head)
            head_grads = head_lanes(grads, head)
            scores = jnp.where(allowed, dot_nt(keys, queries), NEGATIVE)
            probs = jnp.exp(scores - lse[head : head + 1, pl.ds(at, TILE)])
            dprobs = dot_nt(values, head_grads)
            dscores = (probs * (dprobs - delta[head : head + 1, pl.ds(at, TILE)])).astype(
                jnp.bfloat16
            )
            value_part = value_part + dot_nn(probs.astype(jnp.bfloat16), head_grads)
            key_part = key_part + dot_nn(dscores, queries)
            query_part = query_part + dot_tn(dscores, head_keys[head])
        grad_kv[0] = key_part
        grad_kv[1] = value_part
        grad_queries[pl.ds(at, TILE), :] += query_part

    def later_step(i, carry):
        step(i, False)
        return carry

    step(tile, True)
    lax.fori_loop(tile + 1, bounds[1, tile], later_step, 0)

    def store(target):
        at = pl.ds(pl.multiple_of((tile % 4) * TILE, TILE), TILE)
        target[at, 0:LANES] = (
            grad_queries[pl.ds(base, TILE), :] * HEAD_DIM ** (-0.5)
        ).astype(jnp.bfloat16)
        target[at, LANES : 2 * LANES] = grad_kv[0].astype(jnp.bfloat16)
        target[at, 2 * LANES : 3 * LANES] = grad_kv[1].astype(jnp.bfloat16)

    @pl.when(tile // 4 == core)
    def _():
        store(out)

    @pl.when(tile // 4 != core)
    def _():
        store(leaving)


def attend_back(ids, bounds, own, came, grad_own, grad_came, attended, places, lse):
    half = own.shape[0]
    rows = 2 * half
    return pl.pallas_call(
        attend_back_kernel,
        out_shape=(like(own.shape, jnp.bfloat16), like(own.shape, jnp.bfloat16)),
        grid_spec=pltpu.PrefetchScalarGridSpec(
            num_scalar_prefetch=2,
            grid=(rows // TILE,),
            in_specs=[
                whole(*own.shape),
                whole(*came.shape),
                whole(*grad_own.shape),
                whole(*grad_came.shape),
                whole(*attended.shape),
                whole(1, rows),
                whole(2, rows),
            ],
            out_specs=[whole(*own.shape), whole(*own.shape)],
            scratch_shapes=[
                pltpu.VMEM((rows, 3 * LANES), jnp.bfloat16),
                pltpu.VMEM((rows, LANES), jnp.bfloat16),
                pltpu.VMEM((2, rows), jnp.float32),
                pltpu.VMEM((rows, LANES), jnp.float32),
                pltpu.VMEM((2, TILE, LANES), jnp.float32),
                pltpu.VMEM((rows, LANES), jnp.float32),
            ],
        ),
        compiler_params=PARAMS,
        cost_estimate=pl.CostEstimate(
            flops=rows * rows * 640 // SHRINK, bytes_accessed=rows * 2400, transcendentals=rows * rows
        ),
        name="attend_back",
    )(ids, bounds, own, came, grad_own, grad_came, attended, places, lse)


def attend_bounds(start, starts, rows):
    tiles = rows // TILE
    first = start[:: TILE]
    key_last = jnp.arange(1, tiles + 1, dtype=jnp.int32) * TILE - 1
    far_end = jnp.sum((first[None, :] <= key_last[:, None]).astype(jnp.int32), axis=1)
    starts = jnp.pad(starts, (0, tiles - starts.shape[0]))
    return jnp.stack([first // TILE, far_end, starts]).astype(jnp.int32)


def out_kernel(ids, own, came, tokens, w_out, vectors, attended, middle, normed):
    core = ids[CORE]
    rows, width = tokens.shape
    mine, other = [], []
    for j in range(4):
        mine.append(own[pl.ds(2 * j + core, 1)].reshape(rows, LANES))
        other.append(came[pl.ds(2 * j + core, 1)].reshape(rows, LANES))
    mine, other = jnp.concatenate(mine, axis=1), jnp.concatenate(other, axis=1)
    first = jnp.where(core == 0, mine, other)
    second = jnp.where(core == 0, other, mine)
    joined = jnp.concatenate([first, second], axis=1)
    attended[...] = joined
    branch = dot_nn(joined, w_out[...].reshape(width, width)) + vectors[4:5, :]
    value = tokens[...].astype(jnp.float32) + branch
    middle[...] = value
    xhat, _ = norm_stats(value)
    normed[...] = (xhat * vectors[2:3, :] + vectors[3:4, :]).astype(jnp.bfloat16)


def forward_kernel(
    ids,
    normed_own,
    normed_came,
    grad_own,
    grad_came,
    up_a,
    up_b,
    down_a,
    down_b,
    vectors,
    act,
    grad_up,
    up_bias,
    result_own,
    result_came,
    back_own,
    back_came,
    result,
    back,
):
    step = pl.program_id(0)
    core = ids[CORE]
    frames, width = normed_own.shape

    @pl.when(step == 0)
    def _():
        result[...] = jnp.zeros_like(result)
        back[...] = jnp.zeros_like(back)

    w_up = jnp.concatenate(
        [up_a[...].reshape(width, LANES), up_b[...].reshape(width, LANES)], axis=1
    )
    w_down = jnp.concatenate(
        [down_a[...].reshape(LANES, width), down_b[...].reshape(LANES, width)], axis=0
    )
    shift = jnp.where(
        core == 0,
        jnp.concatenate([vectors[6:7, :], vectors[7:8, :]], axis=1),
        jnp.concatenate([vectors[8:9, :], vectors[9:10, :]], axis=1),
    )
    bias = jnp.zeros((1, 2 * LANES), jnp.float32)
    for side, (normed, grad) in enumerate(((normed_own, grad_own), (normed_came, grad_came))):
        value = dot_nn(normed[...], w_up) + shift
        half = 0.5 + 0.5 * lax.erf(value * 0.7071067811865476)
        bell = jnp.exp(-0.5 * value * value) * 0.3989422804014327
        activated = (value * half).astype(jnp.bfloat16)
        act[side] = activated
        change = dot_nt(grad[...], w_down) * (half + value * bell)
        bias = bias + jnp.sum(change.astype(jnp.bfloat16).astype(jnp.float32), axis=0, keepdims=True)
        change = change.astype(jnp.bfloat16)
        grad_up[side] = change
        result[side] += dot_nn(activated, w_down)
        back[side] += dot_nt(change, w_up)
    up_bias[0:1, :] = bias[:, 0:LANES]
    up_bias[1:2, :] = bias[:, LANES:]

    @pl.when(step == 7)
    def _():
        result_own[...] = result[0]
        result_came[...] = result[1].astype(jnp.bfloat16)
        back_own[...] = back[0]
        back_came[...] = back[1].astype(jnp.bfloat16)


def middle_kernel(
    ids, back_own, back_came, middle, cotangent, w_out, vectors, grad_middle, grad_branch, out, sums
):
    step = pl.program_id(0)
    xhat, inverse = norm_stats(middle[...])
    grad = back_own[...] + back_came[...].astype(jnp.float32)
    value = cotangent[...].astype(jnp.float32) + norm_back(grad, xhat, inverse, vectors[2:3, :])
    grad_middle[...] = value
    low = value.astype(jnp.bfloat16)
    grad_branch[...] = low

    @pl.when(step == 0)
    def _():
        sums[...] = jnp.zeros_like(sums)

    sums[0:1, :] += jnp.sum(grad * xhat, axis=0, keepdims=True)
    sums[1:2, :] += jnp.sum(grad, axis=0, keepdims=True)
    sums[2:3, :] += jnp.sum(low.astype(jnp.float32), axis=0, keepdims=True)
    sums[3:4, :] += jnp.sum(cotangent[...].astype(jnp.float32), axis=0, keepdims=True)
    width = w_out.shape[-1]
    spread = dot_nt(low, w_out[...].reshape(width, width)).astype(jnp.bfloat16)
    for group in range(8):
        out[block_order(group)] = spread[:, group * LANES : (group + 1) * LANES]


def grad_out_kernel(ids, attended, grad_branch, kept, leaving):
    core = ids[CORE]
    grad = dot_tn(attended[...], grad_branch[...]).astype(jnp.bfloat16)
    half = grad.shape[1] // 2
    shape = kept.shape
    kept[...] = jnp.where(core == 0, grad[:, :half], grad[:, half:]).reshape(shape)
    leaving[...] = jnp.where(core == 0, grad[:, half:], grad[:, :half]).reshape(shape)


def grad_down_kernel(ids, act, grad_own, grad_came, out):
    grad = dot_tn(act[0], grad_own[...]) + dot_tn(act[1], grad_came[...])
    out[...] = grad.astype(jnp.bfloat16)


def grad_up_kernel(ids, normed_own, normed_came, grad_up, out_own, out_came, kept, leaving):
    chip_x = ids[CHIP_X]
    grad = (dot_tn(normed_own[...], grad_up[0]) + dot_tn(normed_came[...], grad_up[1])).astype(
        jnp.bfloat16
    )
    half = grad.shape[1] // 2
    shape = kept.shape[:2] + (half,)
    kept[:, :, :half] = jnp.where(chip_x == 0, grad[:, :half], grad[:, half:]).reshape(shape)
    leaving[:, :, :half] = jnp.where(chip_x == 0, grad[:, half:], grad[:, :half]).reshape(shape)
    more = (out_own[...].astype(jnp.float32) + out_came[...].astype(jnp.float32)).astype(
        jnp.bfloat16
    )
    cut = more.shape[2] // 2
    kept[:, :, half:] = jnp.where(chip_x == 0, more[:, :, :cut], more[:, :, cut:])
    leaving[:, :, half:] = jnp.where(chip_x == 0, more[:, :, cut:], more[:, :, :cut])


def back_project_kernel(
    ids, own, came, w_own, w_other, first, y_out, z_out, keep_left, keep_right, grads
):
    square = ids[SQUARE]
    size, width = first.shape
    half = width // 2
    rows = 4 * size
    value = dot_nt(own[...].reshape(rows, 3 * LANES), w_own[...])
    value = value + dot_nt(came[...].reshape(rows, 3 * LANES), w_other[...])
    grads[...] = value.reshape(4, size, width)
    first[...] = grads[square]
    y_out[0] = grads[square ^ 1, :, :half].astype(jnp.bfloat16)
    keep_right[...] = grads[square ^ 1, :, half:]
    z_out[0] = grads[square ^ 2, :, half:].astype(jnp.bfloat16)
    keep_left[...] = grads[square ^ 2, :, :half]
    y_out[1] = grads[square ^ 3, :, :half].astype(jnp.bfloat16)
    z_out[1] = grads[square ^ 3, :, half:].astype(jnp.bfloat16)


def second_kernel(ids, keep_left, keep_right, y_came, z_came, z_out, y_out):
    z_out[...] = (keep_left[...] + y_came[1].astype(jnp.float32)).astype(jnp.bfloat16)
    y_out[...] = (keep_right[...] + z_came[1].astype(jnp.float32)).astype(jnp.bfloat16)


def last_kernel(
    ids, first, y_came, z_came, z_second, y_second, tokens, grad_middle, vectors, out, sums
):
    step = pl.program_id(0)
    wide = jnp.float32
    left = y_came[0].astype(wide) + z_second[...].astype(wide)
    right = z_came[0].astype(wide) + y_second[...].astype(wide)
    grad = first[...] + jnp.concatenate([left, right], axis=1)
    xhat, inverse = norm_stats(tokens[...].astype(wide))
    out[...] = (grad_middle[...] + norm_back(grad, xhat, inverse, vectors[0:1, :])).astype(
        jnp.bfloat16
    )

    @pl.when(step == 0)
    def _():
        sums[...] = jnp.zeros_like(sums)

    sums[0:1, :] += jnp.sum(grad * xhat, axis=0, keepdims=True)
    sums[1:2, :] += jnp.sum(grad, axis=0, keepdims=True)


def grad_heads_kernel(ids, normed, own, came, out, leaving):
    out[...] = dot_tn(normed[...], own[...]).astype(jnp.bfloat16)
    leaving[...] = dot_tn(normed[...], came[...]).astype(jnp.bfloat16)


def spread_kernel(
    ids,
    heads,
    heads_came,
    down,
    down_came,
    mixed,
    mixed_x,
    mixed_core,
    mixed_both,
    qkv_out,
    out_out,
    up_out,
    down_out,
):
    wide = jnp.float32
    core, chip_x = ids[CORE], ids[CHIP_X]

    def ordered(side, own, other):
        return jnp.where(side == 0, own, other), jnp.where(side == 0, other, own)

    for side, blocks in enumerate(ordered(core, heads[...], heads_came[...])):
        for j in range(4):
            for k in range(3):
                at = k * 8 * LANES + (4 * side + j) * LANES
                qkv_out[:, at : at + LANES] = blocks[j, :, k * LANES : (k + 1) * LANES].astype(wide)
    rows = down.shape[0]
    for side, block in enumerate(ordered(core, down[...], down_came[...])):
        down_out[side * rows : (side + 1) * rows, :] = block.astype(wide)
    own = ordered(chip_x, mixed[...], mixed_x[...])
    came = ordered(chip_x, mixed_core[...], mixed_both[...])
    width = out_out.shape[1]
    step = 2 * LANES
    for x in range(2):
        for side, block in enumerate(ordered(core, own[x], came[x])):
            for j in range(4):
                at = (4 * x + j) * 2 * step + side * step
                up_out[:, at : at + step] = block[:, j * step : (j + 1) * step].astype(wide)
            at = side * 2 * step + x * step
            out_out[:, at : at + step] = block[:, width:].astype(wide)


def hop_batch(block, bit):
    size = lax.axis_size("batch")
    return lax.ppermute(block, "batch", [(i, i ^ bit) for i in range(size)])


def hop_seq(block, bits):
    size = lax.axis_size("seq")
    return lax.ppermute(block, "seq", [(i, i ^ bits) for i in range(size)])


def swap_halves(block):
    batches, seqs = lax.axis_size("batch"), lax.axis_size("seq")
    route = []
    for b in range(batches):
        for s in range(seqs):
            target = ((b & ~1) | (s >> 2)) * seqs + ((s & 3) | ((b & 1) << 2))
            route.append((b * seqs + s, target))
    return lax.ppermute(block, ("batch", "seq"), route)


def after(value, *anchors):
    return lax.optimization_barrier((value,) + anchors)[0]


def trade(block, groups):
    return lax.all_to_all(block, "seq", 0, 0, tiled=True, axis_index_groups=groups)


IN_SQUARE = [[0, 1, 2, 3], [4, 5, 6, 7]]
ALONG_Z = [[0, 2, 4, 6], [1, 3, 5, 7]]


def square_shards(
    tokens,
    lengths,
    key_mask,
    cotangent,
    w_qkv,
    w_out,
    w_up,
    w_down,
    ln1_gain,
    ln1_bias,
    ln2_gain,
    ln2_bias,
    out_bias,
    up_bias,
    down_bias,
):
    low, wide = jnp.bfloat16, jnp.float32
    batch_index = lax.axis_index("batch")
    seq_index = lax.axis_index("seq")
    core = batch_index & 1
    chip_x = batch_index >> 1
    square = seq_index & 3
    y_bit = seq_index & 1
    ids = jnp.stack([core, chip_x, square, y_bit]).astype(jnp.int32)
    frames, width = tokens.shape[1], tokens.shape[2]
    rows = 8 * frames
    part = width // 8
    quarter = 2 * core + chip_x

    up_piece = lax.dynamic_index_in_dim(w_up.reshape(part, 8, 4, LANES), quarter, 2, False)
    down_piece = lax.dynamic_slice_in_dim(w_down, quarter * part, part, 0)
    out_piece = lax.dynamic_slice_in_dim(w_out, batch_index * (part // 4), part // 4, 0)
    bundle = jnp.concatenate([down_piece, up_piece.reshape(part, width), out_piece], axis=0)
    deep = bundle.shape[0]

    tokens_here = swap_halves(tokens[0])
    small = jnp.concatenate(
        [
            jnp.stack([ln1_gain, ln1_bias, ln2_gain, ln2_bias, out_bias, down_bias]),
            up_bias.reshape(4, part),
            jnp.zeros((6, part), low),
        ],
        axis=0,
    )
    small = lax.all_to_all(
        jnp.broadcast_to(small[None], (8, 16, part)), "seq", 0, 0, tiled=True
    )
    vectors = small.astype(wide).transpose(1, 0, 2).reshape(16, width)

    heads = lax.dynamic_slice_in_dim(w_qkv.reshape(part, 3, 8, LANES), 4 * core, 4, 2)
    heads = heads.transpose(2, 0, 1, 3).reshape(4, part, 3 * LANES)
    heads = after(jnp.concatenate([heads, heads], axis=0), small)
    w_heads = lax.all_to_all(heads, "seq", 0, 0, tiled=True).reshape(width, 3 * LANES)
    w_other = hop_batch(w_heads, 1)

    meta = jnp.concatenate([key_mask[0], jnp.pad(lengths[0], (0, LANES - lengths.shape[1]))])
    meta = meta.reshape(-1, LANES)
    meta = jnp.where(core == (seq_index >> 2), meta, hop_batch(meta, 1)).reshape(-1)
    ends = jnp.cumsum(meta[rows : rows + lengths.shape[1]])
    starts = ends - meta[rows : rows + lengths.shape[1]]
    positions = jnp.arange(rows, dtype=jnp.int32)
    start = jnp.max(
        jnp.where(starts[None, :] <= positions[:, None], starts[None, :], 0), axis=1
    ).astype(jnp.int32)
    bounds = attend_bounds(start, starts, rows)
    places = jnp.where(meta[:rows] == 1, positions, -1).astype(wide)[None, :]

    fourth = frames // 4
    slab = pl.BlockSpec((fourth, width), lambda i, *_: (i, 0))
    normed_one = call(
        norm_kernel, "norm", 4, [slab, whole(16, width)], slab, like((frames, width), low)
    )(ids, tokens_here, vectors)
    y_one = hop_seq(normed_one, 1)
    z_one = hop_seq(normed_one, 2)
    bundle = lax.all_gather(after(bundle, normed_one, w_heads), ("seq", "batch"), axis=0, tiled=True)
    bundle = bundle.reshape(8, 4, deep, width)
    half = frames // 2
    top, bottom = hop_seq(y_one[:half], 2), hop_seq(z_one[half:], 1)
    heads_shape = (4, frames, 3 * LANES)
    top_slab = pl.BlockSpec((fourth, width), lambda i, *_: (jnp.minimum(i, 1), 0))
    bottom_slab = pl.BlockSpec((fourth, width), lambda i, *_: (jnp.maximum(i, 2) - 2, 0))
    heads_slab = pl.BlockSpec((4, fourth, 3 * LANES), lambda i, *_: (0, i, 0))
    natural_slab = pl.BlockSpec((4, fourth, width), lambda i, *_: (0, i, 0))
    heads_like = like(heads_shape, low)
    qkv_own, leaving, natural = call(
        project_kernel,
        "project",
        4,
        [slab] * 3 + [top_slab, bottom_slab] + [whole(*w_heads.shape)] * 2,
        [heads_slab, heads_slab, natural_slab],
        (heads_like, heads_like, like((4, frames, width), low)),
        flops=2 * 4 * frames * width * 6 * LANES,
    )(ids, normed_one, y_one, z_one, top, bottom, w_heads, w_other)
    qkv_came = hop_batch(leaving, 1).reshape(4 * frames, 3 * LANES)
    qkv_own = qkv_own.reshape(4 * frames, 3 * LANES)
    natural = natural.reshape(4 * frames, width)
    cotangent_own = swap_halves(after(cotangent[0], leaving))

    attended_heads, lse = attend(ids, bounds, qkv_own, qkv_came, places)
    cotangent_came = hop_batch(cotangent_own, 1)

    mine = trade(attended_heads, IN_SQUARE)
    mine_came = hop_batch(mine, 1)
    blocks = pl.BlockSpec((8, half, LANES), lambda i, *_: (0, i, 0))
    wide_slab = pl.BlockSpec((half, width), lambda i, *_: (i, 0))
    w_out_spec = pl.BlockSpec(
        (8, 4, part // 4, width), lambda *_: (0, 0, (deep * 4) // part - 1, 0)
    )
    attended, middle, normed_two = call(
        out_kernel,
        "out_project",
        2,
        [blocks, blocks, wide_slab, w_out_spec, whole(16, width)],
        [wide_slab] * 3,
        (like((frames, width), low), like((frames, width), wide), like((frames, width), low)),
        flops=2 * frames * width * width,
    )(ids, mine, mine_came, tokens_here, bundle, vectors)
    normed_two_came = hop_batch(normed_two, 1)

    up_specs = [
        pl.BlockSpec((8, 1, part, LANES), lambda s, ids, k=k: (0, 2 * k + ids[CORE], 1, s))
        for k in range(2)
    ]
    down_specs = [
        pl.BlockSpec((1, 1, part, width), lambda s, ids, k=k: (s, 2 * k + ids[CORE], 0, 0))
        for k in range(2)
    ]
    hidden = pl.BlockSpec((2, frames, 2 * LANES), lambda s, *_: (0, 0, s))
    act, grad_up, up_sums, result_own, result_leaving, back_own, back_leaving = call(
        forward_kernel,
        "feed_forward",
        8,
        [whole(frames, width)] * 4
        + up_specs
        + down_specs
        + [pl.BlockSpec((16, LANES), lambda s, *_: (0, s))],
        [hidden, hidden, pl.BlockSpec((8, LANES), lambda s, *_: (0, s))]
        + [whole(frames, width)] * 4,
        (
            like((2, frames, 2 * width), low),
            like((2, frames, 2 * width), low),
            like((8, width), wide),
            like((frames, width), wide),
            like((frames, width), low),
            like((frames, width), wide),
            like((frames, width), low),
        ),
        scratch=[pltpu.VMEM((2, frames, width), wide)] * 2,
        flops=2 * 4 * 2 * frames * width * 2 * width,
    )(
        ids,
        normed_two,
        normed_two_came,
        cotangent_own,
        cotangent_came,
        bundle,
        bundle,
        bundle,
        bundle,
        vectors,
    )
    back_came = hop_batch(back_leaving, 1)

    hidden_pair = pl.BlockSpec((2, frames, 4 * LANES), lambda s, *_: (0, 0, s))
    down = call(
        grad_down_kernel,
        "grad_down",
        4,
        [hidden_pair, whole(frames, width), whole(frames, width)],
        pl.BlockSpec((4 * LANES, width), lambda s, *_: (s, 0)),
        like((2 * width, width), low),
        flops=2 * 2 * frames * width * 2 * width,
    )(ids, act, cotangent_own, cotangent_came)
    back_own = after(back_own, down)
    down = lax.psum_scatter(down, "seq", scatter_dimension=0, tiled=True)
    grad_middle, grad_branch, spread, middle_sums = call(
        middle_kernel,
        "middle_back",
        2,
        [wide_slab] * 4 + [w_out_spec, whole(16, width)],
        [wide_slab, wide_slab, blocks, whole(8, width)],
        (
            like((frames, width), wide),
            like((frames, width), low),
            like((8, frames, LANES), low),
            like((8, width), wide),
        ),
        flops=2 * frames * width * width,
    )(ids, back_own, back_came, middle, cotangent_own, bundle, vectors)
    grad_mine = trade(spread, IN_SQUARE)
    grad_mine_came = hop_batch(grad_mine, 1)

    split = like((8, part, width // 2), low)
    split_spec = pl.BlockSpec((4,) + split.shape[1:], lambda s, *_: (s, 0, 0))
    column = pl.BlockSpec((frames, 4 * part), lambda s, *_: (0, s))
    out_kept, out_leaving = call(
        grad_out_kernel,
        "grad_out",
        2,
        [column, whole(frames, width)],
        [split_spec, split_spec],
        (split, split),
        flops=2 * frames * width * width,
    )(ids, attended, grad_branch)
    out_came = hop_batch(out_leaving, 1)
    broad = like((8, part, width + width // 4), low)
    broad_spec = pl.BlockSpec((4,) + broad.shape[1:], lambda s, *_: (s, 0, 0))
    up_kept, up_leaving = call(
        grad_up_kernel,
        "grad_up",
        2,
        [column, column, whole(2, frames, 2 * width), split_spec, split_spec],
        [broad_spec, broad_spec],
        (broad, broad),
        flops=2 * 2 * frames * width * 2 * width,
    )(ids, normed_two, normed_two_came, grad_up, out_kept, out_came)
    up_came = hop_batch(up_leaving, 2)

    result = (
        middle
        + result_own
        + hop_batch(result_leaving, 1).astype(wide)
        + vectors[5:6]
    ).astype(low)
    result_home = swap_halves(result[None])

    grad_mine = after(grad_mine, result, up_leaving)
    grad_qkv, grad_leaving = attend_back(
        ids,
        bounds,
        qkv_own,
        qkv_came,
        grad_mine,
        grad_mine_came,
        attended_heads,
        places,
        lse,
    )
    grad_leaving = after(grad_leaving, up_came, result_home)
    mixed = (up_kept.astype(wide) + after(up_came, grad_leaving).astype(wide)).astype(low)
    mixed = lax.psum_scatter(
        mixed.reshape(width, width + width // 4), "seq", scatter_dimension=0, tiled=True
    )
    grad_qkv_came = hop_batch(grad_leaving, 1)

    pair = (2, frames, width // 2)
    half_spec = pl.BlockSpec((fourth, width // 2), lambda i, *_: (i, 0))
    pair_spec = pl.BlockSpec((2, fourth, width // 2), lambda i, *_: (0, i, 0))
    first, y_out, z_out, keep_left, keep_right = call(
        back_project_kernel,
        "back_project",
        4,
        [heads_slab] * 2 + [whole(*w_heads.shape)] * 2,
        [slab, pair_spec, pair_spec, half_spec, half_spec],
        (
            like((frames, width), wide),
            like(pair, low),
            like(pair, low),
            like(pair[1:], wide),
            like(pair[1:], wide),
        ),
        scratch=[pltpu.VMEM((4, fourth, width), wide)],
        flops=2 * 4 * frames * width * 6 * LANES,
    )(
        ids,
        grad_qkv.reshape(heads_shape),
        grad_qkv_came.reshape(heads_shape),
        w_heads,
        w_other,
    )
    y_came, z_came = hop_seq(y_out, 1), hop_seq(z_out, 2)

    heads_out = like((width, 3 * LANES), low)
    heads_kept, heads_leaving = call(
        grad_heads_kernel,
        "grad_heads",
        2,
        [pl.BlockSpec((4 * frames, 4 * part), lambda i, *_: (0, i))]
        + [whole(4 * frames, 3 * LANES)] * 2,
        [pl.BlockSpec((4 * part, 3 * LANES), lambda i, *_: (i, 0))] * 2,
        (heads_out, heads_out),
        flops=2 * 4 * frames * width * 6 * LANES,
    )(ids, after(natural, z_out), grad_qkv, grad_qkv_came)
    heads_came = hop_batch(heads_leaving, 1)
    heads_sum = (heads_kept.astype(wide) + heads_came.astype(wide)).astype(low)
    heads_came = hop_batch(heads_sum, 2)
    down = after(down, z_out)
    down_x = hop_batch(down, 2)
    down = (down.astype(wide) + down_x.astype(wide)).astype(low)
    y_came = after(y_came, heads_sum, down)
    down_came = hop_batch(down, 1)

    z_second, y_second = call(
        second_kernel,
        "second",
        1,
        [whole(*pair[1:])] * 2 + [whole(*pair)] * 2,
        [whole(*pair[1:])] * 2,
        (like(pair[1:], low), like(pair[1:], low)),
    )(ids, keep_left, keep_right, y_came, z_came)
    z_last, y_last = hop_seq(z_second, 2), hop_seq(y_second, 1)
    grad_inputs, last_sums = call(
        last_kernel,
        "last",
        4,
        [slab, pair_spec, pair_spec, half_spec, half_spec, slab, slab, whole(16, width)],
        [slab, whole(8, width)],
        (like((frames, width), low), like((8, width), wide)),
    )(ids, after(first, down_came, mixed), y_came, z_came, z_last, y_last, tokens_here, grad_middle, vectors)
    mixed_x = hop_batch(mixed, 2)
    grad_inputs = swap_halves(after(grad_inputs, mixed_x)[None])

    heads_sum = (
        after(heads_sum, z_last, y_last).astype(wide) + heads_came.astype(wide)
    ).astype(low)
    heads_sum = lax.all_to_all(
        heads_sum.reshape(8, part, 3 * LANES), "seq", 0, 0, tiled=True
    ).astype(wide)
    heads_sum = (heads_sum[:4] + heads_sum[4:]).astype(low)
    heads_came = hop_batch(heads_sum, 1)
    mixed_core, mixed_both = hop_batch(mixed, 1), hop_batch(mixed_x, 1)
    grad_qkv_w, grad_out_w, grad_up_w, grad_down_w = call(
        spread_kernel,
        "spread",
        1,
        [whole(4, part, 3 * LANES)] * 2
        + [whole(2 * part, width)] * 2
        + [whole(part, width + width // 4)] * 4,
        [
            whole(part, 3 * width),
            whole(part, width),
            whole(part, 4 * width),
            whole(4 * part, width),
        ],
        (
            like((part, 3 * width), wide),
            like((part, width), wide),
            like((part, 4 * width), wide),
            like((4 * part, width), wide),
        ),
    )(ids, heads_sum, heads_came, down, down_came, mixed, mixed_x, mixed_core, mixed_both)

    ups = jnp.zeros((4, width), wide)
    ups = lax.dynamic_update_slice(ups, up_sums[:2], (2 * core, 0))
    sums = jnp.concatenate([last_sums[:2], middle_sums[:4], ups, jnp.zeros((6, width), wide)])
    sums = sums + hop_batch(sums, 2)
    sums = sums + hop_batch(sums, 1)
    sums = after(sums, mixed_x)
    for bits in (1, 2, 4):
        sums = sums + hop_seq(sums, bits)
    sums = lax.dynamic_slice_in_dim(sums, seq_index * part, part, 1)
    return (
        result_home,
        grad_inputs,
        grad_qkv_w,
        grad_out_w,
        grad_up_w,
        grad_down_w,
        sums[0],
        sums[1],
        sums[2],
        sums[3],
        sums[4],
        sums[6:10].reshape(4 * LANES),
        sums[5],
    )


def solution(mesh):
    square = mesh.shape["seq"] == 8 and mesh.shape["batch"] == 4
    return jax.shard_map(
        square_shards if square else shards,
        mesh=mesh,
        in_specs=(
            P("batch", "seq", None),
            P("batch", None),
            P("batch", None),
            P("batch", "seq", None),
            P("seq", None),
            P("seq", None),
            P("seq", None),
            P("seq", None),
            P("seq"),
            P("seq"),
            P("seq"),
            P("seq"),
            P("seq"),
            P("seq"),
            P("seq"),
        ),
        out_specs=(
            P("batch", "seq", None),
            P("batch", "seq", None),
            P("seq", None),
            P("seq", None),
            P("seq", None),
            P("seq", None),
            P("seq"),
            P("seq"),
            P("seq"),
            P("seq"),
            P("seq"),
            P("seq"),
            P("seq"),
        ),
        check_vma=False,
    )
```

```python
import jax
import jax.numpy as jnp
from jax import lax
from jax.experimental import pallas as pl
from jax.experimental.pallas import tpu as pltpu
from jax.sharding import PartitionSpec as P

HEAD_COUNT = 16
HEAD_DIM = 64
MAXCAP = 2048


NEGATIVE = -1e30
EPSILON = 1e-05


def shifted(block, axis, distance):
    devices = range(lax.axis_size(axis))
    route = [(i - distance, i) for i in devices if i - distance in devices]
    return lax.ppermute(block, axis, route)


def norm_rows(values, gain, shift):
    centre = jnp.mean(values, axis=-1, keepdims=True)
    centred = values - centre
    spread = jnp.mean(centred * centred, axis=-1, keepdims=True)
    return centred * lax.rsqrt(spread + EPSILON) * gain + shift


def gelu_exact(values):
    return jax.nn.gelu(values, approximate=False)


def segment_ids(lengths_row, total):
    ends = jnp.cumsum(lengths_row)
    places = jnp.arange(total, dtype=jnp.int32)
    return jnp.sum((places[:, None] >= ends[None, :]).astype(jnp.int32), axis=1)


def times_trans(left, right):
    return lax.dot_general(
        left, right, (((1,), (1,)), ((), ())), preferred_element_type=jnp.float32
    )


def trans_times(left, right):
    return lax.dot_general(
        left, right, (((0,), (0,)), ((), ())), preferred_element_type=jnp.float32
    )


def head_split(matrix):
    return matrix.reshape(matrix.shape[0], HEAD_COUNT, HEAD_DIM)


def keep_same(carry):
    return carry


def block_allowed(my_index, offset, frames, seg_all, key_on, query_seg, query_pos):
    source = my_index - offset
    start = jnp.maximum(source, 0) * frames
    key_pos = source * frames + jnp.arange(frames, dtype=jnp.int32)
    key_seg = lax.dynamic_slice_in_dim(seg_all, start, frames)
    key_live = lax.dynamic_slice_in_dim(key_on, start, frames)
    same = key_seg[None, :] == query_seg[:, None]
    causal = (key_pos[None, :] <= query_pos[:, None]) & (key_pos[None, :] >= 0)
    usable = (key_live[None, :] == 1) | (key_pos[None, :] == query_pos[:, None])
    return same & causal & usable


def block_scores(queries, keys, allowed, score_scale):
    scores = (
        jnp.einsum(
            "qhd,khd->hqk",
            head_split(queries),
            head_split(keys),
            preferred_element_type=jnp.float32,
        )
        * score_scale
    )
    return jnp.where(allowed[None], scores, NEGATIVE)


def block_probs(queries, block, allowed, row_max, row_sum, score_scale):
    scores = block_scores(queries, block[:, : queries.shape[1]], allowed, score_scale)
    return jnp.exp(scores - row_max[:, :, None]) / row_sum[:, :, None]


def forward_chain(kv_own, reach):
    blocks = [kv_own]
    moving = kv_own
    for offset in range(reach):
        moving = shifted(moving, "seq", 1)
        blocks.append(moving)
    return blocks


def again_chain(kv_own, reach):
    blocks = [kv_own]
    moving = kv_own
    for offset in range(reach):
        moving = shifted(moving, "seq", 1)
        blocks.append(moving)
    return blocks


def softmax_stats(queries, blocks, allowed_list, live_list, score_scale):
    frames, model_width = queries.shape
    row_max = jnp.full((HEAD_COUNT, frames), NEGATIVE, jnp.float32)
    row_sum = jnp.zeros((HEAD_COUNT, frames), jnp.float32)
    for offset in range(len(blocks)):

        def softmax_update(carry, block=blocks[offset], allowed=allowed_list[offset]):
            old_max, old_sum = carry
            scores = block_scores(queries, block[:, :model_width], allowed, score_scale)
            new_max = jnp.maximum(old_max, jnp.max(scores, axis=2))
            new_sum = old_sum * jnp.exp(old_max - new_max) + jnp.sum(
                jnp.exp(scores - new_max[:, :, None]), axis=2
            )
            return (new_max, new_sum)

        row_max, row_sum = lax.cond(
            live_list[offset], softmax_update, keep_same, (row_max, row_sum)
        )
    return (row_max, row_sum)


def attend_values(queries, blocks, allowed_list, live_list, row_max, row_sum, score_scale):
    frames, model_width = queries.shape
    total = jnp.zeros((frames, HEAD_COUNT, HEAD_DIM), jnp.float32)
    for offset in range(len(blocks)):

        def attend_update(carry, block=blocks[offset], allowed=allowed_list[offset]):
            probs = block_probs(queries, block, allowed, row_max, row_sum, score_scale).astype(
                jnp.bfloat16
            )
            return carry + jnp.einsum(
                "hqk,khd->qhd",
                probs,
                head_split(block[:, model_width:]),
                preferred_element_type=jnp.float32,
            )

        total = lax.cond(live_list[offset], attend_update, keep_same, total)
    return total.reshape(frames, model_width).astype(jnp.bfloat16)


def attention_grads(
    queries, grad_attended, blocks, allowed_list, live_list, row_max, row_sum, score_scale
):
    frames, model_width = queries.shape
    grad_heads = head_split(grad_attended)
    query_heads = head_split(queries)
    delta = jnp.zeros((HEAD_COUNT, frames), jnp.float32)
    for offset in range(len(blocks)):

        def attention_update(carry, block=blocks[offset], allowed=allowed_list[offset]):
            probs = block_probs(queries, block, allowed, row_max, row_sum, score_scale)
            dprobs = jnp.einsum(
                "qhd,khd->hqk",
                grad_heads,
                head_split(block[:, model_width:]),
                preferred_element_type=jnp.float32,
            )
            return carry + jnp.sum(probs * dprobs, axis=2)

        delta = lax.cond(live_list[offset], attention_update, keep_same, delta)
    grad_queries = jnp.zeros((frames, HEAD_COUNT, HEAD_DIM), jnp.float32)
    contributions = []
    for offset in range(len(blocks)):

        def block_grads(block=blocks[offset], allowed=allowed_list[offset]):
            probs = block_probs(queries, block, allowed, row_max, row_sum, score_scale)
            value_heads = head_split(block[:, model_width:])
            dprobs = jnp.einsum(
                "qhd,khd->hqk", grad_heads, value_heads, preferred_element_type=jnp.float32
            )
            dscores = (probs * (dprobs - delta[:, :, None]) * score_scale).astype(jnp.bfloat16)
            query_part = jnp.einsum(
                "hqk,khd->qhd",
                dscores,
                head_split(block[:, :model_width]),
                preferred_element_type=jnp.float32,
            )
            key_part = jnp.einsum(
                "hqk,qhd->khd", dscores, query_heads, preferred_element_type=jnp.float32
            )
            value_part = jnp.einsum(
                "hqk,qhd->khd",
                probs.astype(jnp.bfloat16),
                grad_heads,
                preferred_element_type=jnp.float32,
            )
            joined = jnp.concatenate(
                [key_part.reshape(frames, model_width), value_part.reshape(frames, model_width)],
                axis=1,
            )
            return (query_part, joined)

        def no_grads():
            return (
                jnp.zeros((frames, HEAD_COUNT, HEAD_DIM), jnp.float32),
                jnp.zeros((frames, 2 * model_width), jnp.float32),
            )

        query_part, joined = lax.cond(live_list[offset], block_grads, no_grads)
        grad_queries = grad_queries + query_part
        contributions.append(joined)
    return (grad_queries.reshape(frames, model_width), contributions)


def shards(
    tokens,
    lengths,
    key_mask,
    cotangent,
    w_qkv,
    w_out,
    w_up,
    w_down,
    ln1_gain,
    ln1_bias,
    ln2_gain,
    ln2_bias,
    out_bias,
    up_bias,
    down_bias,
):
    gathered = (
        lax.all_gather(w_qkv, "seq", axis=0, tiled=True),
        lax.all_gather(w_out, "seq", axis=0, tiled=True),
        lax.all_gather(w_up, "seq", axis=0, tiled=True),
        lax.all_gather(w_down, "seq", axis=0, tiled=True),
        lax.all_gather(ln1_gain, "seq", axis=0, tiled=True),
        lax.all_gather(ln1_bias, "seq", axis=0, tiled=True),
        lax.all_gather(ln2_gain, "seq", axis=0, tiled=True),
        lax.all_gather(ln2_bias, "seq", axis=0, tiled=True),
        lax.all_gather(out_bias, "seq", axis=0, tiled=True),
        lax.all_gather(up_bias, "seq", axis=0, tiled=True),
        lax.all_gather(down_bias, "seq", axis=0, tiled=True),
    )
    qkv_full, out_full, up_full, down_full = (gathered[0], gathered[1], gathered[2], gathered[3])
    gain_one, shift_one, gain_two, shift_two, out_shift, up_shift, down_shift = tuple(
        (member.astype(jnp.float32) for member in gathered[4:])
    )
    frames = tokens.shape[1]
    model_width = tokens.shape[2]
    cycle_size = lax.axis_size("seq")
    group_frames = frames * cycle_size
    longest = min(MAXCAP, group_frames // 2)
    reach = longest // frames
    my_index = lax.axis_index("seq")
    score_scale = HEAD_DIM ** (-0.5)
    seg_all = segment_ids(lengths[0], group_frames)
    key_on = key_mask[0]
    query_pos = my_index * frames + jnp.arange(frames, dtype=jnp.int32)
    query_seg = lax.dynamic_slice_in_dim(seg_all, my_index * frames, frames)
    allowed_list = [
        block_allowed(my_index, offset, frames, seg_all, key_on, query_seg, query_pos)
        for offset in range(reach + 1)
    ]
    live_list = [jnp.any(allowed) for allowed in allowed_list]
    inputs = tokens[0].astype(jnp.float32)
    normed_one = norm_rows(inputs, gain_one, shift_one).astype(jnp.bfloat16)
    qkv_low = jnp.dot(normed_one, qkv_full, preferred_element_type=jnp.float32).astype(jnp.bfloat16)
    queries = qkv_low[:, :model_width]
    kv_own = qkv_low[:, model_width:]
    blocks = forward_chain(kv_own, reach)
    row_max, row_sum = softmax_stats(queries, blocks, allowed_list, live_list, score_scale)
    attended = attend_values(
        queries, blocks, allowed_list, live_list, row_max, row_sum, score_scale
    )
    branch = jnp.dot(attended, out_full, preferred_element_type=jnp.float32) + out_shift
    middle = inputs + branch
    normed_two = norm_rows(middle, gain_two, shift_two).astype(jnp.bfloat16)
    up_value = jnp.dot(normed_two, up_full, preferred_element_type=jnp.float32) + up_shift
    activated = gelu_exact(up_value).astype(jnp.bfloat16)
    result = middle + jnp.dot(activated, down_full, preferred_element_type=jnp.float32) + down_shift
    grad_result = cotangent[0]
    grad_down_w = trans_times(activated, grad_result)
    grad_down_b = jnp.sum(grad_result.astype(jnp.float32), axis=0)
    grad_act = times_trans(grad_result, down_full)
    grad_up = jax.vjp(gelu_exact, up_value)[1](grad_act)[0].astype(jnp.bfloat16)
    grad_up_w = trans_times(normed_two, grad_up)
    grad_up_b = jnp.sum(grad_up.astype(jnp.float32), axis=0)
    grad_normed_two = times_trans(grad_up, up_full)
    pull_two = jax.vjp(norm_rows, middle, gain_two, shift_two)[1]
    grad_mid_norm, grad_gain_two, grad_shift_two = pull_two(grad_normed_two)
    grad_middle = grad_result.astype(jnp.float32) + grad_mid_norm
    grad_branch = grad_middle.astype(jnp.bfloat16)
    grad_out_w = trans_times(attended, grad_branch)
    grad_out_b = jnp.sum(grad_branch.astype(jnp.float32), axis=0)
    grad_attended = times_trans(grad_branch, out_full).astype(jnp.bfloat16)
    back_blocks = again_chain(kv_own, reach)
    grad_queries, contributions = attention_grads(
        queries, grad_attended, back_blocks, allowed_list, live_list, row_max, row_sum, score_scale
    )
    flowing = contributions[reach]
    for offset in range(reach - 1, -1, -1):
        flowing = (
            shifted(flowing.astype(jnp.bfloat16), "seq", -1).astype(flowing.dtype)
            + contributions[offset]
        )
    grad_qkv = jnp.concatenate([grad_queries, flowing], axis=1).astype(jnp.bfloat16)
    grad_qkv_w = trans_times(normed_one, grad_qkv)
    grad_normed_one = times_trans(grad_qkv, qkv_full)
    pull_one = jax.vjp(norm_rows, inputs, gain_one, shift_one)[1]
    grad_in_norm, grad_gain_one, grad_shift_one = pull_one(grad_normed_one)
    grad_inputs = (grad_middle + grad_in_norm).astype(jnp.bfloat16)
    shares = (
        lax.psum_scatter(
            grad_qkv_w.astype(jnp.bfloat16), "seq", scatter_dimension=0, tiled=True
        ).astype(jnp.float32),
        lax.psum_scatter(
            grad_out_w.astype(jnp.bfloat16), "seq", scatter_dimension=0, tiled=True
        ).astype(jnp.float32),
        lax.psum_scatter(
            grad_up_w.astype(jnp.bfloat16), "seq", scatter_dimension=0, tiled=True
        ).astype(jnp.float32),
        lax.psum_scatter(
            grad_down_w.astype(jnp.bfloat16), "seq", scatter_dimension=0, tiled=True
        ).astype(jnp.float32),
        lax.psum_scatter(
            grad_gain_one.astype(jnp.bfloat16), "seq", scatter_dimension=0, tiled=True
        ).astype(jnp.float32),
        lax.psum_scatter(
            grad_shift_one.astype(jnp.bfloat16), "seq", scatter_dimension=0, tiled=True
        ).astype(jnp.float32),
        lax.psum_scatter(
            grad_gain_two.astype(jnp.bfloat16), "seq", scatter_dimension=0, tiled=True
        ).astype(jnp.float32),
        lax.psum_scatter(
            grad_shift_two.astype(jnp.bfloat16), "seq", scatter_dimension=0, tiled=True
        ).astype(jnp.float32),
        lax.psum_scatter(
            grad_out_b.astype(jnp.bfloat16), "seq", scatter_dimension=0, tiled=True
        ).astype(jnp.float32),
        lax.psum_scatter(
            grad_up_b.astype(jnp.bfloat16), "seq", scatter_dimension=0, tiled=True
        ).astype(jnp.float32),
        lax.psum_scatter(
            grad_down_b.astype(jnp.bfloat16), "seq", scatter_dimension=0, tiled=True
        ).astype(jnp.float32),
    )
    reduced = (
        lax.psum(shares[0].astype(jnp.bfloat16), "batch").astype(jnp.float32),
        lax.psum(shares[1].astype(jnp.bfloat16), "batch").astype(jnp.float32),
        lax.psum(shares[2].astype(jnp.bfloat16), "batch").astype(jnp.float32),
        lax.psum(shares[3].astype(jnp.bfloat16), "batch").astype(jnp.float32),
        lax.psum(shares[4].astype(jnp.bfloat16), "batch").astype(jnp.float32),
        lax.psum(shares[5].astype(jnp.bfloat16), "batch").astype(jnp.float32),
        lax.psum(shares[6].astype(jnp.bfloat16), "batch").astype(jnp.float32),
        lax.psum(shares[7].astype(jnp.bfloat16), "batch").astype(jnp.float32),
        lax.psum(shares[8].astype(jnp.bfloat16), "batch").astype(jnp.float32),
        lax.psum(shares[9].astype(jnp.bfloat16), "batch").astype(jnp.float32),
        lax.psum(shares[10].astype(jnp.bfloat16), "batch").astype(jnp.float32),
    )
    return (
        result.astype(jnp.bfloat16)[None],
        grad_inputs[None],
        reduced[0],
        reduced[1],
        reduced[2],
        reduced[3],
        reduced[4],
        reduced[5],
        reduced[6],
        reduced[7],
        reduced[8],
        reduced[9],
        reduced[10],
    )


LANES = 128
TILE = 512
UTTERANCES = 4
SHRINK = 1
PARAMS = pltpu.CompilerParams(dimension_semantics=("arbitrary",), vmem_limit_bytes=56 << 20)


def dot_nt(left, right):
    return lax.dot_general(
        left, right, (((1,), (1,)), ((), ())), preferred_element_type=jnp.float32
    )


def dot_nn(left, right):
    return lax.dot_general(
        left, right, (((1,), (0,)), ((), ())), preferred_element_type=jnp.float32
    )


def dot_tn(left, right):
    return lax.dot_general(
        left, right, (((0,), (0,)), ((), ())), preferred_element_type=jnp.float32
    )


def norm_stats(values):
    centre = jnp.mean(values, axis=-1, keepdims=True)
    centred = values - centre
    spread = jnp.mean(centred * centred, axis=-1, keepdims=True)
    inverse = lax.rsqrt(spread + EPSILON)
    return centred * inverse, inverse


def norm_back(grad, normed, inverse, gain):
    g = grad * gain
    return inverse * (
        g
        - jnp.mean(g, axis=-1, keepdims=True)
        - normed * jnp.mean(g * normed, axis=-1, keepdims=True)
    )


def whole(*shape):
    return pl.BlockSpec(shape, lambda *_: (0,) * len(shape))


def like(shape, kind):
    return jax.ShapeDtypeStruct(shape, kind)


def call(kernel, name, grid, in_specs, out_specs, out_shape, scratch=(), flops=0):
    def run(ids, *args):
        bytes_accessed = sum(a.size * a.dtype.itemsize for a in args)
        return pl.pallas_call(
            kernel,
            out_shape=out_shape,
            grid_spec=pltpu.PrefetchScalarGridSpec(
                num_scalar_prefetch=1,
                grid=(grid,),
                in_specs=in_specs,
                out_specs=out_specs,
                scratch_shapes=list(scratch),
            ),
            compiler_params=PARAMS,
            cost_estimate=pl.CostEstimate(
                flops=flops // SHRINK,
                bytes_accessed=2 * bytes_accessed // SHRINK,
                transcendentals=0,
            ),
            name=name,
        )(ids, *args)

    return run


CORE, CHIP_X, SQUARE, Y_BIT = 0, 1, 2, 3


def norm_kernel(ids, tokens, vectors, out):
    normed, _ = norm_stats(tokens[...].astype(jnp.float32))
    out[...] = (normed * vectors[0:1, :] + vectors[1:2, :]).astype(jnp.bfloat16)


def project_kernel(ids, own, y_one, z_one, top, bottom, w_own, w_other, out, leaving, natural):
    square = ids[SQUARE]
    corner = jnp.where(pl.program_id(0) < 2, top[...], bottom[...])
    pieces = (own[...], y_one[...], z_one[...], corner)
    rows = jnp.concatenate(pieces, axis=0)
    size = corner.shape[0]
    mine = dot_nn(rows, w_own[...]).astype(jnp.bfloat16)
    other = dot_nn(rows, w_other[...]).astype(jnp.bfloat16)
    for j in range(4):
        at = pl.ds(square ^ j, 1)
        natural[at] = pieces[j][None]
        out[at] = mine[None, j * size : (j + 1) * size]
        leaving[at] = other[None, j * size : (j + 1) * size]


def head_lanes(block, head):
    lane = lax.broadcasted_iota(jnp.int32, block.shape, 1)
    keep = (lane < HEAD_DIM) if head == 0 else (lane >= HEAD_DIM)
    return jnp.where(keep, block, jnp.zeros_like(block))


def join_heads(ids, own, came, qkv):
    half = own.shape[0]
    for rows, side in ((own, ids[CORE]), (came, 1 - ids[CORE])):
        at = pl.ds(pl.multiple_of(side * half, half), half)
        qkv[at, 0:LANES] = rows[:, 0:LANES] * jnp.bfloat16(HEAD_DIM ** (-0.5))
        qkv[at, LANES : 3 * LANES] = rows[:, LANES : 3 * LANES]


def first_frames(bounds, positions):
    start = jnp.zeros_like(positions)
    for u in range(1, UTTERANCES):
        start = jnp.where(positions >= bounds[2, u], bounds[2, u], start)
    return start


def spread_places(places_row, column):
    for j in range(places_row.shape[1] // TILE):
        row = places_row[:, j * TILE : (j + 1) * TILE]
        column[j * TILE : (j + 1) * TILE, :] = jnp.transpose(
            jnp.broadcast_to(row, (LANES, TILE))
        )


def allowed_keys(column, at, start, diagonal):
    places = jnp.concatenate([column[pl.ds(at, TILE), :]] * (TILE // LANES), axis=1)
    allowed = places >= start
    if diagonal:
        key = lax.broadcasted_iota(jnp.int32, (TILE, TILE), 0)
        query = lax.broadcasted_iota(jnp.int32, (TILE, TILE), 1)
        allowed = (allowed & (key < query)) | (key == query)
    return allowed


def row_starts(bounds, base):
    return first_frames(bounds, base + lax.broadcasted_iota(jnp.int32, (1, TILE), 1)).astype(
        jnp.float32
    )


def attend_kernel(
    ids, bounds, own, came, places_row, out, lse, qkv, turned, column, scores, top, total, acc
):
    tile = pl.program_id(0)
    base = pl.multiple_of(tile * TILE, TILE)

    @pl.when(tile == 0)
    def _():
        join_heads(ids, own, came, qkv)
        spread_places(places_row, column)
        for j in range(qkv.shape[0] // TILE):
            rows = slice(j * TILE, (j + 1) * TILE)
            turned[:, rows] = jnp.transpose(qkv[rows, 2 * LANES : 3 * LANES])

    queries = [head_lanes(qkv[pl.ds(base, TILE), 0:LANES], head) for head in range(2)]
    top[...] = jnp.full_like(top, NEGATIVE)
    total[...] = jnp.zeros_like(total)
    acc[...] = jnp.zeros_like(acc)

    start = row_starts(bounds, base)

    def step(j, diagonal):
        at = pl.multiple_of(j * TILE, TILE)
        keys = qkv[pl.ds(at, TILE), LANES : 2 * LANES]
        allowed = allowed_keys(column, at, start, diagonal)
        for head in range(2):
            value = jnp.where(allowed, dot_nt(keys, queries[head]), NEGATIVE)
            scores[head, j] = value
            top[head : head + 1, :] = jnp.maximum(
                top[head : head + 1, :], jnp.max(value, axis=0, keepdims=True)
            )

    def first_pass(j, carry):
        step(j, False)
        return carry

    def second_pass(j, carry):
        at = pl.multiple_of(j * TILE, TILE)
        for head in range(2):
            probs = jnp.exp(scores[head, j] - top[head : head + 1, :])
            total[head : head + 1, :] += jnp.sum(probs, axis=0, keepdims=True)
            values = turned[head * HEAD_DIM : (head + 1) * HEAD_DIM, pl.ds(at, TILE)]
            acc[head] += dot_nn(values, probs.astype(jnp.bfloat16))
        return carry

    lax.fori_loop(bounds[0, tile], tile, first_pass, 0)
    step(tile, True)
    lax.fori_loop(bounds[0, tile], tile + 1, second_pass, 0)
    both = jnp.concatenate([acc[0] / total[0:1, :], acc[1] / total[1:2, :]], axis=0)
    out[0] = jnp.transpose(both).astype(jnp.bfloat16)
    lse[:, pl.ds(base, TILE)] = top[...] + jnp.log(total[...])


def block_order(i):
    return 2 * (i % 4) + i // 4


def attend(ids, bounds, own, came, places):
    rows = 2 * own.shape[0]
    return pl.pallas_call(
        attend_kernel,
        out_shape=(like((8, TILE, LANES), jnp.bfloat16), like((2, rows), jnp.float32)),
        grid_spec=pltpu.PrefetchScalarGridSpec(
            num_scalar_prefetch=2,
            grid=(rows // TILE,),
            in_specs=[
                whole(*own.shape),
                whole(*came.shape),
                whole(1, rows),
            ],
            out_specs=[
                pl.BlockSpec((1, TILE, LANES), lambda i, *_: (block_order(i), 0, 0)),
                whole(2, rows),
            ],
            scratch_shapes=[
                pltpu.VMEM((rows, 3 * LANES), jnp.bfloat16),
                pltpu.VMEM((LANES, rows), jnp.bfloat16),
                pltpu.VMEM((rows, LANES), jnp.float32),
                pltpu.VMEM((2, rows // TILE, TILE, TILE), jnp.float32),
                pltpu.VMEM((2, TILE), jnp.float32),
                pltpu.VMEM((2, TILE), jnp.float32),
                pltpu.VMEM((2, HEAD_DIM, TILE), jnp.float32),
            ],
        ),
        compiler_params=PARAMS,
        cost_estimate=pl.CostEstimate(
            flops=rows * rows * 256 // SHRINK, bytes_accessed=rows * 2400, transcendentals=rows * rows
        ),
        name="attend",
    )(ids, bounds, own, came, places)


def attend_back_kernel(
    ids,
    bounds,
    own,
    came,
    grad_own,
    grad_came,
    attended,
    places_row,
    lse,
    out,
    leaving,
    qkv,
    grad,
    delta,
    grad_queries,
    grad_kv,
    column,
):
    tile = pl.program_id(0)
    base = pl.multiple_of(tile * TILE, TILE)
    core = ids[CORE]

    @pl.when(tile == 0)
    def _():
        join_heads(ids, own, came, qkv)
        spread_places(places_row, column)
        grad_queries[...] = jnp.zeros_like(grad_queries)
        for j in range(4):
            for rows, side in ((grad_own, core), (grad_came, 1 - core)):
                at = pl.multiple_of((4 * side + j) * TILE, TILE)
                block = rows[pl.ds(2 * j + core, 1)].reshape(TILE, LANES)
                grad[pl.ds(at, TILE), :] = block
                product = block.astype(jnp.float32) * attended[
                    pl.ds(2 * j + side, 1)
                ].reshape(TILE, LANES).astype(jnp.float32)
                turned = jnp.transpose(product)
                delta[0:1, pl.ds(at, TILE)] = jnp.sum(turned[:HEAD_DIM], axis=0, keepdims=True)
                delta[1:2, pl.ds(at, TILE)] = jnp.sum(turned[HEAD_DIM:], axis=0, keepdims=True)

    keys = qkv[pl.ds(base, TILE), LANES : 2 * LANES]
    values = qkv[pl.ds(base, TILE), 2 * LANES : 3 * LANES]
    turned_keys = jnp.transpose(keys)
    grad_kv[...] = jnp.zeros_like(grad_kv)

    def step(i, diagonal):
        at = pl.multiple_of(i * TILE, TILE)
        scaled = qkv[pl.ds(at, TILE), 0:LANES]
        grads = grad[pl.ds(at, TILE), :]
        allowed = allowed_keys(column, base, row_starts(bounds, at), diagonal)
        key_part = grad_kv[0]
        value_part = grad_kv[1]
        for head in range(2):
            queries = head_lanes(scaled, head)
            head_grads = head_lanes(grads, head)
            scores = jnp.where(allowed, dot_nt(keys, queries), NEGATIVE)
            probs = jnp.exp(scores - lse[head : head + 1, pl.ds(at, TILE)])
            dprobs = dot_nt(values, head_grads)
            dscores = (probs * (dprobs - delta[head : head + 1, pl.ds(at, TILE)])).astype(
                jnp.bfloat16
            )
            value_part = value_part + dot_nn(probs.astype(jnp.bfloat16), head_grads)
            key_part = key_part + dot_nn(dscores, queries)
            lanes = slice(head * HEAD_DIM, (head + 1) * HEAD_DIM)
            grad_queries[lanes, pl.ds(at, TILE)] += dot_nn(turned_keys[lanes, :], dscores)
        grad_kv[0] = key_part
        grad_kv[1] = value_part

    def later_step(i, carry):
        step(i, False)
        return carry

    step(tile, True)
    lax.fori_loop(tile + 1, bounds[1, tile], later_step, 0)

    def store(target):
        at = pl.ds(pl.multiple_of((tile % 4) * TILE, TILE), TILE)
        target[at, 0:LANES] = (
            jnp.transpose(grad_queries[:, pl.ds(base, TILE)]) * HEAD_DIM ** (-0.5)
        ).astype(jnp.bfloat16)
        target[at, LANES : 2 * LANES] = grad_kv[0].astype(jnp.bfloat16)
        target[at, 2 * LANES : 3 * LANES] = grad_kv[1].astype(jnp.bfloat16)

    @pl.when(tile // 4 == core)
    def _():
        store(out)

    @pl.when(tile // 4 != core)
    def _():
        store(leaving)


def attend_back(ids, bounds, own, came, grad_own, grad_came, attended, places, lse):
    half = own.shape[0]
    rows = 2 * half
    return pl.pallas_call(
        attend_back_kernel,
        out_shape=(like(own.shape, jnp.bfloat16), like(own.shape, jnp.bfloat16)),
        grid_spec=pltpu.PrefetchScalarGridSpec(
            num_scalar_prefetch=2,
            grid=(rows // TILE,),
            in_specs=[
                whole(*own.shape),
                whole(*came.shape),
                whole(*grad_own.shape),
                whole(*grad_came.shape),
                whole(*attended.shape),
                whole(1, rows),
                whole(2, rows),
            ],
            out_specs=[whole(*own.shape), whole(*own.shape)],
            scratch_shapes=[
                pltpu.VMEM((rows, 3 * LANES), jnp.bfloat16),
                pltpu.VMEM((rows, LANES), jnp.bfloat16),
                pltpu.VMEM((2, rows), jnp.float32),
                pltpu.VMEM((LANES, rows), jnp.float32),
                pltpu.VMEM((2, TILE, LANES), jnp.float32),
                pltpu.VMEM((rows, LANES), jnp.float32),
            ],
        ),
        compiler_params=PARAMS,
        cost_estimate=pl.CostEstimate(
            flops=rows * rows * 640 // SHRINK, bytes_accessed=rows * 2400, transcendentals=rows * rows
        ),
        name="attend_back",
    )(ids, bounds, own, came, grad_own, grad_came, attended, places, lse)


def attend_bounds(start, starts, rows):
    tiles = rows // TILE
    first = start[:: TILE]
    key_last = jnp.arange(1, tiles + 1, dtype=jnp.int32) * TILE - 1
    far_end = jnp.sum((first[None, :] <= key_last[:, None]).astype(jnp.int32), axis=1)
    starts = jnp.pad(starts, (0, tiles - starts.shape[0]))
    return jnp.stack([first // TILE, far_end, starts]).astype(jnp.int32)


def out_kernel(ids, own, came, tokens, w_out, vectors, attended, middle, normed):
    core = ids[CORE]
    rows, width = tokens.shape
    mine, other = [], []
    for j in range(4):
        mine.append(own[pl.ds(2 * j + core, 1)].reshape(rows, LANES))
        other.append(came[pl.ds(2 * j + core, 1)].reshape(rows, LANES))
    mine, other = jnp.concatenate(mine, axis=1), jnp.concatenate(other, axis=1)
    first = jnp.where(core == 0, mine, other)
    second = jnp.where(core == 0, other, mine)
    joined = jnp.concatenate([first, second], axis=1)
    attended[...] = joined
    branch = dot_nn(joined, w_out[...].reshape(width, width)) + vectors[4:5, :]
    value = tokens[...].astype(jnp.float32) + branch
    middle[...] = value
    xhat, _ = norm_stats(value)
    normed[...] = (xhat * vectors[2:3, :] + vectors[3:4, :]).astype(jnp.bfloat16)


def forward_kernel(
    ids,
    normed_own,
    normed_came,
    grad_own,
    grad_came,
    up_a,
    up_b,
    down_a,
    down_b,
    vectors,
    act,
    grad_up,
    up_bias,
    result_own,
    result_came,
    back_own,
    back_came,
    result,
    back,
):
    step = pl.program_id(0)
    core = ids[CORE]
    frames, width = normed_own.shape

    @pl.when(step == 0)
    def _():
        result[...] = jnp.zeros_like(result)
        back[...] = jnp.zeros_like(back)

    def weave(first, second, axis):
        parts = []
        for k in range(2):
            for block in (first, second):
                at = [slice(None), slice(None)]
                at[axis] = slice(k * LANES, (k + 1) * LANES)
                parts.append(block[tuple(at)])
        return jnp.concatenate(parts, axis=axis)

    wide_step = 2 * LANES
    w_up = weave(up_a[...].reshape(width, wide_step), up_b[...].reshape(width, wide_step), 1)
    w_down = weave(down_a[...].reshape(wide_step, width), down_b[...].reshape(wide_step, width), 0)
    shift = jnp.where(
        core == 0,
        weave(vectors[6:7, :], vectors[7:8, :], 1),
        weave(vectors[8:9, :], vectors[9:10, :], 1),
    )
    sides = ((normed_own, grad_own), (normed_came, grad_came))
    values = [dot_nn(normed[...], w_up) + shift for normed, _ in sides]
    slopes = [dot_nt(grad[...], w_down) for _, grad in sides]
    bias = jnp.zeros((1, 4 * LANES), jnp.float32)
    for side, (value, slope) in enumerate(zip(values, slopes)):
        half = 0.5 + 0.5 * lax.erf(value * 0.7071067811865476)
        bell = jnp.exp(-0.5 * value * value) * 0.3989422804014327
        activated = (value * half).astype(jnp.bfloat16)
        change = (slope * (half + value * bell)).astype(jnp.bfloat16)
        act[side] = activated
        grad_up[side] = change
        bias = bias + jnp.sum(change.astype(jnp.float32), axis=0, keepdims=True)
        result[side] += dot_nn(activated, w_down)
        back[side] += dot_nt(change, w_up)
    for k in range(4):
        at = slice((k // 2) * LANES, (k // 2 + 1) * LANES)
        up_bias[k % 2 : k % 2 + 1, at] = bias[:, k * LANES : (k + 1) * LANES]

    @pl.when(step == 3)
    def _():
        result_own[...] = result[0]
        result_came[...] = result[1].astype(jnp.bfloat16)
        back_own[...] = back[0]
        back_came[...] = back[1].astype(jnp.bfloat16)


def middle_kernel(
    ids, back_own, back_came, middle, cotangent, w_out, vectors, grad_middle, grad_branch, out, sums
):
    step = pl.program_id(0)
    xhat, inverse = norm_stats(middle[...])
    grad = back_own[...] + back_came[...].astype(jnp.float32)
    value = cotangent[...].astype(jnp.float32) + norm_back(grad, xhat, inverse, vectors[2:3, :])
    grad_middle[...] = value
    low = value.astype(jnp.bfloat16)
    grad_branch[...] = low

    @pl.when(step == 0)
    def _():
        sums[...] = jnp.zeros_like(sums)

    sums[0:1, :] += jnp.sum(grad * xhat, axis=0, keepdims=True)
    sums[1:2, :] += jnp.sum(grad, axis=0, keepdims=True)
    sums[2:3, :] += jnp.sum(low.astype(jnp.float32), axis=0, keepdims=True)
    sums[3:4, :] += jnp.sum(cotangent[...].astype(jnp.float32), axis=0, keepdims=True)
    width = w_out.shape[-1]
    spread = dot_nt(low, w_out[...].reshape(width, width)).astype(jnp.bfloat16)
    for group in range(8):
        out[block_order(group)] = spread[:, group * LANES : (group + 1) * LANES]


def grad_out_kernel(ids, attended, grad_branch, kept, leaving):
    core = ids[CORE]
    grad = dot_tn(attended[...], grad_branch[...]).astype(jnp.bfloat16)
    half = grad.shape[1] // 2
    shape = kept.shape
    kept[...] = jnp.where(core == 0, grad[:, :half], grad[:, half:]).reshape(shape)
    leaving[...] = jnp.where(core == 0, grad[:, half:], grad[:, :half]).reshape(shape)


def grad_down_kernel(ids, act, grad_own, grad_came, out):
    grad = dot_tn(act[0], grad_own[...]) + dot_tn(act[1], grad_came[...])
    out[...] = grad.astype(jnp.bfloat16)


def grad_up_kernel(ids, normed_own, normed_came, grad_up, out_own, out_came, kept, leaving):
    chip_x = ids[CHIP_X]
    grad = (dot_tn(normed_own[...], grad_up[0]) + dot_tn(normed_came[...], grad_up[1])).astype(
        jnp.bfloat16
    )
    half = grad.shape[1] // 2
    shape = kept.shape[:2] + (half,)
    kept[:, :, :half] = jnp.where(chip_x == 0, grad[:, :half], grad[:, half:]).reshape(shape)
    leaving[:, :, :half] = jnp.where(chip_x == 0, grad[:, half:], grad[:, :half]).reshape(shape)
    more = (out_own[...].astype(jnp.float32) + out_came[...].astype(jnp.float32)).astype(
        jnp.bfloat16
    )
    cut = more.shape[2] // 2
    kept[:, :, half:] = jnp.where(chip_x == 0, more[:, :, :cut], more[:, :, cut:])
    leaving[:, :, half:] = jnp.where(chip_x == 0, more[:, :, cut:], more[:, :, :cut])


def back_project_kernel(
    ids,
    own,
    came,
    w_own,
    w_other,
    first,
    y_out,
    z_out,
    keep_left,
    keep_right,
    grads,
):
    square = ids[SQUARE]
    size, width = first.shape
    half = width // 2
    rows = 4 * size
    value = dot_nt(own[...].reshape(rows, 3 * LANES), w_own[...])
    value = value + dot_nt(came[...].reshape(rows, 3 * LANES), w_other[...])
    grads[...] = value.reshape(4, size, width)
    first[...] = grads[square]
    y_out[0] = grads[square ^ 1, :, :half].astype(jnp.bfloat16)
    keep_right[...] = grads[square ^ 1, :, half:]
    z_out[0] = grads[square ^ 2, :, half:].astype(jnp.bfloat16)
    keep_left[...] = grads[square ^ 2, :, :half]
    y_out[1] = grads[square ^ 3, :, :half].astype(jnp.bfloat16)
    z_out[1] = grads[square ^ 3, :, half:].astype(jnp.bfloat16)


def first_sums_kernel(
    ids, first, y_out, z_out, keep_left, keep_right, natural, vectors, sums
):
    square = ids[SQUARE]
    half = first.shape[1] // 2
    wide = jnp.float32
    parts = (
        (first[:, :half], first[:, half:]),
        (y_out[0].astype(wide), keep_right[...]),
        (keep_left[...], z_out[0].astype(wide)),
        (y_out[1].astype(wide), z_out[1].astype(wide)),
    )

    @pl.when(pl.program_id(0) == 0)
    def _():
        sums[...] = jnp.zeros_like(sums)

    for j in range(4):
        for side in range(2):
            lanes = slice(side * half, (side + 1) * half)
            value = parts[j][side]
            rows = natural[square ^ j, :, lanes].astype(wide)
            normed = (rows - vectors[1:2, lanes]) / vectors[0:1, lanes]
            sums[0:1, lanes] += jnp.sum(value * normed, axis=0, keepdims=True)
            sums[1:2, lanes] += jnp.sum(value, axis=0, keepdims=True)


def second_kernel(ids, keep_left, keep_right, y_came, z_came, z_out, y_out):
    z_out[...] = (keep_left[...] + y_came[1].astype(jnp.float32)).astype(jnp.bfloat16)
    y_out[...] = (keep_right[...] + z_came[1].astype(jnp.float32)).astype(jnp.bfloat16)


def last_kernel(ids, first, y_came, z_came, z_second, y_second, tokens, grad_middle, vectors, out):
    wide = jnp.float32
    left = y_came[0].astype(wide) + z_second[...].astype(wide)
    right = z_came[0].astype(wide) + y_second[...].astype(wide)
    grad = first[...] + jnp.concatenate([left, right], axis=1)
    xhat, inverse = norm_stats(tokens[...].astype(wide))
    out[...] = (grad_middle[...] + norm_back(grad, xhat, inverse, vectors[0:1, :])).astype(
        jnp.bfloat16
    )


def grad_heads_kernel(ids, normed, grads, out):
    out[...] = dot_tn(normed[...], grads[...]).astype(jnp.bfloat16)


def spread_kernel(
    ids,
    heads,
    heads_came,
    down,
    down_came,
    mixed,
    mixed_x,
    mixed_core,
    mixed_both,
    qkv_out,
    out_out,
    up_out,
    down_out,
):
    wide = jnp.float32
    core, chip_x = ids[CORE], ids[CHIP_X]

    def ordered(side, own, other):
        return jnp.where(side == 0, own, other), jnp.where(side == 0, other, own)

    for side, blocks in enumerate(ordered(core, heads[...], heads_came[...])):
        for j in range(4):
            for k in range(3):
                at = k * 8 * LANES + (4 * side + j) * LANES
                qkv_out[:, at : at + LANES] = blocks[j, :, k * LANES : (k + 1) * LANES].astype(wide)
    rows = down.shape[0]
    for side, block in enumerate(ordered(core, down[...], down_came[...])):
        down_out[side * rows : (side + 1) * rows, :] = block.astype(wide)
    own = ordered(chip_x, mixed[...], mixed_x[...])
    came = ordered(chip_x, mixed_core[...], mixed_both[...])
    width = out_out.shape[1]
    step = 2 * LANES
    for x in range(2):
        for side, block in enumerate(ordered(core, own[x], came[x])):
            for j in range(4):
                at = (4 * x + j) * 2 * step + side * step
                up_out[:, at : at + step] = block[:, j * step : (j + 1) * step].astype(wide)
            at = side * 2 * step + x * step
            out_out[:, at : at + step] = block[:, width:].astype(wide)


def hop_batch(block, bit):
    size = lax.axis_size("batch")
    return lax.ppermute(block, "batch", [(i, i ^ bit) for i in range(size)])


def hop_seq(block, bits):
    size = lax.axis_size("seq")
    return lax.ppermute(block, "seq", [(i, i ^ bits) for i in range(size)])


def swap_halves(block):
    batches, seqs = lax.axis_size("batch"), lax.axis_size("seq")
    route = []
    for b in range(batches):
        for s in range(seqs):
            target = ((b & ~1) | (s >> 2)) * seqs + ((s & 3) | ((b & 1) << 2))
            route.append((b * seqs + s, target))
    return lax.ppermute(block, ("batch", "seq"), route)


def after(value, *anchors):
    return lax.optimization_barrier((value,) + anchors)[0]


def trade(block, groups):
    return lax.all_to_all(block, "seq", 0, 0, tiled=True, axis_index_groups=groups)


IN_SQUARE = [[0, 1, 2, 3], [4, 5, 6, 7]]
ALONG_Z = [[0, 2, 4, 6], [1, 3, 5, 7]]


def square_shards(
    tokens,
    lengths,
    key_mask,
    cotangent,
    w_qkv,
    w_out,
    w_up,
    w_down,
    ln1_gain,
    ln1_bias,
    ln2_gain,
    ln2_bias,
    out_bias,
    up_bias,
    down_bias,
):
    low, wide = jnp.bfloat16, jnp.float32
    batch_index = lax.axis_index("batch")
    seq_index = lax.axis_index("seq")
    core = batch_index & 1
    chip_x = batch_index >> 1
    square = seq_index & 3
    y_bit = seq_index & 1
    ids = jnp.stack([core, chip_x, square, y_bit]).astype(jnp.int32)
    frames, width = tokens.shape[1], tokens.shape[2]
    rows = 8 * frames
    part = width // 8
    quarter = 2 * core + chip_x

    up_piece = lax.dynamic_index_in_dim(w_up.reshape(part, 8, 4, LANES), quarter, 2, False)
    down_piece = lax.dynamic_slice_in_dim(w_down, quarter * part, part, 0)
    out_piece = lax.dynamic_slice_in_dim(w_out, batch_index * (part // 4), part // 4, 0)
    bundle = jnp.concatenate([down_piece, up_piece.reshape(part, width), out_piece], axis=0)
    deep = bundle.shape[0]

    tokens_here = swap_halves(tokens[0])
    heads = lax.dynamic_slice_in_dim(w_qkv.reshape(part, 3, 8, LANES), 4 * core, 4, 2)
    heads = heads.transpose(2, 0, 1, 3).reshape(4, part, 3 * LANES)
    small = jnp.concatenate(
        [
            jnp.stack([ln1_gain, ln1_bias, ln2_gain, ln2_bias, out_bias, down_bias]),
            up_bias.reshape(4, part),
            jnp.zeros((6, part), low),
        ],
        axis=0,
    )
    small = jnp.broadcast_to(jnp.pad(small, ((0, 0), (0, 2 * part)))[None], (4, 16, 3 * part))
    heads = jnp.concatenate([heads, small], axis=1)
    came = lax.all_to_all(jnp.concatenate([heads, heads], axis=0), "seq", 0, 0, tiled=True)
    vectors = came[:, part:, :part].astype(wide).transpose(1, 0, 2).reshape(16, width)
    w_heads = came[:, :part].reshape(width, 3 * LANES)
    w_other = hop_batch(w_heads, 1)

    meta = jnp.concatenate([key_mask[0], jnp.pad(lengths[0], (0, LANES - lengths.shape[1]))])
    meta = meta.reshape(-1, LANES)
    meta = jnp.where(core == (seq_index >> 2), meta, hop_batch(meta, 1)).reshape(-1)
    ends = jnp.cumsum(meta[rows : rows + lengths.shape[1]])
    starts = ends - meta[rows : rows + lengths.shape[1]]
    positions = jnp.arange(rows, dtype=jnp.int32)
    start = jnp.max(
        jnp.where(starts[None, :] <= positions[:, None], starts[None, :], 0), axis=1
    ).astype(jnp.int32)
    bounds = attend_bounds(start, starts, rows)
    places = jnp.where(meta[:rows] == 1, positions, -1).astype(wide)[None, :]

    fourth = frames // 4
    slab = pl.BlockSpec((fourth, width), lambda i, *_: (i, 0))
    normed_one = call(
        norm_kernel, "norm", 4, [slab, whole(16, width)], slab, like((frames, width), low)
    )(ids, tokens_here, vectors)
    y_one = hop_seq(normed_one, 1)
    z_one = hop_seq(normed_one, 2)
    bundle = lax.all_gather(after(bundle, tokens_here, came), ("seq", "batch"), axis=0, tiled=True)
    bundle = bundle.reshape(8, 4, deep, width)
    half = frames // 2
    top, bottom = hop_seq(y_one[:half], 2), hop_seq(z_one[half:], 1)
    heads_shape = (4, frames, 3 * LANES)
    top_slab = pl.BlockSpec((fourth, width), lambda i, *_: (jnp.minimum(i, 1), 0))
    bottom_slab = pl.BlockSpec((fourth, width), lambda i, *_: (jnp.maximum(i, 2) - 2, 0))
    heads_slab = pl.BlockSpec((4, fourth, 3 * LANES), lambda i, *_: (0, i, 0))
    natural_slab = pl.BlockSpec((4, fourth, width), lambda i, *_: (0, i, 0))
    heads_like = like(heads_shape, low)
    qkv_own, leaving, natural = call(
        project_kernel,
        "project",
        4,
        [slab] * 3 + [top_slab, bottom_slab] + [whole(*w_heads.shape)] * 2,
        [heads_slab, heads_slab, natural_slab],
        (heads_like, heads_like, like((4, frames, width), low)),
        flops=2 * 4 * frames * width * 6 * LANES,
    )(ids, normed_one, y_one, z_one, top, bottom, w_heads, w_other)
    qkv_came = hop_batch(leaving, 1).reshape(4 * frames, 3 * LANES)
    qkv_own = qkv_own.reshape(4 * frames, 3 * LANES)
    natural = natural.reshape(4 * frames, width)
    cotangent_own = swap_halves(after(cotangent[0], leaving))

    attended_heads, lse = attend(ids, bounds, qkv_own, qkv_came, places)
    cotangent_came = hop_batch(cotangent_own, 1)

    mine = trade(attended_heads, IN_SQUARE)
    mine_came = hop_batch(mine, 1)
    blocks = pl.BlockSpec((8, half, LANES), lambda i, *_: (0, i, 0))
    wide_slab = pl.BlockSpec((half, width), lambda i, *_: (i, 0))
    w_out_spec = pl.BlockSpec(
        (8, 4, part // 4, width), lambda *_: (0, 0, (deep * 4) // part - 1, 0)
    )
    attended, middle, normed_two = call(
        out_kernel,
        "out_project",
        2,
        [blocks, blocks, wide_slab, w_out_spec, whole(16, width)],
        [wide_slab] * 3,
        (like((frames, width), low), like((frames, width), wide), like((frames, width), low)),
        flops=2 * frames * width * width,
    )(ids, mine, mine_came, tokens_here, bundle, vectors)
    normed_two_came = hop_batch(normed_two, 1)

    up_specs = [
        pl.BlockSpec((8, 1, part, 2 * LANES), lambda s, ids, k=k: (0, 2 * k + ids[CORE], 1, s))
        for k in range(2)
    ]
    down_specs = [
        pl.BlockSpec((2, 1, part, width), lambda s, ids, k=k: (s, 2 * k + ids[CORE], 0, 0))
        for k in range(2)
    ]
    hidden = pl.BlockSpec((2, frames, 4 * LANES), lambda s, *_: (0, 0, s))
    act, grad_up, up_sums, result_own, result_leaving, back_own, back_leaving = call(
        forward_kernel,
        "feed_forward",
        4,
        [whole(frames, width)] * 4
        + up_specs
        + down_specs
        + [pl.BlockSpec((16, 2 * LANES), lambda s, *_: (0, s))],
        [hidden, hidden, pl.BlockSpec((8, 2 * LANES), lambda s, *_: (0, s))]
        + [whole(frames, width)] * 4,
        (
            like((2, frames, 2 * width), low),
            like((2, frames, 2 * width), low),
            like((8, width), wide),
            like((frames, width), wide),
            like((frames, width), low),
            like((frames, width), wide),
            like((frames, width), low),
        ),
        scratch=[pltpu.VMEM((2, frames, width), wide)] * 2,
        flops=2 * 4 * 2 * frames * width * 2 * width,
    )(
        ids,
        normed_two,
        normed_two_came,
        cotangent_own,
        cotangent_came,
        bundle,
        bundle,
        bundle,
        bundle,
        vectors,
    )
    back_came = hop_batch(back_leaving, 1)

    hidden_pair = pl.BlockSpec((2, frames, 4 * LANES), lambda s, *_: (0, 0, s))
    down = call(
        grad_down_kernel,
        "grad_down",
        4,
        [hidden_pair, whole(frames, width), whole(frames, width)],
        pl.BlockSpec((4 * LANES, width), lambda s, *_: (s, 0)),
        like((2 * width, width), low),
        flops=2 * 2 * frames * width * 2 * width,
    )(ids, act, cotangent_own, cotangent_came)
    back_own = after(back_own, down)
    down = lax.psum_scatter(down, "seq", scatter_dimension=0, tiled=True)
    grad_middle, grad_branch, spread, middle_sums = call(
        middle_kernel,
        "middle_back",
        2,
        [wide_slab] * 4 + [w_out_spec, whole(16, width)],
        [wide_slab, wide_slab, blocks, whole(8, width)],
        (
            like((frames, width), wide),
            like((frames, width), low),
            like((8, frames, LANES), low),
            like((8, width), wide),
        ),
        flops=2 * frames * width * width,
    )(ids, back_own, back_came, middle, cotangent_own, bundle, vectors)
    grad_mine = trade(spread, IN_SQUARE)
    grad_mine_came = hop_batch(grad_mine, 1)

    split = like((8, part, width // 2), low)
    split_spec = pl.BlockSpec((4,) + split.shape[1:], lambda s, *_: (s, 0, 0))
    column = pl.BlockSpec((frames, 4 * part), lambda s, *_: (0, s))
    out_kept, out_leaving = call(
        grad_out_kernel,
        "grad_out",
        2,
        [column, whole(frames, width)],
        [split_spec, split_spec],
        (split, split),
        flops=frames * width,
    )(ids, attended, grad_branch)
    out_came = hop_batch(out_leaving, 1)
    broad = like((8, part, width + width // 4), low)
    broad_spec = pl.BlockSpec((4,) + broad.shape[1:], lambda s, *_: (s, 0, 0))
    up_kept, up_leaving = call(
        grad_up_kernel,
        "grad_up",
        2,
        [column, column, whole(2, frames, 2 * width), split_spec, split_spec],
        [broad_spec, broad_spec],
        (broad, broad),
        flops=frames * width,
    )(ids, normed_two, normed_two_came, grad_up, out_kept, out_came)
    up_came = hop_batch(up_leaving, 2)

    result = (
        middle
        + result_own
        + hop_batch(result_leaving, 1).astype(wide)
        + vectors[5:6]
    ).astype(low)
    result_home = swap_halves(result[None])

    grad_mine = after(grad_mine, result, up_leaving)
    grad_qkv, grad_leaving = attend_back(
        ids,
        bounds,
        qkv_own,
        qkv_came,
        grad_mine,
        grad_mine_came,
        attended_heads,
        places,
        lse,
    )
    grad_leaving = after(grad_leaving, up_came, result_home)
    mixed = (up_kept.astype(wide) + after(up_came, grad_leaving).astype(wide)).astype(low)
    mixed = lax.psum_scatter(
        mixed.reshape(width, width + width // 4), "seq", scatter_dimension=0, tiled=True
    )
    grad_qkv_came = hop_batch(grad_leaving, 1)

    pair = (2, frames, width // 2)
    half_spec = pl.BlockSpec((fourth, width // 2), lambda i, *_: (i, 0))
    pair_spec = pl.BlockSpec((2, fourth, width // 2), lambda i, *_: (0, i, 0))
    first, y_out, z_out, keep_left, keep_right = call(
        back_project_kernel,
        "back_project",
        4,
        [heads_slab] * 2 + [whole(*w_heads.shape)] * 2,
        [slab, pair_spec, pair_spec, half_spec, half_spec],
        (
            like((frames, width), wide),
            like(pair, low),
            like(pair, low),
            like(pair[1:], wide),
            like(pair[1:], wide),
        ),
        scratch=[pltpu.VMEM((4, fourth, width), wide)],
        flops=2 * 4 * frames * width * 6 * LANES,
    )(
        ids,
        grad_qkv.reshape(heads_shape),
        grad_qkv_came.reshape(heads_shape),
        w_heads,
        w_other,
    )
    y_came, z_came = hop_seq(y_out, 1), hop_seq(z_out, 2)

    first_sums = call(
        first_sums_kernel,
        "first_sums",
        4,
        [slab, pair_spec, pair_spec, half_spec, half_spec, natural_slab, whole(16, width)],
        whole(8, width),
        like((8, width), wide),
    )(
        ids,
        first,
        y_out,
        z_out,
        keep_left,
        keep_right,
        natural.reshape(4, frames, width),
        vectors,
    )
    y_came = after(y_came, first_sums)
    ups = jnp.zeros((4, width), wide)
    ups = lax.dynamic_update_slice(ups, up_sums[:2], (2 * core, 0))
    sums = jnp.concatenate([first_sums[:2], middle_sums[:4], ups, jnp.zeros((6, width), wide)])
    sums = sums.reshape(16, 8, 1, part).transpose(1, 2, 0, 3)
    sums = jnp.broadcast_to(sums, (8, 4, 16, part)).reshape(32, 16, part)

    heads_out = like((width, 3 * LANES), low)
    grad_heads = call(
        grad_heads_kernel,
        "grad_heads",
        2,
        [
            pl.BlockSpec((4 * frames, 4 * part), lambda i, *_: (0, i)),
            whole(4 * frames, 3 * LANES),
        ],
        pl.BlockSpec((4 * part, 3 * LANES), lambda i, *_: (i, 0)),
        like((width, 3 * LANES), low),
        flops=2 * 4 * frames * width * 3 * LANES,
    )
    heads_leaving = grad_heads(ids, after(natural, z_out), grad_qkv_came)
    heads_kept = grad_heads(ids, after(natural, z_out), grad_qkv)
    heads_came = hop_batch(heads_leaving, 1)
    heads_sum = (heads_kept.astype(wide) + heads_came.astype(wide)).astype(low)
    heads_came = hop_batch(heads_sum, 2)
    down = after(down, z_out)
    down_x = hop_batch(down, 2)
    down = (down.astype(wide) + down_x.astype(wide)).astype(low)
    y_came = after(y_came, heads_sum, down)
    down_came = hop_batch(down, 1)

    z_second, y_second = call(
        second_kernel,
        "second",
        1,
        [whole(*pair[1:])] * 2 + [whole(*pair)] * 2,
        [whole(*pair[1:])] * 2,
        (like(pair[1:], low), like(pair[1:], low)),
    )(ids, keep_left, keep_right, y_came, z_came)
    z_last, y_last = hop_seq(z_second, 2), hop_seq(y_second, 1)
    sums = lax.all_to_all(after(sums, z_second), ("seq", "batch"), 0, 0, tiled=True)
    sums = jnp.sum(sums, axis=0)
    grad_inputs = call(
        last_kernel,
        "last",
        4,
        [slab, pair_spec, pair_spec, half_spec, half_spec, slab, slab, whole(16, width)],
        slab,
        like((frames, width), low),
    )(ids, after(first, mixed, sums), y_came, z_came, z_last, y_last, tokens_here, grad_middle, vectors)
    mixed_x = hop_batch(mixed, 2)
    grad_inputs = swap_halves(grad_inputs[None])

    heads_sum = (
        after(heads_sum, z_last, y_last).astype(wide) + heads_came.astype(wide)
    ).astype(low)
    heads_sum = lax.all_to_all(
        heads_sum.reshape(8, part, 3 * LANES), "seq", 0, 0, tiled=True
    ).astype(wide)
    heads_sum = (heads_sum[:4] + heads_sum[4:]).astype(low)
    heads_came = hop_batch(heads_sum, 1)
    mixed_core, mixed_both = hop_batch(mixed, 1), hop_batch(mixed_x, 1)
    grad_qkv_w, grad_out_w, grad_up_w, grad_down_w = call(
        spread_kernel,
        "spread",
        1,
        [whole(4, part, 3 * LANES)] * 2
        + [whole(2 * part, width)] * 2
        + [whole(part, width + width // 4)] * 4,
        [
            whole(part, 3 * width),
            whole(part, width),
            whole(part, 4 * width),
            whole(4 * part, width),
        ],
        (
            like((part, 3 * width), wide),
            like((part, width), wide),
            like((part, 4 * width), wide),
            like((4 * part, width), wide),
        ),
    )(ids, heads_sum, heads_came, down, down_came, mixed, mixed_x, mixed_core, mixed_both)

    grad_inputs = after(grad_inputs, grad_qkv_w)
    return (
        result_home,
        grad_inputs,
        grad_qkv_w,
        grad_out_w,
        grad_up_w,
        grad_down_w,
        sums[0],
        sums[1],
        sums[2],
        sums[3],
        sums[4],
        sums[6:10].reshape(4 * LANES),
        sums[5],
    )


def solution(mesh):
    square = mesh.shape["seq"] == 8 and mesh.shape["batch"] == 4
    return jax.shard_map(
        square_shards if square else shards,
        mesh=mesh,
        in_specs=(
            P("batch", "seq", None),
            P("batch", None),
            P("batch", None),
            P("batch", "seq", None),
            P("seq", None),
            P("seq", None),
            P("seq", None),
            P("seq", None),
            P("seq"),
            P("seq"),
            P("seq"),
            P("seq"),
            P("seq"),
            P("seq"),
            P("seq"),
        ),
        out_specs=(
            P("batch", "seq", None),
            P("batch", "seq", None),
            P("seq", None),
            P("seq", None),
            P("seq", None),
            P("seq", None),
            P("seq"),
            P("seq"),
            P("seq"),
            P("seq"),
            P("seq"),
            P("seq"),
            P("seq"),
        ),
        check_vma=False,
    )
```

```python
import jax
import jax.numpy as jnp
from jax import lax
from jax.experimental import pallas as pl
from jax.experimental.pallas import tpu as pltpu
from jax.sharding import PartitionSpec as P

HEAD_COUNT = 16
HEAD_DIM = 64
MAXCAP = 2048


NEGATIVE = -1e30
EPSILON = 1e-05


def shifted(block, axis, distance):
    devices = range(lax.axis_size(axis))
    route = [(i - distance, i) for i in devices if i - distance in devices]
    return lax.ppermute(block, axis, route)


def norm_rows(values, gain, shift):
    centre = jnp.mean(values, axis=-1, keepdims=True)
    centred = values - centre
    spread = jnp.mean(centred * centred, axis=-1, keepdims=True)
    return centred * lax.rsqrt(spread + EPSILON) * gain + shift


def gelu_exact(values):
    return jax.nn.gelu(values, approximate=False)


def segment_ids(lengths_row, total):
    ends = jnp.cumsum(lengths_row)
    places = jnp.arange(total, dtype=jnp.int32)
    return jnp.sum((places[:, None] >= ends[None, :]).astype(jnp.int32), axis=1)


def times_trans(left, right):
    return lax.dot_general(
        left, right, (((1,), (1,)), ((), ())), preferred_element_type=jnp.float32
    )


def trans_times(left, right):
    return lax.dot_general(
        left, right, (((0,), (0,)), ((), ())), preferred_element_type=jnp.float32
    )


def head_split(matrix):
    return matrix.reshape(matrix.shape[0], HEAD_COUNT, HEAD_DIM)


def keep_same(carry):
    return carry


def block_allowed(my_index, offset, frames, seg_all, key_on, query_seg, query_pos):
    source = my_index - offset
    start = jnp.maximum(source, 0) * frames
    key_pos = source * frames + jnp.arange(frames, dtype=jnp.int32)
    key_seg = lax.dynamic_slice_in_dim(seg_all, start, frames)
    key_live = lax.dynamic_slice_in_dim(key_on, start, frames)
    same = key_seg[None, :] == query_seg[:, None]
    causal = (key_pos[None, :] <= query_pos[:, None]) & (key_pos[None, :] >= 0)
    usable = (key_live[None, :] == 1) | (key_pos[None, :] == query_pos[:, None])
    return same & causal & usable


def block_scores(queries, keys, allowed, score_scale):
    scores = (
        jnp.einsum(
            "qhd,khd->hqk",
            head_split(queries),
            head_split(keys),
            preferred_element_type=jnp.float32,
        )
        * score_scale
    )
    return jnp.where(allowed[None], scores, NEGATIVE)


def block_probs(queries, block, allowed, row_max, row_sum, score_scale):
    scores = block_scores(queries, block[:, : queries.shape[1]], allowed, score_scale)
    return jnp.exp(scores - row_max[:, :, None]) / row_sum[:, :, None]


def forward_chain(kv_own, reach):
    blocks = [kv_own]
    moving = kv_own
    for offset in range(reach):
        moving = shifted(moving, "seq", 1)
        blocks.append(moving)
    return blocks


def again_chain(kv_own, reach):
    blocks = [kv_own]
    moving = kv_own
    for offset in range(reach):
        moving = shifted(moving, "seq", 1)
        blocks.append(moving)
    return blocks


def softmax_stats(queries, blocks, allowed_list, live_list, score_scale):
    frames, model_width = queries.shape
    row_max = jnp.full((HEAD_COUNT, frames), NEGATIVE, jnp.float32)
    row_sum = jnp.zeros((HEAD_COUNT, frames), jnp.float32)
    for offset in range(len(blocks)):

        def softmax_update(carry, block=blocks[offset], allowed=allowed_list[offset]):
            old_max, old_sum = carry
            scores = block_scores(queries, block[:, :model_width], allowed, score_scale)
            new_max = jnp.maximum(old_max, jnp.max(scores, axis=2))
            new_sum = old_sum * jnp.exp(old_max - new_max) + jnp.sum(
                jnp.exp(scores - new_max[:, :, None]), axis=2
            )
            return (new_max, new_sum)

        row_max, row_sum = lax.cond(
            live_list[offset], softmax_update, keep_same, (row_max, row_sum)
        )
    return (row_max, row_sum)


def attend_values(queries, blocks, allowed_list, live_list, row_max, row_sum, score_scale):
    frames, model_width = queries.shape
    total = jnp.zeros((frames, HEAD_COUNT, HEAD_DIM), jnp.float32)
    for offset in range(len(blocks)):

        def attend_update(carry, block=blocks[offset], allowed=allowed_list[offset]):
            probs = block_probs(queries, block, allowed, row_max, row_sum, score_scale).astype(
                jnp.bfloat16
            )
            return carry + jnp.einsum(
                "hqk,khd->qhd",
                probs,
                head_split(block[:, model_width:]),
                preferred_element_type=jnp.float32,
            )

        total = lax.cond(live_list[offset], attend_update, keep_same, total)
    return total.reshape(frames, model_width).astype(jnp.bfloat16)


def attention_grads(
    queries, grad_attended, blocks, allowed_list, live_list, row_max, row_sum, score_scale
):
    frames, model_width = queries.shape
    grad_heads = head_split(grad_attended)
    query_heads = head_split(queries)
    delta = jnp.zeros((HEAD_COUNT, frames), jnp.float32)
    for offset in range(len(blocks)):

        def attention_update(carry, block=blocks[offset], allowed=allowed_list[offset]):
            probs = block_probs(queries, block, allowed, row_max, row_sum, score_scale)
            dprobs = jnp.einsum(
                "qhd,khd->hqk",
                grad_heads,
                head_split(block[:, model_width:]),
                preferred_element_type=jnp.float32,
            )
            return carry + jnp.sum(probs * dprobs, axis=2)

        delta = lax.cond(live_list[offset], attention_update, keep_same, delta)
    grad_queries = jnp.zeros((frames, HEAD_COUNT, HEAD_DIM), jnp.float32)
    contributions = []
    for offset in range(len(blocks)):

        def block_grads(block=blocks[offset], allowed=allowed_list[offset]):
            probs = block_probs(queries, block, allowed, row_max, row_sum, score_scale)
            value_heads = head_split(block[:, model_width:])
            dprobs = jnp.einsum(
                "qhd,khd->hqk", grad_heads, value_heads, preferred_element_type=jnp.float32
            )
            dscores = (probs * (dprobs - delta[:, :, None]) * score_scale).astype(jnp.bfloat16)
            query_part = jnp.einsum(
                "hqk,khd->qhd",
                dscores,
                head_split(block[:, :model_width]),
                preferred_element_type=jnp.float32,
            )
            key_part = jnp.einsum(
                "hqk,qhd->khd", dscores, query_heads, preferred_element_type=jnp.float32
            )
            value_part = jnp.einsum(
                "hqk,qhd->khd",
                probs.astype(jnp.bfloat16),
                grad_heads,
                preferred_element_type=jnp.float32,
            )
            joined = jnp.concatenate(
                [key_part.reshape(frames, model_width), value_part.reshape(frames, model_width)],
                axis=1,
            )
            return (query_part, joined)

        def no_grads():
            return (
                jnp.zeros((frames, HEAD_COUNT, HEAD_DIM), jnp.float32),
                jnp.zeros((frames, 2 * model_width), jnp.float32),
            )

        query_part, joined = lax.cond(live_list[offset], block_grads, no_grads)
        grad_queries = grad_queries + query_part
        contributions.append(joined)
    return (grad_queries.reshape(frames, model_width), contributions)


def shards(
    tokens,
    lengths,
    key_mask,
    cotangent,
    w_qkv,
    w_out,
    w_up,
    w_down,
    ln1_gain,
    ln1_bias,
    ln2_gain,
    ln2_bias,
    out_bias,
    up_bias,
    down_bias,
):
    gathered = (
        lax.all_gather(w_qkv, "seq", axis=0, tiled=True),
        lax.all_gather(w_out, "seq", axis=0, tiled=True),
        lax.all_gather(w_up, "seq", axis=0, tiled=True),
        lax.all_gather(w_down, "seq", axis=0, tiled=True),
        lax.all_gather(ln1_gain, "seq", axis=0, tiled=True),
        lax.all_gather(ln1_bias, "seq", axis=0, tiled=True),
        lax.all_gather(ln2_gain, "seq", axis=0, tiled=True),
        lax.all_gather(ln2_bias, "seq", axis=0, tiled=True),
        lax.all_gather(out_bias, "seq", axis=0, tiled=True),
        lax.all_gather(up_bias, "seq", axis=0, tiled=True),
        lax.all_gather(down_bias, "seq", axis=0, tiled=True),
    )
    qkv_full, out_full, up_full, down_full = (gathered[0], gathered[1], gathered[2], gathered[3])
    gain_one, shift_one, gain_two, shift_two, out_shift, up_shift, down_shift = tuple(
        (member.astype(jnp.float32) for member in gathered[4:])
    )
    frames = tokens.shape[1]
    model_width = tokens.shape[2]
    cycle_size = lax.axis_size("seq")
    group_frames = frames * cycle_size
    longest = min(MAXCAP, group_frames // 2)
    reach = longest // frames
    my_index = lax.axis_index("seq")
    score_scale = HEAD_DIM ** (-0.5)
    seg_all = segment_ids(lengths[0], group_frames)
    key_on = key_mask[0]
    query_pos = my_index * frames + jnp.arange(frames, dtype=jnp.int32)
    query_seg = lax.dynamic_slice_in_dim(seg_all, my_index * frames, frames)
    allowed_list = [
        block_allowed(my_index, offset, frames, seg_all, key_on, query_seg, query_pos)
        for offset in range(reach + 1)
    ]
    live_list = [jnp.any(allowed) for allowed in allowed_list]
    inputs = tokens[0].astype(jnp.float32)
    normed_one = norm_rows(inputs, gain_one, shift_one).astype(jnp.bfloat16)
    qkv_low = jnp.dot(normed_one, qkv_full, preferred_element_type=jnp.float32).astype(jnp.bfloat16)
    queries = qkv_low[:, :model_width]
    kv_own = qkv_low[:, model_width:]
    blocks = forward_chain(kv_own, reach)
    row_max, row_sum = softmax_stats(queries, blocks, allowed_list, live_list, score_scale)
    attended = attend_values(
        queries, blocks, allowed_list, live_list, row_max, row_sum, score_scale
    )
    branch = jnp.dot(attended, out_full, preferred_element_type=jnp.float32) + out_shift
    middle = inputs + branch
    normed_two = norm_rows(middle, gain_two, shift_two).astype(jnp.bfloat16)
    up_value = jnp.dot(normed_two, up_full, preferred_element_type=jnp.float32) + up_shift
    activated = gelu_exact(up_value).astype(jnp.bfloat16)
    result = middle + jnp.dot(activated, down_full, preferred_element_type=jnp.float32) + down_shift
    grad_result = cotangent[0]
    grad_down_w = trans_times(activated, grad_result)
    grad_down_b = jnp.sum(grad_result.astype(jnp.float32), axis=0)
    grad_act = times_trans(grad_result, down_full)
    grad_up = jax.vjp(gelu_exact, up_value)[1](grad_act)[0].astype(jnp.bfloat16)
    grad_up_w = trans_times(normed_two, grad_up)
    grad_up_b = jnp.sum(grad_up.astype(jnp.float32), axis=0)
    grad_normed_two = times_trans(grad_up, up_full)
    pull_two = jax.vjp(norm_rows, middle, gain_two, shift_two)[1]
    grad_mid_norm, grad_gain_two, grad_shift_two = pull_two(grad_normed_two)
    grad_middle = grad_result.astype(jnp.float32) + grad_mid_norm
    grad_branch = grad_middle.astype(jnp.bfloat16)
    grad_out_w = trans_times(attended, grad_branch)
    grad_out_b = jnp.sum(grad_branch.astype(jnp.float32), axis=0)
    grad_attended = times_trans(grad_branch, out_full).astype(jnp.bfloat16)
    back_blocks = again_chain(kv_own, reach)
    grad_queries, contributions = attention_grads(
        queries, grad_attended, back_blocks, allowed_list, live_list, row_max, row_sum, score_scale
    )
    flowing = contributions[reach]
    for offset in range(reach - 1, -1, -1):
        flowing = (
            shifted(flowing.astype(jnp.bfloat16), "seq", -1).astype(flowing.dtype)
            + contributions[offset]
        )
    grad_qkv = jnp.concatenate([grad_queries, flowing], axis=1).astype(jnp.bfloat16)
    grad_qkv_w = trans_times(normed_one, grad_qkv)
    grad_normed_one = times_trans(grad_qkv, qkv_full)
    pull_one = jax.vjp(norm_rows, inputs, gain_one, shift_one)[1]
    grad_in_norm, grad_gain_one, grad_shift_one = pull_one(grad_normed_one)
    grad_inputs = (grad_middle + grad_in_norm).astype(jnp.bfloat16)
    shares = (
        lax.psum_scatter(
            grad_qkv_w.astype(jnp.bfloat16), "seq", scatter_dimension=0, tiled=True
        ).astype(jnp.float32),
        lax.psum_scatter(
            grad_out_w.astype(jnp.bfloat16), "seq", scatter_dimension=0, tiled=True
        ).astype(jnp.float32),
        lax.psum_scatter(
            grad_up_w.astype(jnp.bfloat16), "seq", scatter_dimension=0, tiled=True
        ).astype(jnp.float32),
        lax.psum_scatter(
            grad_down_w.astype(jnp.bfloat16), "seq", scatter_dimension=0, tiled=True
        ).astype(jnp.float32),
        lax.psum_scatter(
            grad_gain_one.astype(jnp.bfloat16), "seq", scatter_dimension=0, tiled=True
        ).astype(jnp.float32),
        lax.psum_scatter(
            grad_shift_one.astype(jnp.bfloat16), "seq", scatter_dimension=0, tiled=True
        ).astype(jnp.float32),
        lax.psum_scatter(
            grad_gain_two.astype(jnp.bfloat16), "seq", scatter_dimension=0, tiled=True
        ).astype(jnp.float32),
        lax.psum_scatter(
            grad_shift_two.astype(jnp.bfloat16), "seq", scatter_dimension=0, tiled=True
        ).astype(jnp.float32),
        lax.psum_scatter(
            grad_out_b.astype(jnp.bfloat16), "seq", scatter_dimension=0, tiled=True
        ).astype(jnp.float32),
        lax.psum_scatter(
            grad_up_b.astype(jnp.bfloat16), "seq", scatter_dimension=0, tiled=True
        ).astype(jnp.float32),
        lax.psum_scatter(
            grad_down_b.astype(jnp.bfloat16), "seq", scatter_dimension=0, tiled=True
        ).astype(jnp.float32),
    )
    reduced = (
        lax.psum(shares[0].astype(jnp.bfloat16), "batch").astype(jnp.float32),
        lax.psum(shares[1].astype(jnp.bfloat16), "batch").astype(jnp.float32),
        lax.psum(shares[2].astype(jnp.bfloat16), "batch").astype(jnp.float32),
        lax.psum(shares[3].astype(jnp.bfloat16), "batch").astype(jnp.float32),
        lax.psum(shares[4].astype(jnp.bfloat16), "batch").astype(jnp.float32),
        lax.psum(shares[5].astype(jnp.bfloat16), "batch").astype(jnp.float32),
        lax.psum(shares[6].astype(jnp.bfloat16), "batch").astype(jnp.float32),
        lax.psum(shares[7].astype(jnp.bfloat16), "batch").astype(jnp.float32),
        lax.psum(shares[8].astype(jnp.bfloat16), "batch").astype(jnp.float32),
        lax.psum(shares[9].astype(jnp.bfloat16), "batch").astype(jnp.float32),
        lax.psum(shares[10].astype(jnp.bfloat16), "batch").astype(jnp.float32),
    )
    return (
        result.astype(jnp.bfloat16)[None],
        grad_inputs[None],
        reduced[0],
        reduced[1],
        reduced[2],
        reduced[3],
        reduced[4],
        reduced[5],
        reduced[6],
        reduced[7],
        reduced[8],
        reduced[9],
        reduced[10],
    )


LANES = 128
TILE = 512
UTTERANCES = 4
SHRINK = 1
PARAMS = pltpu.CompilerParams(dimension_semantics=("arbitrary",), vmem_limit_bytes=56 << 20)


def dot_nt(left, right):
    return lax.dot_general(
        left, right, (((1,), (1,)), ((), ())), preferred_element_type=jnp.float32
    )


def dot_nn(left, right):
    return lax.dot_general(
        left, right, (((1,), (0,)), ((), ())), preferred_element_type=jnp.float32
    )


def dot_tn(left, right):
    return lax.dot_general(
        left, right, (((0,), (0,)), ((), ())), preferred_element_type=jnp.float32
    )


def norm_stats(values):
    centre = jnp.mean(values, axis=-1, keepdims=True)
    centred = values - centre
    spread = jnp.mean(centred * centred, axis=-1, keepdims=True)
    inverse = lax.rsqrt(spread + EPSILON)
    return centred * inverse, inverse


def norm_back(grad, normed, inverse, gain):
    g = grad * gain
    return inverse * (
        g
        - jnp.mean(g, axis=-1, keepdims=True)
        - normed * jnp.mean(g * normed, axis=-1, keepdims=True)
    )


def whole(*shape):
    return pl.BlockSpec(shape, lambda *_: (0,) * len(shape))


def like(shape, kind):
    return jax.ShapeDtypeStruct(shape, kind)


def call(kernel, name, grid, in_specs, out_specs, out_shape, scratch=(), flops=0):
    def run(ids, *args):
        bytes_accessed = sum(a.size * a.dtype.itemsize for a in args)
        return pl.pallas_call(
            kernel,
            out_shape=out_shape,
            grid_spec=pltpu.PrefetchScalarGridSpec(
                num_scalar_prefetch=1,
                grid=(grid,),
                in_specs=in_specs,
                out_specs=out_specs,
                scratch_shapes=list(scratch),
            ),
            compiler_params=PARAMS,
            cost_estimate=pl.CostEstimate(
                flops=flops // SHRINK,
                bytes_accessed=2 * bytes_accessed // SHRINK,
                transcendentals=0,
            ),
            name=name,
        )(ids, *args)

    return run


CORE, CHIP_X, SQUARE, Y_BIT = 0, 1, 2, 3


def norm_kernel(ids, tokens, vectors, out):
    normed, _ = norm_stats(tokens[...].astype(jnp.float32))
    out[...] = (normed * vectors[0:1, :] + vectors[1:2, :]).astype(jnp.bfloat16)


def project_kernel(ids, own, y_one, z_one, top, bottom, w_own, w_other, out, leaving, natural):
    square = ids[SQUARE]
    corner = jnp.where(pl.program_id(0) < 2, top[...], bottom[...])
    pieces = (own[...], y_one[...], z_one[...], corner)
    rows = jnp.concatenate(pieces, axis=0)
    size = corner.shape[0]
    mine = dot_nn(rows, w_own[...]).astype(jnp.bfloat16)
    other = dot_nn(rows, w_other[...]).astype(jnp.bfloat16)
    for j in range(4):
        at = pl.ds(square ^ j, 1)
        natural[at] = pieces[j][None]
        out[at] = mine[None, j * size : (j + 1) * size]
        leaving[at] = other[None, j * size : (j + 1) * size]


def head_lanes(block, head):
    lane = lax.broadcasted_iota(jnp.int32, block.shape, 1)
    keep = (lane < HEAD_DIM) if head == 0 else (lane >= HEAD_DIM)
    return jnp.where(keep, block, jnp.zeros_like(block))


def join_heads(ids, own, came, qkv):
    half = own.shape[0]
    for rows, side in ((own, ids[CORE]), (came, 1 - ids[CORE])):
        at = pl.ds(pl.multiple_of(side * half, half), half)
        qkv[at, 0:LANES] = rows[:, 0:LANES] * jnp.bfloat16(HEAD_DIM ** (-0.5))
        qkv[at, LANES : 3 * LANES] = rows[:, LANES : 3 * LANES]


def first_frames(bounds, positions):
    start = jnp.zeros_like(positions)
    for u in range(1, UTTERANCES):
        start = jnp.where(positions >= bounds[2, u], bounds[2, u], start)
    return start


def spread_places(places_row, column):
    for j in range(places_row.shape[1] // TILE):
        row = places_row[:, j * TILE : (j + 1) * TILE]
        column[j * TILE : (j + 1) * TILE, :] = jnp.transpose(
            jnp.broadcast_to(row, (LANES, TILE))
        )


def allowed_keys(column, at, start, diagonal):
    places = jnp.concatenate([column[pl.ds(at, TILE), :]] * (TILE // LANES), axis=1)
    allowed = places >= start
    if diagonal:
        key = lax.broadcasted_iota(jnp.int32, (TILE, TILE), 0)
        query = lax.broadcasted_iota(jnp.int32, (TILE, TILE), 1)
        allowed = (allowed & (key < query)) | (key == query)
    return allowed


def row_starts(bounds, base):
    return first_frames(bounds, base + lax.broadcasted_iota(jnp.int32, (1, TILE), 1)).astype(
        jnp.float32
    )


def attend_kernel(
    ids, bounds, own, came, places_row, out, lse, qkv, turned, column, scores, top, total, acc
):
    tile = pl.program_id(0)
    base = pl.multiple_of(tile * TILE, TILE)

    @pl.when(tile == 0)
    def _():
        join_heads(ids, own, came, qkv)
        spread_places(places_row, column)
        for j in range(qkv.shape[0] // TILE):
            rows = slice(j * TILE, (j + 1) * TILE)
            turned[:, rows] = jnp.transpose(qkv[rows, 2 * LANES : 3 * LANES])

    queries = [head_lanes(qkv[pl.ds(base, TILE), 0:LANES], head) for head in range(2)]
    top[...] = jnp.full_like(top, NEGATIVE)
    total[...] = jnp.zeros_like(total)
    acc[...] = jnp.zeros_like(acc)

    start = row_starts(bounds, base)

    def step(j, diagonal):
        at = pl.multiple_of(j * TILE, TILE)
        keys = qkv[pl.ds(at, TILE), LANES : 2 * LANES]
        allowed = allowed_keys(column, at, start, diagonal)
        for head in range(2):
            value = jnp.where(allowed, dot_nt(keys, queries[head]), NEGATIVE)
            scores[head, j] = value
            top[head : head + 1, :] = jnp.maximum(
                top[head : head + 1, :], jnp.max(value, axis=0, keepdims=True)
            )

    def first_pass(j, carry):
        step(j, False)
        return carry

    def second_pass(j, carry):
        at = pl.multiple_of(j * TILE, TILE)
        for head in range(2):
            probs = jnp.exp(scores[head, j] - top[head : head + 1, :])
            total[head : head + 1, :] += jnp.sum(probs, axis=0, keepdims=True)
            values = turned[head * HEAD_DIM : (head + 1) * HEAD_DIM, pl.ds(at, TILE)]
            acc[head] += dot_nn(values, probs.astype(jnp.bfloat16))
        return carry

    lax.fori_loop(bounds[0, tile], tile, first_pass, 0)
    step(tile, True)
    lax.fori_loop(bounds[0, tile], tile + 1, second_pass, 0)
    both = jnp.concatenate([acc[0] / total[0:1, :], acc[1] / total[1:2, :]], axis=0)
    out[0] = jnp.transpose(both).astype(jnp.bfloat16)
    lse[:, pl.ds(base, TILE)] = top[...] + jnp.log(total[...])


def block_order(i):
    return 2 * (i % 4) + i // 4


def attend(ids, bounds, own, came, places):
    rows = 2 * own.shape[0]
    return pl.pallas_call(
        attend_kernel,
        out_shape=(like((8, TILE, LANES), jnp.bfloat16), like((2, rows), jnp.float32)),
        grid_spec=pltpu.PrefetchScalarGridSpec(
            num_scalar_prefetch=2,
            grid=(rows // TILE,),
            in_specs=[
                whole(*own.shape),
                whole(*came.shape),
                whole(1, rows),
            ],
            out_specs=[
                pl.BlockSpec((1, TILE, LANES), lambda i, *_: (block_order(i), 0, 0)),
                whole(2, rows),
            ],
            scratch_shapes=[
                pltpu.VMEM((rows, 3 * LANES), jnp.bfloat16),
                pltpu.VMEM((LANES, rows), jnp.bfloat16),
                pltpu.VMEM((rows, LANES), jnp.float32),
                pltpu.VMEM((2, rows // TILE, TILE, TILE), jnp.float32),
                pltpu.VMEM((2, TILE), jnp.float32),
                pltpu.VMEM((2, TILE), jnp.float32),
                pltpu.VMEM((2, HEAD_DIM, TILE), jnp.float32),
            ],
        ),
        compiler_params=PARAMS,
        cost_estimate=pl.CostEstimate(
            flops=rows * rows * 256 // SHRINK, bytes_accessed=rows * 2400, transcendentals=rows * rows
        ),
        name="attend",
    )(ids, bounds, own, came, places)


def attend_back_kernel(
    ids,
    bounds,
    own,
    came,
    grad_own,
    grad_came,
    attended,
    places_row,
    lse,
    out,
    leaving,
    qkv,
    grad,
    delta,
    grad_queries,
    grad_kv,
    column,
):
    tile = pl.program_id(0)
    base = pl.multiple_of(tile * TILE, TILE)
    core = ids[CORE]

    @pl.when(tile == 0)
    def _():
        join_heads(ids, own, came, qkv)
        spread_places(places_row, column)
        grad_queries[...] = jnp.zeros_like(grad_queries)
        for j in range(4):
            for rows, side in ((grad_own, core), (grad_came, 1 - core)):
                at = pl.multiple_of((4 * side + j) * TILE, TILE)
                block = rows[pl.ds(2 * j + core, 1)].reshape(TILE, LANES)
                grad[pl.ds(at, TILE), :] = block
                product = block.astype(jnp.float32) * attended[
                    pl.ds(2 * j + side, 1)
                ].reshape(TILE, LANES).astype(jnp.float32)
                turned = jnp.transpose(product)
                delta[0:1, pl.ds(at, TILE)] = jnp.sum(turned[:HEAD_DIM], axis=0, keepdims=True)
                delta[1:2, pl.ds(at, TILE)] = jnp.sum(turned[HEAD_DIM:], axis=0, keepdims=True)

    keys = qkv[pl.ds(base, TILE), LANES : 2 * LANES]
    values = qkv[pl.ds(base, TILE), 2 * LANES : 3 * LANES]
    turned_keys = jnp.transpose(keys)
    grad_kv[...] = jnp.zeros_like(grad_kv)

    def step(i, diagonal):
        at = pl.multiple_of(i * TILE, TILE)
        scaled = qkv[pl.ds(at, TILE), 0:LANES]
        grads = grad[pl.ds(at, TILE), :]
        allowed = allowed_keys(column, base, row_starts(bounds, at), diagonal)
        key_part = grad_kv[0]
        value_part = grad_kv[1]
        for head in range(2):
            queries = head_lanes(scaled, head)
            head_grads = head_lanes(grads, head)
            scores = jnp.where(allowed, dot_nt(keys, queries), NEGATIVE)
            probs = jnp.exp(scores - lse[head : head + 1, pl.ds(at, TILE)])
            dprobs = dot_nt(values, head_grads)
            dscores = (probs * (dprobs - delta[head : head + 1, pl.ds(at, TILE)])).astype(
                jnp.bfloat16
            )
            value_part = value_part + dot_nn(probs.astype(jnp.bfloat16), head_grads)
            key_part = key_part + dot_nn(dscores, queries)
            lanes = slice(head * HEAD_DIM, (head + 1) * HEAD_DIM)
            grad_queries[lanes, pl.ds(at, TILE)] += dot_nn(turned_keys[lanes, :], dscores)
        grad_kv[0] = key_part
        grad_kv[1] = value_part

    def later_step(i, carry):
        step(i, False)
        return carry

    step(tile, True)
    lax.fori_loop(tile + 1, bounds[1, tile], later_step, 0)

    def store(target):
        at = pl.ds(pl.multiple_of((tile % 4) * TILE, TILE), TILE)
        target[at, 0:LANES] = (
            jnp.transpose(grad_queries[:, pl.ds(base, TILE)]) * HEAD_DIM ** (-0.5)
        ).astype(jnp.bfloat16)
        target[at, LANES : 2 * LANES] = grad_kv[0].astype(jnp.bfloat16)
        target[at, 2 * LANES : 3 * LANES] = grad_kv[1].astype(jnp.bfloat16)

    @pl.when(tile // 4 == core)
    def _():
        store(out)

    @pl.when(tile // 4 != core)
    def _():
        store(leaving)


def attend_back(ids, bounds, own, came, grad_own, grad_came, attended, places, lse):
    half = own.shape[0]
    rows = 2 * half
    return pl.pallas_call(
        attend_back_kernel,
        out_shape=(like(own.shape, jnp.bfloat16), like(own.shape, jnp.bfloat16)),
        grid_spec=pltpu.PrefetchScalarGridSpec(
            num_scalar_prefetch=2,
            grid=(rows // TILE,),
            in_specs=[
                whole(*own.shape),
                whole(*came.shape),
                whole(*grad_own.shape),
                whole(*grad_came.shape),
                whole(*attended.shape),
                whole(1, rows),
                whole(2, rows),
            ],
            out_specs=[whole(*own.shape), whole(*own.shape)],
            scratch_shapes=[
                pltpu.VMEM((rows, 3 * LANES), jnp.bfloat16),
                pltpu.VMEM((rows, LANES), jnp.bfloat16),
                pltpu.VMEM((2, rows), jnp.float32),
                pltpu.VMEM((LANES, rows), jnp.float32),
                pltpu.VMEM((2, TILE, LANES), jnp.float32),
                pltpu.VMEM((rows, LANES), jnp.float32),
            ],
        ),
        compiler_params=PARAMS,
        cost_estimate=pl.CostEstimate(
            flops=rows * rows * 640 // SHRINK, bytes_accessed=rows * 2400, transcendentals=rows * rows
        ),
        name="attend_back",
    )(ids, bounds, own, came, grad_own, grad_came, attended, places, lse)


def attend_bounds(start, starts, rows):
    tiles = rows // TILE
    first = start[:: TILE]
    key_last = jnp.arange(1, tiles + 1, dtype=jnp.int32) * TILE - 1
    far_end = jnp.sum((first[None, :] <= key_last[:, None]).astype(jnp.int32), axis=1)
    starts = jnp.pad(starts, (0, tiles - starts.shape[0]))
    return jnp.stack([first // TILE, far_end, starts]).astype(jnp.int32)


def out_kernel(ids, own, came, tokens, w_out, vectors, attended, middle, normed):
    core = ids[CORE]
    rows, width = tokens.shape
    mine, other = [], []
    for j in range(4):
        mine.append(own[pl.ds(2 * j + core, 1)].reshape(rows, LANES))
        other.append(came[pl.ds(2 * j + core, 1)].reshape(rows, LANES))
    mine, other = jnp.concatenate(mine, axis=1), jnp.concatenate(other, axis=1)
    first = jnp.where(core == 0, mine, other)
    second = jnp.where(core == 0, other, mine)
    joined = jnp.concatenate([first, second], axis=1)
    attended[...] = joined
    branch = dot_nn(joined, w_out[...].reshape(width, width)) + vectors[4:5, :]
    value = tokens[...].astype(jnp.float32) + branch
    middle[...] = value
    xhat, _ = norm_stats(value)
    normed[...] = (xhat * vectors[2:3, :] + vectors[3:4, :]).astype(jnp.bfloat16)


def forward_kernel(
    ids,
    normed_own,
    normed_came,
    grad_own,
    grad_came,
    up_a,
    up_b,
    down_a,
    down_b,
    vectors,
    act,
    grad_up,
    up_bias,
    result_own,
    result_came,
    back_own,
    back_came,
    result,
    back,
):
    step = pl.program_id(0)
    core = ids[CORE]
    frames, width = normed_own.shape

    @pl.when(step == 0)
    def _():
        result[...] = jnp.zeros_like(result)
        back[...] = jnp.zeros_like(back)

    def weave(first, second, axis):
        parts = []
        for k in range(2):
            for block in (first, second):
                at = [slice(None), slice(None)]
                at[axis] = slice(k * LANES, (k + 1) * LANES)
                parts.append(block[tuple(at)])
        return jnp.concatenate(parts, axis=axis)

    wide_step = 2 * LANES
    w_up = weave(up_a[...].reshape(width, wide_step), up_b[...].reshape(width, wide_step), 1)
    w_down = weave(down_a[...].reshape(wide_step, width), down_b[...].reshape(wide_step, width), 0)
    shift = jnp.where(
        core == 0,
        weave(vectors[6:7, :], vectors[7:8, :], 1),
        weave(vectors[8:9, :], vectors[9:10, :], 1),
    )
    sides = ((normed_own, grad_own), (normed_came, grad_came))
    values = [dot_nn(normed[...], w_up) + shift for normed, _ in sides]
    slopes = [dot_nt(grad[...], w_down) for _, grad in sides]
    bias = jnp.zeros((1, 4 * LANES), jnp.float32)
    for side, (value, slope) in enumerate(zip(values, slopes)):
        half = 0.5 + 0.5 * lax.erf(value * 0.7071067811865476)
        bell = jnp.exp(-0.5 * value * value) * 0.3989422804014327
        activated = (value * half).astype(jnp.bfloat16)
        change = (slope * (half + value * bell)).astype(jnp.bfloat16)
        act[side] = activated
        grad_up[side] = change
        bias = bias + jnp.sum(change.astype(jnp.float32), axis=0, keepdims=True)
        result[side] += dot_nn(activated, w_down)
        back[side] += dot_nt(change, w_up)
    for k in range(4):
        at = slice((k // 2) * LANES, (k // 2 + 1) * LANES)
        up_bias[k % 2 : k % 2 + 1, at] = bias[:, k * LANES : (k + 1) * LANES]

    @pl.when(step == 3)
    def _():
        result_own[...] = result[0]
        result_came[...] = result[1].astype(jnp.bfloat16)
        back_own[...] = back[0]
        back_came[...] = back[1].astype(jnp.bfloat16)


def middle_kernel(
    ids, back_own, back_came, middle, cotangent, w_out, vectors, grad_middle, grad_branch, out, sums
):
    step = pl.program_id(0)
    xhat, inverse = norm_stats(middle[...])
    grad = back_own[...] + back_came[...].astype(jnp.float32)
    value = cotangent[...].astype(jnp.float32) + norm_back(grad, xhat, inverse, vectors[2:3, :])
    grad_middle[...] = value
    low = value.astype(jnp.bfloat16)
    grad_branch[...] = low

    @pl.when(step == 0)
    def _():
        sums[...] = jnp.zeros_like(sums)

    sums[0:1, :] += jnp.sum(grad * xhat, axis=0, keepdims=True)
    sums[1:2, :] += jnp.sum(grad, axis=0, keepdims=True)
    sums[2:3, :] += jnp.sum(low.astype(jnp.float32), axis=0, keepdims=True)
    sums[3:4, :] += jnp.sum(cotangent[...].astype(jnp.float32), axis=0, keepdims=True)
    width = w_out.shape[-1]
    spread = dot_nt(low, w_out[...].reshape(width, width)).astype(jnp.bfloat16)
    for group in range(8):
        out[block_order(group)] = spread[:, group * LANES : (group + 1) * LANES]


def grad_out_kernel(ids, attended, grad_branch, kept, leaving):
    core = ids[CORE]
    grad = dot_tn(attended[...], grad_branch[...]).astype(jnp.bfloat16)
    half = grad.shape[1] // 2
    shape = kept.shape
    kept[...] = jnp.where(core == 0, grad[:, :half], grad[:, half:]).reshape(shape)
    leaving[...] = jnp.where(core == 0, grad[:, half:], grad[:, :half]).reshape(shape)


def grad_down_kernel(ids, act, grad_own, grad_came, out):
    grad = dot_tn(act[0], grad_own[...]) + dot_tn(act[1], grad_came[...])
    out[...] = grad.astype(jnp.bfloat16)


def grad_up_kernel(ids, normed_own, normed_came, grad_up, out_own, out_came, kept, leaving):
    chip_x = ids[CHIP_X]
    grad = (dot_tn(normed_own[...], grad_up[0]) + dot_tn(normed_came[...], grad_up[1])).astype(
        jnp.bfloat16
    )
    half = grad.shape[1] // 2
    shape = kept.shape[:2] + (half,)
    kept[:, :, :half] = jnp.where(chip_x == 0, grad[:, :half], grad[:, half:]).reshape(shape)
    leaving[:, :, :half] = jnp.where(chip_x == 0, grad[:, half:], grad[:, :half]).reshape(shape)
    more = (out_own[...].astype(jnp.float32) + out_came[...].astype(jnp.float32)).astype(
        jnp.bfloat16
    )
    cut = more.shape[2] // 2
    kept[:, :, half:] = jnp.where(chip_x == 0, more[:, :, :cut], more[:, :, cut:])
    leaving[:, :, half:] = jnp.where(chip_x == 0, more[:, :, cut:], more[:, :, :cut])


def back_project_kernel(
    ids,
    own,
    came,
    w_own,
    w_other,
    first,
    y_out,
    z_out,
    keep_left,
    keep_right,
    grads,
):
    square = ids[SQUARE]
    size, width = first.shape
    half = width // 2
    rows = 4 * size
    value = dot_nt(own[...].reshape(rows, 3 * LANES), w_own[...])
    value = value + dot_nt(came[...].reshape(rows, 3 * LANES), w_other[...])
    grads[...] = value.reshape(4, size, width)
    first[...] = grads[square]
    y_out[0] = grads[square ^ 1, :, :half].astype(jnp.bfloat16)
    keep_right[...] = grads[square ^ 1, :, half:]
    z_out[0] = grads[square ^ 2, :, half:].astype(jnp.bfloat16)
    keep_left[...] = grads[square ^ 2, :, :half]
    y_out[1] = grads[square ^ 3, :, :half].astype(jnp.bfloat16)
    z_out[1] = grads[square ^ 3, :, half:].astype(jnp.bfloat16)


def first_sums_kernel(
    ids, first, y_out, z_out, keep_left, keep_right, natural, vectors, sums
):
    square = ids[SQUARE]
    half = first.shape[1] // 2
    wide = jnp.float32
    parts = (
        (first[:, :half], first[:, half:]),
        (y_out[0].astype(wide), keep_right[...]),
        (keep_left[...], z_out[0].astype(wide)),
        (y_out[1].astype(wide), z_out[1].astype(wide)),
    )

    @pl.when(pl.program_id(0) == 0)
    def _():
        sums[...] = jnp.zeros_like(sums)

    for j in range(4):
        for side in range(2):
            lanes = slice(side * half, (side + 1) * half)
            value = parts[j][side]
            rows = natural[square ^ j, :, lanes].astype(wide)
            normed = (rows - vectors[1:2, lanes]) / vectors[0:1, lanes]
            sums[0:1, lanes] += jnp.sum(value * normed, axis=0, keepdims=True)
            sums[1:2, lanes] += jnp.sum(value, axis=0, keepdims=True)


def second_kernel(ids, keep_left, keep_right, y_came, z_came, z_out, y_out):
    z_out[...] = (keep_left[...] + y_came[1].astype(jnp.float32)).astype(jnp.bfloat16)
    y_out[...] = (keep_right[...] + z_came[1].astype(jnp.float32)).astype(jnp.bfloat16)


def last_kernel(ids, first, y_came, z_came, z_second, y_second, tokens, grad_middle, vectors, out):
    wide = jnp.float32
    left = y_came[0].astype(wide) + z_second[...].astype(wide)
    right = z_came[0].astype(wide) + y_second[...].astype(wide)
    grad = first[...] + jnp.concatenate([left, right], axis=1)
    xhat, inverse = norm_stats(tokens[...].astype(wide))
    out[...] = (grad_middle[...] + norm_back(grad, xhat, inverse, vectors[0:1, :])).astype(
        jnp.bfloat16
    )


def grad_heads_kernel(ids, normed, grads, out):
    out[...] = dot_tn(normed[...], grads[...]).astype(jnp.bfloat16)


def spread_kernel(
    ids,
    heads,
    heads_came,
    down,
    down_came,
    mixed,
    mixed_x,
    mixed_core,
    mixed_both,
    qkv_out,
    out_out,
    up_out,
    down_out,
):
    wide = jnp.float32
    core, chip_x = ids[CORE], ids[CHIP_X]

    def ordered(side, own, other):
        return jnp.where(side == 0, own, other), jnp.where(side == 0, other, own)

    for side, blocks in enumerate(ordered(core, heads[...], heads_came[...])):
        for j in range(4):
            for k in range(3):
                at = k * 8 * LANES + (4 * side + j) * LANES
                qkv_out[:, at : at + LANES] = blocks[j, :, k * LANES : (k + 1) * LANES].astype(wide)
    rows = down.shape[0]
    for side, block in enumerate(ordered(core, down[...], down_came[...])):
        down_out[side * rows : (side + 1) * rows, :] = block.astype(wide)
    own = ordered(chip_x, mixed[...], mixed_x[...])
    came = ordered(chip_x, mixed_core[...], mixed_both[...])
    width = out_out.shape[1]
    step = 2 * LANES
    for x in range(2):
        for side, block in enumerate(ordered(core, own[x], came[x])):
            for j in range(4):
                at = (4 * x + j) * 2 * step + side * step
                up_out[:, at : at + step] = block[:, j * step : (j + 1) * step].astype(wide)
            at = side * 2 * step + x * step
            out_out[:, at : at + step] = block[:, width:].astype(wide)


def hop_batch(block, bit):
    size = lax.axis_size("batch")
    return lax.ppermute(block, "batch", [(i, i ^ bit) for i in range(size)])


def hop_seq(block, bits):
    size = lax.axis_size("seq")
    return lax.ppermute(block, "seq", [(i, i ^ bits) for i in range(size)])


def swap_halves(block):
    batches, seqs = lax.axis_size("batch"), lax.axis_size("seq")
    route = []
    for b in range(batches):
        for s in range(seqs):
            target = ((b & ~1) | (s >> 2)) * seqs + ((s & 3) | ((b & 1) << 2))
            route.append((b * seqs + s, target))
    return lax.ppermute(block, ("batch", "seq"), route)


def after(value, *anchors):
    return lax.optimization_barrier((value,) + anchors)[0]


def trade(block, groups):
    return lax.all_to_all(block, "seq", 0, 0, tiled=True, axis_index_groups=groups)


IN_SQUARE = [[0, 1, 2, 3], [4, 5, 6, 7]]
ALONG_Z = [[0, 2, 4, 6], [1, 3, 5, 7]]


def square_shards(
    tokens,
    lengths,
    key_mask,
    cotangent,
    w_qkv,
    w_out,
    w_up,
    w_down,
    ln1_gain,
    ln1_bias,
    ln2_gain,
    ln2_bias,
    out_bias,
    up_bias,
    down_bias,
):
    low, wide = jnp.bfloat16, jnp.float32
    batch_index = lax.axis_index("batch")
    seq_index = lax.axis_index("seq")
    core = batch_index & 1
    chip_x = batch_index >> 1
    square = seq_index & 3
    y_bit = seq_index & 1
    ids = jnp.stack([core, chip_x, square, y_bit]).astype(jnp.int32)
    frames, width = tokens.shape[1], tokens.shape[2]
    rows = 8 * frames
    part = width // 8
    quarter = 2 * core + chip_x

    up_piece = lax.dynamic_index_in_dim(w_up.reshape(part, 8, 4, LANES), quarter, 2, False)
    down_piece = lax.dynamic_slice_in_dim(w_down, quarter * part, part, 0)
    out_piece = lax.dynamic_slice_in_dim(w_out, batch_index * (part // 4), part // 4, 0)
    bundle = jnp.concatenate([down_piece, up_piece.reshape(part, width), out_piece], axis=0)
    deep = bundle.shape[0]

    tokens_here = swap_halves(tokens[0])
    heads = lax.dynamic_slice_in_dim(w_qkv.reshape(part, 3, 8, LANES), 4 * core, 4, 2)
    heads = heads.transpose(2, 0, 1, 3).reshape(4, part, 3 * LANES)
    small = jnp.concatenate(
        [
            jnp.stack([ln1_gain, ln1_bias, ln2_gain, ln2_bias, out_bias, down_bias]),
            up_bias.reshape(4, part),
            jnp.zeros((6, part), low),
        ],
        axis=0,
    )
    small = jnp.broadcast_to(jnp.pad(small, ((0, 0), (0, 2 * part)))[None], (4, 16, 3 * part))
    heads = jnp.concatenate([heads, small], axis=1)
    came = lax.all_to_all(jnp.concatenate([heads, heads], axis=0), "seq", 0, 0, tiled=True)
    vectors = came[:, part:, :part].astype(wide).transpose(1, 0, 2).reshape(16, width)
    w_heads = came[:, :part].reshape(width, 3 * LANES)
    w_other = hop_batch(w_heads, 1)

    meta = jnp.concatenate([key_mask[0], jnp.pad(lengths[0], (0, LANES - lengths.shape[1]))])
    meta = meta.reshape(-1, LANES)
    meta = jnp.where(core == (seq_index >> 2), meta, hop_batch(meta, 1)).reshape(-1)
    ends = jnp.cumsum(meta[rows : rows + lengths.shape[1]])
    starts = ends - meta[rows : rows + lengths.shape[1]]
    positions = jnp.arange(rows, dtype=jnp.int32)
    start = jnp.max(
        jnp.where(starts[None, :] <= positions[:, None], starts[None, :], 0), axis=1
    ).astype(jnp.int32)
    bounds = attend_bounds(start, starts, rows)
    places = jnp.where(meta[:rows] == 1, positions, -1).astype(wide)[None, :]

    fourth = frames // 4
    slab = pl.BlockSpec((fourth, width), lambda i, *_: (i, 0))
    normed_one = call(
        norm_kernel, "norm", 4, [slab, whole(16, width)], slab, like((frames, width), low)
    )(ids, tokens_here, vectors)
    y_one = hop_seq(normed_one, 1)
    z_one = hop_seq(normed_one, 2)
    bundle = lax.all_gather(after(bundle, tokens_here, came), ("seq", "batch"), axis=0, tiled=True)
    bundle = bundle.reshape(8, 4, deep, width)
    half = frames // 2
    top, bottom = hop_seq(y_one[:half], 2), hop_seq(z_one[half:], 1)
    heads_shape = (4, frames, 3 * LANES)
    top_slab = pl.BlockSpec((fourth, width), lambda i, *_: (jnp.minimum(i, 1), 0))
    bottom_slab = pl.BlockSpec((fourth, width), lambda i, *_: (jnp.maximum(i, 2) - 2, 0))
    heads_slab = pl.BlockSpec((4, fourth, 3 * LANES), lambda i, *_: (0, i, 0))
    natural_slab = pl.BlockSpec((4, fourth, width), lambda i, *_: (0, i, 0))
    heads_like = like(heads_shape, low)
    qkv_own, leaving, natural = call(
        project_kernel,
        "project",
        4,
        [slab] * 3 + [top_slab, bottom_slab] + [whole(*w_heads.shape)] * 2,
        [heads_slab, heads_slab, natural_slab],
        (heads_like, heads_like, like((4, frames, width), low)),
        flops=2 * 4 * frames * width * 6 * LANES,
    )(ids, normed_one, y_one, z_one, top, bottom, w_heads, w_other)
    qkv_came = hop_batch(leaving, 1).reshape(4 * frames, 3 * LANES)
    qkv_own = qkv_own.reshape(4 * frames, 3 * LANES)
    natural = natural.reshape(4 * frames, width)
    cotangent_own = swap_halves(after(cotangent[0], leaving))

    attended_heads, lse = attend(ids, bounds, qkv_own, qkv_came, places)
    cotangent_came = hop_batch(cotangent_own, 1)

    mine = trade(attended_heads, IN_SQUARE)
    mine_came = hop_batch(mine, 1)
    blocks = pl.BlockSpec((8, half, LANES), lambda i, *_: (0, i, 0))
    wide_slab = pl.BlockSpec((half, width), lambda i, *_: (i, 0))
    w_out_spec = pl.BlockSpec(
        (8, 4, part // 4, width), lambda *_: (0, 0, (deep * 4) // part - 1, 0)
    )
    attended, middle, normed_two = call(
        out_kernel,
        "out_project",
        2,
        [blocks, blocks, wide_slab, w_out_spec, whole(16, width)],
        [wide_slab] * 3,
        (like((frames, width), low), like((frames, width), wide), like((frames, width), low)),
        flops=2 * frames * width * width,
    )(ids, mine, mine_came, tokens_here, bundle, vectors)
    normed_two_came = hop_batch(normed_two, 1)

    up_specs = [
        pl.BlockSpec((8, 1, part, 2 * LANES), lambda s, ids, k=k: (0, 2 * k + ids[CORE], 1, s))
        for k in range(2)
    ]
    down_specs = [
        pl.BlockSpec((2, 1, part, width), lambda s, ids, k=k: (s, 2 * k + ids[CORE], 0, 0))
        for k in range(2)
    ]
    hidden = pl.BlockSpec((2, frames, 4 * LANES), lambda s, *_: (0, 0, s))
    act, grad_up, up_sums, result_own, result_leaving, back_own, back_leaving = call(
        forward_kernel,
        "feed_forward",
        4,
        [whole(frames, width)] * 4
        + up_specs
        + down_specs
        + [pl.BlockSpec((16, 2 * LANES), lambda s, *_: (0, s))],
        [hidden, hidden, pl.BlockSpec((8, 2 * LANES), lambda s, *_: (0, s))]
        + [whole(frames, width)] * 4,
        (
            like((2, frames, 2 * width), low),
            like((2, frames, 2 * width), low),
            like((8, width), wide),
            like((frames, width), wide),
            like((frames, width), low),
            like((frames, width), wide),
            like((frames, width), low),
        ),
        scratch=[pltpu.VMEM((2, frames, width), wide)] * 2,
        flops=2 * 4 * 2 * frames * width * 2 * width,
    )(
        ids,
        normed_two,
        normed_two_came,
        cotangent_own,
        cotangent_came,
        bundle,
        bundle,
        bundle,
        bundle,
        vectors,
    )
    back_came = hop_batch(back_leaving, 1)

    hidden_pair = pl.BlockSpec((2, frames, 4 * LANES), lambda s, *_: (0, 0, s))
    down = call(
        grad_down_kernel,
        "grad_down",
        4,
        [hidden_pair, whole(frames, width), whole(frames, width)],
        pl.BlockSpec((4 * LANES, width), lambda s, *_: (s, 0)),
        like((2 * width, width), low),
        flops=2 * 2 * frames * width * 2 * width,
    )(ids, act, cotangent_own, cotangent_came)
    back_own = after(back_own, down)
    down = lax.psum_scatter(down, "seq", scatter_dimension=0, tiled=True)
    grad_middle, grad_branch, spread, middle_sums = call(
        middle_kernel,
        "middle_back",
        2,
        [wide_slab] * 4 + [w_out_spec, whole(16, width)],
        [wide_slab, wide_slab, blocks, whole(8, width)],
        (
            like((frames, width), wide),
            like((frames, width), low),
            like((8, frames, LANES), low),
            like((8, width), wide),
        ),
        flops=2 * frames * width * width,
    )(ids, back_own, back_came, middle, cotangent_own, bundle, vectors)
    grad_mine = trade(spread, IN_SQUARE)
    grad_mine_came = hop_batch(grad_mine, 1)

    split = like((8, part, width // 2), low)
    split_spec = pl.BlockSpec((4,) + split.shape[1:], lambda s, *_: (s, 0, 0))
    column = pl.BlockSpec((frames, 4 * part), lambda s, *_: (0, s))
    out_kept, out_leaving = call(
        grad_out_kernel,
        "grad_out",
        2,
        [column, whole(frames, width)],
        [split_spec, split_spec],
        (split, split),
        flops=frames * width,
    )(ids, attended, grad_branch)
    out_came = hop_batch(out_leaving, 1)
    broad = like((8, part, width + width // 4), low)
    broad_spec = pl.BlockSpec((4,) + broad.shape[1:], lambda s, *_: (s, 0, 0))
    up_kept, up_leaving = call(
        grad_up_kernel,
        "grad_up",
        2,
        [column, column, whole(2, frames, 2 * width), split_spec, split_spec],
        [broad_spec, broad_spec],
        (broad, broad),
        flops=frames * width,
    )(ids, normed_two, normed_two_came, grad_up, out_kept, out_came)
    up_came = hop_batch(up_leaving, 2)

    result = (
        middle
        + result_own
        + hop_batch(result_leaving, 1).astype(wide)
        + vectors[5:6]
    ).astype(low)
    result_home = swap_halves(result[None])

    grad_mine = after(grad_mine, result, up_leaving)
    grad_qkv, grad_leaving = attend_back(
        ids,
        bounds,
        qkv_own,
        qkv_came,
        grad_mine,
        grad_mine_came,
        attended_heads,
        places,
        lse,
    )
    grad_leaving = after(grad_leaving, up_came, result_home)
    mixed = (up_kept.astype(wide) + after(up_came, grad_leaving).astype(wide)).astype(low)
    mixed = lax.psum_scatter(
        mixed.reshape(width, width + width // 4), "seq", scatter_dimension=0, tiled=True
    )
    grad_qkv_came = hop_batch(grad_leaving, 1)

    pair = (2, frames, width // 2)
    half_spec = pl.BlockSpec((fourth, width // 2), lambda i, *_: (i, 0))
    pair_spec = pl.BlockSpec((2, fourth, width // 2), lambda i, *_: (0, i, 0))
    first, y_out, z_out, keep_left, keep_right = call(
        back_project_kernel,
        "back_project",
        4,
        [heads_slab] * 2 + [whole(*w_heads.shape)] * 2,
        [slab, pair_spec, pair_spec, half_spec, half_spec],
        (
            like((frames, width), wide),
            like(pair, low),
            like(pair, low),
            like(pair[1:], wide),
            like(pair[1:], wide),
        ),
        scratch=[pltpu.VMEM((4, fourth, width), wide)],
        flops=2 * 4 * frames * width * 6 * LANES,
    )(
        ids,
        grad_qkv.reshape(heads_shape),
        grad_qkv_came.reshape(heads_shape),
        w_heads,
        w_other,
    )
    y_came, z_came = hop_seq(y_out, 1), hop_seq(z_out, 2)

    first_sums = call(
        first_sums_kernel,
        "first_sums",
        4,
        [slab, pair_spec, pair_spec, half_spec, half_spec, natural_slab, whole(16, width)],
        whole(8, width),
        like((8, width), wide),
    )(
        ids,
        first,
        y_out,
        z_out,
        keep_left,
        keep_right,
        natural.reshape(4, frames, width),
        vectors,
    )
    y_came = after(y_came, first_sums)
    ups = jnp.zeros((4, width), wide)
    ups = lax.dynamic_update_slice(ups, up_sums[:2], (2 * core, 0))
    sums = jnp.concatenate([first_sums[:2], middle_sums[:4], ups, jnp.zeros((6, width), wide)])
    sums = sums.reshape(16, 8, 1, part).transpose(1, 2, 0, 3)
    sums = jnp.broadcast_to(sums, (8, 4, 16, part)).reshape(32, 16, part)

    heads_out = like((width, 3 * LANES), low)
    grad_heads = call(
        grad_heads_kernel,
        "grad_heads",
        2,
        [
            pl.BlockSpec((4 * frames, 4 * part), lambda i, *_: (0, i)),
            whole(4 * frames, 3 * LANES),
        ],
        pl.BlockSpec((4 * part, 3 * LANES), lambda i, *_: (i, 0)),
        like((width, 3 * LANES), low),
        flops=2 * 4 * frames * width * 3 * LANES,
    )
    heads_leaving = grad_heads(ids, after(natural, z_out), grad_qkv_came)
    heads_kept = grad_heads(ids, after(natural, z_out), grad_qkv)
    heads_came = hop_batch(heads_leaving, 1)
    heads_sum = (heads_kept.astype(wide) + heads_came.astype(wide)).astype(low)
    heads_came = hop_batch(heads_sum, 2)
    down = after(down, z_out)
    down_x = hop_batch(down, 2)
    down = (down.astype(wide) + down_x.astype(wide)).astype(low)
    y_came = after(y_came, heads_sum, down)
    down_came = hop_batch(down, 1)

    z_second, y_second = call(
        second_kernel,
        "second",
        1,
        [whole(*pair[1:])] * 2 + [whole(*pair)] * 2,
        [whole(*pair[1:])] * 2,
        (like(pair[1:], low), like(pair[1:], low)),
    )(ids, keep_left, keep_right, y_came, z_came)
    z_last, y_last = hop_seq(z_second, 2), hop_seq(y_second, 1)
    grad_inputs = call(
        last_kernel,
        "last",
        4,
        [slab, pair_spec, pair_spec, half_spec, half_spec, slab, slab, whole(16, width)],
        slab,
        like((frames, width), low),
    )(ids, after(first, mixed), y_came, z_came, z_last, y_last, tokens_here, grad_middle, vectors)
    mixed_x = hop_batch(mixed, 2)
    grad_inputs = swap_halves(grad_inputs[None])

    heads_sum = (
        after(heads_sum, z_last, y_last).astype(wide) + heads_came.astype(wide)
    ).astype(low)
    heads_sum = lax.all_to_all(
        heads_sum.reshape(8, part, 3 * LANES), "seq", 0, 0, tiled=True
    ).astype(wide)
    heads_sum = (heads_sum[:4] + heads_sum[4:]).astype(low)
    sums = lax.all_to_all(after(sums, heads_sum), ("seq", "batch"), 0, 0, tiled=True)
    sums = jnp.sum(sums, axis=0)
    heads_came = hop_batch(heads_sum, 1)
    mixed_core, mixed_both = hop_batch(mixed, 1), hop_batch(mixed_x, 1)
    grad_qkv_w, grad_out_w, grad_up_w, grad_down_w = call(
        spread_kernel,
        "spread",
        1,
        [whole(4, part, 3 * LANES)] * 2
        + [whole(2 * part, width)] * 2
        + [whole(part, width + width // 4)] * 4,
        [
            whole(part, 3 * width),
            whole(part, width),
            whole(part, 4 * width),
            whole(4 * part, width),
        ],
        (
            like((part, 3 * width), wide),
            like((part, width), wide),
            like((part, 4 * width), wide),
            like((4 * part, width), wide),
        ),
    )(ids, heads_sum, heads_came, down, down_came, mixed, mixed_x, mixed_core, mixed_both)

    grad_inputs = after(grad_inputs, grad_qkv_w)
    return (
        result_home,
        grad_inputs,
        grad_qkv_w,
        grad_out_w,
        grad_up_w,
        grad_down_w,
        sums[0],
        sums[1],
        sums[2],
        sums[3],
        sums[4],
        sums[6:10].reshape(4 * LANES),
        sums[5],
    )


def solution(mesh):
    square = mesh.shape["seq"] == 8 and mesh.shape["batch"] == 4
    return jax.shard_map(
        square_shards if square else shards,
        mesh=mesh,
        in_specs=(
            P("batch", "seq", None),
            P("batch", None),
            P("batch", None),
            P("batch", "seq", None),
            P("seq", None),
            P("seq", None),
            P("seq", None),
            P("seq", None),
            P("seq"),
            P("seq"),
            P("seq"),
            P("seq"),
            P("seq"),
            P("seq"),
            P("seq"),
        ),
        out_specs=(
            P("batch", "seq", None),
            P("batch", "seq", None),
            P("seq", None),
            P("seq", None),
            P("seq", None),
            P("seq", None),
            P("seq"),
            P("seq"),
            P("seq"),
            P("seq"),
            P("seq"),
            P("seq"),
            P("seq"),
        ),
        check_vma=False,
    )
```

```python
import jax
import jax.numpy as jnp
from jax import lax
from jax.experimental import pallas as pl
from jax.experimental.pallas import tpu as pltpu
from jax.sharding import PartitionSpec as P

HEAD_COUNT = 16
HEAD_DIM = 64
MAXCAP = 2048


NEGATIVE = -1e30
EPSILON = 1e-05


def shifted(block, axis, distance):
    devices = range(lax.axis_size(axis))
    route = [(i - distance, i) for i in devices if i - distance in devices]
    return lax.ppermute(block, axis, route)


def norm_rows(values, gain, shift):
    centre = jnp.mean(values, axis=-1, keepdims=True)
    centred = values - centre
    spread = jnp.mean(centred * centred, axis=-1, keepdims=True)
    return centred * lax.rsqrt(spread + EPSILON) * gain + shift


def gelu_exact(values):
    return jax.nn.gelu(values, approximate=False)


def segment_ids(lengths_row, total):
    ends = jnp.cumsum(lengths_row)
    places = jnp.arange(total, dtype=jnp.int32)
    return jnp.sum((places[:, None] >= ends[None, :]).astype(jnp.int32), axis=1)


def times_trans(left, right):
    return lax.dot_general(
        left, right, (((1,), (1,)), ((), ())), preferred_element_type=jnp.float32
    )


def trans_times(left, right):
    return lax.dot_general(
        left, right, (((0,), (0,)), ((), ())), preferred_element_type=jnp.float32
    )


def head_split(matrix):
    return matrix.reshape(matrix.shape[0], HEAD_COUNT, HEAD_DIM)


def keep_same(carry):
    return carry


def block_allowed(my_index, offset, frames, seg_all, key_on, query_seg, query_pos):
    source = my_index - offset
    start = jnp.maximum(source, 0) * frames
    key_pos = source * frames + jnp.arange(frames, dtype=jnp.int32)
    key_seg = lax.dynamic_slice_in_dim(seg_all, start, frames)
    key_live = lax.dynamic_slice_in_dim(key_on, start, frames)
    same = key_seg[None, :] == query_seg[:, None]
    causal = (key_pos[None, :] <= query_pos[:, None]) & (key_pos[None, :] >= 0)
    usable = (key_live[None, :] == 1) | (key_pos[None, :] == query_pos[:, None])
    return same & causal & usable


def block_scores(queries, keys, allowed, score_scale):
    scores = (
        jnp.einsum(
            "qhd,khd->hqk",
            head_split(queries),
            head_split(keys),
            preferred_element_type=jnp.float32,
        )
        * score_scale
    )
    return jnp.where(allowed[None], scores, NEGATIVE)


def block_probs(queries, block, allowed, row_max, row_sum, score_scale):
    scores = block_scores(queries, block[:, : queries.shape[1]], allowed, score_scale)
    return jnp.exp(scores - row_max[:, :, None]) / row_sum[:, :, None]


def forward_chain(kv_own, reach):
    blocks = [kv_own]
    moving = kv_own
    for offset in range(reach):
        moving = shifted(moving, "seq", 1)
        blocks.append(moving)
    return blocks


def again_chain(kv_own, reach):
    blocks = [kv_own]
    moving = kv_own
    for offset in range(reach):
        moving = shifted(moving, "seq", 1)
        blocks.append(moving)
    return blocks


def softmax_stats(queries, blocks, allowed_list, live_list, score_scale):
    frames, model_width = queries.shape
    row_max = jnp.full((HEAD_COUNT, frames), NEGATIVE, jnp.float32)
    row_sum = jnp.zeros((HEAD_COUNT, frames), jnp.float32)
    for offset in range(len(blocks)):

        def softmax_update(carry, block=blocks[offset], allowed=allowed_list[offset]):
            old_max, old_sum = carry
            scores = block_scores(queries, block[:, :model_width], allowed, score_scale)
            new_max = jnp.maximum(old_max, jnp.max(scores, axis=2))
            new_sum = old_sum * jnp.exp(old_max - new_max) + jnp.sum(
                jnp.exp(scores - new_max[:, :, None]), axis=2
            )
            return (new_max, new_sum)

        row_max, row_sum = lax.cond(
            live_list[offset], softmax_update, keep_same, (row_max, row_sum)
        )
    return (row_max, row_sum)


def attend_values(queries, blocks, allowed_list, live_list, row_max, row_sum, score_scale):
    frames, model_width = queries.shape
    total = jnp.zeros((frames, HEAD_COUNT, HEAD_DIM), jnp.float32)
    for offset in range(len(blocks)):

        def attend_update(carry, block=blocks[offset], allowed=allowed_list[offset]):
            probs = block_probs(queries, block, allowed, row_max, row_sum, score_scale).astype(
                jnp.bfloat16
            )
            return carry + jnp.einsum(
                "hqk,khd->qhd",
                probs,
                head_split(block[:, model_width:]),
                preferred_element_type=jnp.float32,
            )

        total = lax.cond(live_list[offset], attend_update, keep_same, total)
    return total.reshape(frames, model_width).astype(jnp.bfloat16)


def attention_grads(
    queries, grad_attended, blocks, allowed_list, live_list, row_max, row_sum, score_scale
):
    frames, model_width = queries.shape
    grad_heads = head_split(grad_attended)
    query_heads = head_split(queries)
    delta = jnp.zeros((HEAD_COUNT, frames), jnp.float32)
    for offset in range(len(blocks)):

        def attention_update(carry, block=blocks[offset], allowed=allowed_list[offset]):
            probs = block_probs(queries, block, allowed, row_max, row_sum, score_scale)
            dprobs = jnp.einsum(
                "qhd,khd->hqk",
                grad_heads,
                head_split(block[:, model_width:]),
                preferred_element_type=jnp.float32,
            )
            return carry + jnp.sum(probs * dprobs, axis=2)

        delta = lax.cond(live_list[offset], attention_update, keep_same, delta)
    grad_queries = jnp.zeros((frames, HEAD_COUNT, HEAD_DIM), jnp.float32)
    contributions = []
    for offset in range(len(blocks)):

        def block_grads(block=blocks[offset], allowed=allowed_list[offset]):
            probs = block_probs(queries, block, allowed, row_max, row_sum, score_scale)
            value_heads = head_split(block[:, model_width:])
            dprobs = jnp.einsum(
                "qhd,khd->hqk", grad_heads, value_heads, preferred_element_type=jnp.float32
            )
            dscores = (probs * (dprobs - delta[:, :, None]) * score_scale).astype(jnp.bfloat16)
            query_part = jnp.einsum(
                "hqk,khd->qhd",
                dscores,
                head_split(block[:, :model_width]),
                preferred_element_type=jnp.float32,
            )
            key_part = jnp.einsum(
                "hqk,qhd->khd", dscores, query_heads, preferred_element_type=jnp.float32
            )
            value_part = jnp.einsum(
                "hqk,qhd->khd",
                probs.astype(jnp.bfloat16),
                grad_heads,
                preferred_element_type=jnp.float32,
            )
            joined = jnp.concatenate(
                [key_part.reshape(frames, model_width), value_part.reshape(frames, model_width)],
                axis=1,
            )
            return (query_part, joined)

        def no_grads():
            return (
                jnp.zeros((frames, HEAD_COUNT, HEAD_DIM), jnp.float32),
                jnp.zeros((frames, 2 * model_width), jnp.float32),
            )

        query_part, joined = lax.cond(live_list[offset], block_grads, no_grads)
        grad_queries = grad_queries + query_part
        contributions.append(joined)
    return (grad_queries.reshape(frames, model_width), contributions)


def shards(
    tokens,
    lengths,
    key_mask,
    cotangent,
    w_qkv,
    w_out,
    w_up,
    w_down,
    ln1_gain,
    ln1_bias,
    ln2_gain,
    ln2_bias,
    out_bias,
    up_bias,
    down_bias,
):
    gathered = (
        lax.all_gather(w_qkv, "seq", axis=0, tiled=True),
        lax.all_gather(w_out, "seq", axis=0, tiled=True),
        lax.all_gather(w_up, "seq", axis=0, tiled=True),
        lax.all_gather(w_down, "seq", axis=0, tiled=True),
        lax.all_gather(ln1_gain, "seq", axis=0, tiled=True),
        lax.all_gather(ln1_bias, "seq", axis=0, tiled=True),
        lax.all_gather(ln2_gain, "seq", axis=0, tiled=True),
        lax.all_gather(ln2_bias, "seq", axis=0, tiled=True),
        lax.all_gather(out_bias, "seq", axis=0, tiled=True),
        lax.all_gather(up_bias, "seq", axis=0, tiled=True),
        lax.all_gather(down_bias, "seq", axis=0, tiled=True),
    )
    qkv_full, out_full, up_full, down_full = (gathered[0], gathered[1], gathered[2], gathered[3])
    gain_one, shift_one, gain_two, shift_two, out_shift, up_shift, down_shift = tuple(
        (member.astype(jnp.float32) for member in gathered[4:])
    )
    frames = tokens.shape[1]
    model_width = tokens.shape[2]
    cycle_size = lax.axis_size("seq")
    group_frames = frames * cycle_size
    longest = min(MAXCAP, group_frames // 2)
    reach = longest // frames
    my_index = lax.axis_index("seq")
    score_scale = HEAD_DIM ** (-0.5)
    seg_all = segment_ids(lengths[0], group_frames)
    key_on = key_mask[0]
    query_pos = my_index * frames + jnp.arange(frames, dtype=jnp.int32)
    query_seg = lax.dynamic_slice_in_dim(seg_all, my_index * frames, frames)
    allowed_list = [
        block_allowed(my_index, offset, frames, seg_all, key_on, query_seg, query_pos)
        for offset in range(reach + 1)
    ]
    live_list = [jnp.any(allowed) for allowed in allowed_list]
    inputs = tokens[0].astype(jnp.float32)
    normed_one = norm_rows(inputs, gain_one, shift_one).astype(jnp.bfloat16)
    qkv_low = jnp.dot(normed_one, qkv_full, preferred_element_type=jnp.float32).astype(jnp.bfloat16)
    queries = qkv_low[:, :model_width]
    kv_own = qkv_low[:, model_width:]
    blocks = forward_chain(kv_own, reach)
    row_max, row_sum = softmax_stats(queries, blocks, allowed_list, live_list, score_scale)
    attended = attend_values(
        queries, blocks, allowed_list, live_list, row_max, row_sum, score_scale
    )
    branch = jnp.dot(attended, out_full, preferred_element_type=jnp.float32) + out_shift
    middle = inputs + branch
    normed_two = norm_rows(middle, gain_two, shift_two).astype(jnp.bfloat16)
    up_value = jnp.dot(normed_two, up_full, preferred_element_type=jnp.float32) + up_shift
    activated = gelu_exact(up_value).astype(jnp.bfloat16)
    result = middle + jnp.dot(activated, down_full, preferred_element_type=jnp.float32) + down_shift
    grad_result = cotangent[0]
    grad_down_w = trans_times(activated, grad_result)
    grad_down_b = jnp.sum(grad_result.astype(jnp.float32), axis=0)
    grad_act = times_trans(grad_result, down_full)
    grad_up = jax.vjp(gelu_exact, up_value)[1](grad_act)[0].astype(jnp.bfloat16)
    grad_up_w = trans_times(normed_two, grad_up)
    grad_up_b = jnp.sum(grad_up.astype(jnp.float32), axis=0)
    grad_normed_two = times_trans(grad_up, up_full)
    pull_two = jax.vjp(norm_rows, middle, gain_two, shift_two)[1]
    grad_mid_norm, grad_gain_two, grad_shift_two = pull_two(grad_normed_two)
    grad_middle = grad_result.astype(jnp.float32) + grad_mid_norm
    grad_branch = grad_middle.astype(jnp.bfloat16)
    grad_out_w = trans_times(attended, grad_branch)
    grad_out_b = jnp.sum(grad_branch.astype(jnp.float32), axis=0)
    grad_attended = times_trans(grad_branch, out_full).astype(jnp.bfloat16)
    back_blocks = again_chain(kv_own, reach)
    grad_queries, contributions = attention_grads(
        queries, grad_attended, back_blocks, allowed_list, live_list, row_max, row_sum, score_scale
    )
    flowing = contributions[reach]
    for offset in range(reach - 1, -1, -1):
        flowing = (
            shifted(flowing.astype(jnp.bfloat16), "seq", -1).astype(flowing.dtype)
            + contributions[offset]
        )
    grad_qkv = jnp.concatenate([grad_queries, flowing], axis=1).astype(jnp.bfloat16)
    grad_qkv_w = trans_times(normed_one, grad_qkv)
    grad_normed_one = times_trans(grad_qkv, qkv_full)
    pull_one = jax.vjp(norm_rows, inputs, gain_one, shift_one)[1]
    grad_in_norm, grad_gain_one, grad_shift_one = pull_one(grad_normed_one)
    grad_inputs = (grad_middle + grad_in_norm).astype(jnp.bfloat16)
    shares = (
        lax.psum_scatter(
            grad_qkv_w.astype(jnp.bfloat16), "seq", scatter_dimension=0, tiled=True
        ).astype(jnp.float32),
        lax.psum_scatter(
            grad_out_w.astype(jnp.bfloat16), "seq", scatter_dimension=0, tiled=True
        ).astype(jnp.float32),
        lax.psum_scatter(
            grad_up_w.astype(jnp.bfloat16), "seq", scatter_dimension=0, tiled=True
        ).astype(jnp.float32),
        lax.psum_scatter(
            grad_down_w.astype(jnp.bfloat16), "seq", scatter_dimension=0, tiled=True
        ).astype(jnp.float32),
        lax.psum_scatter(
            grad_gain_one.astype(jnp.bfloat16), "seq", scatter_dimension=0, tiled=True
        ).astype(jnp.float32),
        lax.psum_scatter(
            grad_shift_one.astype(jnp.bfloat16), "seq", scatter_dimension=0, tiled=True
        ).astype(jnp.float32),
        lax.psum_scatter(
            grad_gain_two.astype(jnp.bfloat16), "seq", scatter_dimension=0, tiled=True
        ).astype(jnp.float32),
        lax.psum_scatter(
            grad_shift_two.astype(jnp.bfloat16), "seq", scatter_dimension=0, tiled=True
        ).astype(jnp.float32),
        lax.psum_scatter(
            grad_out_b.astype(jnp.bfloat16), "seq", scatter_dimension=0, tiled=True
        ).astype(jnp.float32),
        lax.psum_scatter(
            grad_up_b.astype(jnp.bfloat16), "seq", scatter_dimension=0, tiled=True
        ).astype(jnp.float32),
        lax.psum_scatter(
            grad_down_b.astype(jnp.bfloat16), "seq", scatter_dimension=0, tiled=True
        ).astype(jnp.float32),
    )
    reduced = (
        lax.psum(shares[0].astype(jnp.bfloat16), "batch").astype(jnp.float32),
        lax.psum(shares[1].astype(jnp.bfloat16), "batch").astype(jnp.float32),
        lax.psum(shares[2].astype(jnp.bfloat16), "batch").astype(jnp.float32),
        lax.psum(shares[3].astype(jnp.bfloat16), "batch").astype(jnp.float32),
        lax.psum(shares[4].astype(jnp.bfloat16), "batch").astype(jnp.float32),
        lax.psum(shares[5].astype(jnp.bfloat16), "batch").astype(jnp.float32),
        lax.psum(shares[6].astype(jnp.bfloat16), "batch").astype(jnp.float32),
        lax.psum(shares[7].astype(jnp.bfloat16), "batch").astype(jnp.float32),
        lax.psum(shares[8].astype(jnp.bfloat16), "batch").astype(jnp.float32),
        lax.psum(shares[9].astype(jnp.bfloat16), "batch").astype(jnp.float32),
        lax.psum(shares[10].astype(jnp.bfloat16), "batch").astype(jnp.float32),
    )
    return (
        result.astype(jnp.bfloat16)[None],
        grad_inputs[None],
        reduced[0],
        reduced[1],
        reduced[2],
        reduced[3],
        reduced[4],
        reduced[5],
        reduced[6],
        reduced[7],
        reduced[8],
        reduced[9],
        reduced[10],
    )


LANES = 128
TILE = 512
UTTERANCES = 4
SHRINK = 1
PARAMS = pltpu.CompilerParams(dimension_semantics=("arbitrary",), vmem_limit_bytes=56 << 20)


def dot_nt(left, right):
    return lax.dot_general(
        left, right, (((1,), (1,)), ((), ())), preferred_element_type=jnp.float32
    )


def dot_nn(left, right):
    return lax.dot_general(
        left, right, (((1,), (0,)), ((), ())), preferred_element_type=jnp.float32
    )


def dot_tn(left, right):
    return lax.dot_general(
        left, right, (((0,), (0,)), ((), ())), preferred_element_type=jnp.float32
    )


def norm_stats(values):
    centre = jnp.mean(values, axis=-1, keepdims=True)
    centred = values - centre
    spread = jnp.mean(centred * centred, axis=-1, keepdims=True)
    inverse = lax.rsqrt(spread + EPSILON)
    return centred * inverse, inverse


def norm_back(grad, normed, inverse, gain):
    g = grad * gain
    return inverse * (
        g
        - jnp.mean(g, axis=-1, keepdims=True)
        - normed * jnp.mean(g * normed, axis=-1, keepdims=True)
    )


def whole(*shape):
    return pl.BlockSpec(shape, lambda *_: (0,) * len(shape))


def like(shape, kind):
    return jax.ShapeDtypeStruct(shape, kind)


def call(kernel, name, grid, in_specs, out_specs, out_shape, scratch=(), flops=0):
    def run(ids, *args):
        bytes_accessed = sum(a.size * a.dtype.itemsize for a in args)
        return pl.pallas_call(
            kernel,
            out_shape=out_shape,
            grid_spec=pltpu.PrefetchScalarGridSpec(
                num_scalar_prefetch=1,
                grid=(grid,),
                in_specs=in_specs,
                out_specs=out_specs,
                scratch_shapes=list(scratch),
            ),
            compiler_params=PARAMS,
            cost_estimate=pl.CostEstimate(
                flops=flops // SHRINK,
                bytes_accessed=2 * bytes_accessed // SHRINK,
                transcendentals=0,
            ),
            name=name,
        )(ids, *args)

    return run


CORE, CHIP_X, SQUARE, Y_BIT = 0, 1, 2, 3


def norm_kernel(ids, tokens, vectors, out):
    normed, _ = norm_stats(tokens[...].astype(jnp.float32))
    out[...] = (normed * vectors[0:1, :] + vectors[1:2, :]).astype(jnp.bfloat16)


def project_kernel(ids, own, y_one, z_one, top, bottom, w_own, w_other, out, leaving, natural):
    square = ids[SQUARE]
    corner = jnp.where(pl.program_id(0) < 2, top[...], bottom[...])
    pieces = (own[...], y_one[...], z_one[...], corner)
    rows = jnp.concatenate(pieces, axis=0)
    size = corner.shape[0]
    mine = dot_nn(rows, w_own[...]).astype(jnp.bfloat16)
    other = dot_nn(rows, w_other[...]).astype(jnp.bfloat16)
    for j in range(4):
        at = pl.ds(square ^ j, 1)
        natural[at] = pieces[j][None]
        out[at] = mine[None, j * size : (j + 1) * size]
        leaving[at] = other[None, j * size : (j + 1) * size]


def head_lanes(block, head):
    lane = lax.broadcasted_iota(jnp.int32, block.shape, 1)
    keep = (lane < HEAD_DIM) if head == 0 else (lane >= HEAD_DIM)
    return jnp.where(keep, block, jnp.zeros_like(block))


def join_heads(ids, own, came, qkv):
    half = own.shape[0]
    for rows, side in ((own, ids[CORE]), (came, 1 - ids[CORE])):
        at = pl.ds(pl.multiple_of(side * half, half), half)
        qkv[at, 0:LANES] = rows[:, 0:LANES] * jnp.bfloat16(HEAD_DIM ** (-0.5))
        qkv[at, LANES : 3 * LANES] = rows[:, LANES : 3 * LANES]


def first_frames(bounds, positions):
    start = jnp.zeros_like(positions)
    for u in range(1, UTTERANCES):
        start = jnp.where(positions >= bounds[2, u], bounds[2, u], start)
    return start


def spread_places(places_row, column):
    for j in range(places_row.shape[1] // TILE):
        row = places_row[:, j * TILE : (j + 1) * TILE]
        column[j * TILE : (j + 1) * TILE, :] = jnp.transpose(
            jnp.broadcast_to(row, (LANES, TILE))
        )


def allowed_keys(column, at, start, diagonal):
    places = jnp.concatenate([column[pl.ds(at, TILE), :]] * (TILE // LANES), axis=1)
    allowed = places >= start
    if diagonal:
        key = lax.broadcasted_iota(jnp.int32, (TILE, TILE), 0)
        query = lax.broadcasted_iota(jnp.int32, (TILE, TILE), 1)
        allowed = (allowed & (key < query)) | (key == query)
    return allowed


def row_starts(bounds, base):
    return first_frames(bounds, base + lax.broadcasted_iota(jnp.int32, (1, TILE), 1)).astype(
        jnp.float32
    )


def attend_kernel(
    ids, bounds, own, came, places_row, out, lse, qkv, turned, column, scores, top, total, acc
):
    tile = pl.program_id(0)
    base = pl.multiple_of(tile * TILE, TILE)

    @pl.when(tile == 0)
    def _():
        join_heads(ids, own, came, qkv)
        spread_places(places_row, column)
        for j in range(qkv.shape[0] // TILE):
            rows = slice(j * TILE, (j + 1) * TILE)
            turned[:, rows] = jnp.transpose(qkv[rows, 2 * LANES : 3 * LANES])

    queries = [head_lanes(qkv[pl.ds(base, TILE), 0:LANES], head) for head in range(2)]
    top[...] = jnp.full_like(top, NEGATIVE)
    total[...] = jnp.zeros_like(total)
    acc[...] = jnp.zeros_like(acc)

    start = row_starts(bounds, base)

    def step(j, diagonal):
        at = pl.multiple_of(j * TILE, TILE)
        keys = qkv[pl.ds(at, TILE), LANES : 2 * LANES]
        allowed = allowed_keys(column, at, start, diagonal)
        for head in range(2):
            value = jnp.where(allowed, dot_nt(keys, queries[head]), NEGATIVE)
            scores[head, j] = value
            top[head : head + 1, :] = jnp.maximum(
                top[head : head + 1, :], jnp.max(value, axis=0, keepdims=True)
            )

    def first_pass(j, carry):
        step(j, False)
        return carry

    def second_pass(j, carry):
        at = pl.multiple_of(j * TILE, TILE)
        for head in range(2):
            probs = jnp.exp(scores[head, j] - top[head : head + 1, :])
            total[head : head + 1, :] += jnp.sum(probs, axis=0, keepdims=True)
            values = turned[head * HEAD_DIM : (head + 1) * HEAD_DIM, pl.ds(at, TILE)]
            acc[head] += dot_nn(values, probs.astype(jnp.bfloat16))
        return carry

    lax.fori_loop(bounds[0, tile], tile, first_pass, 0)
    step(tile, True)
    lax.fori_loop(bounds[0, tile], tile + 1, second_pass, 0)
    both = jnp.concatenate([acc[0] / total[0:1, :], acc[1] / total[1:2, :]], axis=0)
    out[0] = jnp.transpose(both).astype(jnp.bfloat16)
    lse[:, pl.ds(base, TILE)] = top[...] + jnp.log(total[...])


def block_order(i):
    return 2 * (i % 4) + i // 4


def attend(ids, bounds, own, came, places):
    rows = 2 * own.shape[0]
    return pl.pallas_call(
        attend_kernel,
        out_shape=(like((8, TILE, LANES), jnp.bfloat16), like((2, rows), jnp.float32)),
        grid_spec=pltpu.PrefetchScalarGridSpec(
            num_scalar_prefetch=2,
            grid=(rows // TILE,),
            in_specs=[
                whole(*own.shape),
                whole(*came.shape),
                whole(1, rows),
            ],
            out_specs=[
                pl.BlockSpec((1, TILE, LANES), lambda i, *_: (block_order(i), 0, 0)),
                whole(2, rows),
            ],
            scratch_shapes=[
                pltpu.VMEM((rows, 3 * LANES), jnp.bfloat16),
                pltpu.VMEM((LANES, rows), jnp.bfloat16),
                pltpu.VMEM((rows, LANES), jnp.float32),
                pltpu.VMEM((2, rows // TILE, TILE, TILE), jnp.float32),
                pltpu.VMEM((2, TILE), jnp.float32),
                pltpu.VMEM((2, TILE), jnp.float32),
                pltpu.VMEM((2, HEAD_DIM, TILE), jnp.float32),
            ],
        ),
        compiler_params=PARAMS,
        cost_estimate=pl.CostEstimate(
            flops=rows * rows * 256 // SHRINK, bytes_accessed=rows * 2400, transcendentals=rows * rows
        ),
        name="attend",
    )(ids, bounds, own, came, places)


def attend_back_kernel(
    ids,
    bounds,
    own,
    came,
    grad_own,
    grad_came,
    attended,
    places_row,
    lse,
    out,
    leaving,
    qkv,
    grad,
    delta,
    grad_queries,
    grad_kv,
    column,
):
    tile = pl.program_id(0)
    base = pl.multiple_of(tile * TILE, TILE)
    core = ids[CORE]

    @pl.when(tile == 0)
    def _():
        join_heads(ids, own, came, qkv)
        spread_places(places_row, column)
        grad_queries[...] = jnp.zeros_like(grad_queries)
        for j in range(4):
            for rows, side in ((grad_own, core), (grad_came, 1 - core)):
                at = pl.multiple_of((4 * side + j) * TILE, TILE)
                block = rows[pl.ds(2 * j + core, 1)].reshape(TILE, LANES)
                grad[pl.ds(at, TILE), :] = block
                product = block.astype(jnp.float32) * attended[
                    pl.ds(2 * j + side, 1)
                ].reshape(TILE, LANES).astype(jnp.float32)
                turned = jnp.transpose(product)
                delta[0:1, pl.ds(at, TILE)] = jnp.sum(turned[:HEAD_DIM], axis=0, keepdims=True)
                delta[1:2, pl.ds(at, TILE)] = jnp.sum(turned[HEAD_DIM:], axis=0, keepdims=True)

    keys = qkv[pl.ds(base, TILE), LANES : 2 * LANES]
    values = qkv[pl.ds(base, TILE), 2 * LANES : 3 * LANES]
    turned_keys = jnp.transpose(keys)
    grad_kv[...] = jnp.zeros_like(grad_kv)

    def step(i, diagonal):
        at = pl.multiple_of(i * TILE, TILE)
        scaled = qkv[pl.ds(at, TILE), 0:LANES]
        grads = grad[pl.ds(at, TILE), :]
        allowed = allowed_keys(column, base, row_starts(bounds, at), diagonal)
        key_part = grad_kv[0]
        value_part = grad_kv[1]
        for head in range(2):
            queries = head_lanes(scaled, head)
            head_grads = head_lanes(grads, head)
            scores = jnp.where(allowed, dot_nt(keys, queries), NEGATIVE)
            probs = jnp.exp(scores - lse[head : head + 1, pl.ds(at, TILE)])
            dprobs = dot_nt(values, head_grads)
            dscores = (probs * (dprobs - delta[head : head + 1, pl.ds(at, TILE)])).astype(
                jnp.bfloat16
            )
            value_part = value_part + dot_nn(probs.astype(jnp.bfloat16), head_grads)
            key_part = key_part + dot_nn(dscores, queries)
            lanes = slice(head * HEAD_DIM, (head + 1) * HEAD_DIM)
            grad_queries[lanes, pl.ds(at, TILE)] += dot_nn(turned_keys[lanes, :], dscores)
        grad_kv[0] = key_part
        grad_kv[1] = value_part

    def later_step(i, carry):
        step(i, False)
        return carry

    step(tile, True)
    lax.fori_loop(tile + 1, bounds[1, tile], later_step, 0)

    def store(target):
        at = pl.ds(pl.multiple_of((tile % 4) * TILE, TILE), TILE)
        target[at, 0:LANES] = (
            jnp.transpose(grad_queries[:, pl.ds(base, TILE)]) * HEAD_DIM ** (-0.5)
        ).astype(jnp.bfloat16)
        target[at, LANES : 2 * LANES] = grad_kv[0].astype(jnp.bfloat16)
        target[at, 2 * LANES : 3 * LANES] = grad_kv[1].astype(jnp.bfloat16)

    @pl.when(tile // 4 == core)
    def _():
        store(out)

    @pl.when(tile // 4 != core)
    def _():
        store(leaving)


def attend_back(ids, bounds, own, came, grad_own, grad_came, attended, places, lse):
    half = own.shape[0]
    rows = 2 * half
    return pl.pallas_call(
        attend_back_kernel,
        out_shape=(like(own.shape, jnp.bfloat16), like(own.shape, jnp.bfloat16)),
        grid_spec=pltpu.PrefetchScalarGridSpec(
            num_scalar_prefetch=2,
            grid=(rows // TILE,),
            in_specs=[
                whole(*own.shape),
                whole(*came.shape),
                whole(*grad_own.shape),
                whole(*grad_came.shape),
                whole(*attended.shape),
                whole(1, rows),
                whole(2, rows),
            ],
            out_specs=[whole(*own.shape), whole(*own.shape)],
            scratch_shapes=[
                pltpu.VMEM((rows, 3 * LANES), jnp.bfloat16),
                pltpu.VMEM((rows, LANES), jnp.bfloat16),
                pltpu.VMEM((2, rows), jnp.float32),
                pltpu.VMEM((LANES, rows), jnp.float32),
                pltpu.VMEM((2, TILE, LANES), jnp.float32),
                pltpu.VMEM((rows, LANES), jnp.float32),
            ],
        ),
        compiler_params=PARAMS,
        cost_estimate=pl.CostEstimate(
            flops=rows * rows * 640 // SHRINK, bytes_accessed=rows * 2400, transcendentals=rows * rows
        ),
        name="attend_back",
    )(ids, bounds, own, came, grad_own, grad_came, attended, places, lse)


def attend_bounds(start, starts, rows):
    tiles = rows // TILE
    first = start[:: TILE]
    key_last = jnp.arange(1, tiles + 1, dtype=jnp.int32) * TILE - 1
    far_end = jnp.sum((first[None, :] <= key_last[:, None]).astype(jnp.int32), axis=1)
    starts = jnp.pad(starts, (0, tiles - starts.shape[0]))
    return jnp.stack([first // TILE, far_end, starts]).astype(jnp.int32)


def out_kernel(ids, own, came, tokens, w_out, vectors, attended, middle, normed):
    core = ids[CORE]
    rows, width = tokens.shape
    mine, other = [], []
    for j in range(4):
        mine.append(own[pl.ds(2 * j + core, 1)].reshape(rows, LANES))
        other.append(came[pl.ds(2 * j + core, 1)].reshape(rows, LANES))
    mine, other = jnp.concatenate(mine, axis=1), jnp.concatenate(other, axis=1)
    first = jnp.where(core == 0, mine, other)
    second = jnp.where(core == 0, other, mine)
    joined = jnp.concatenate([first, second], axis=1)
    attended[...] = joined
    branch = dot_nn(joined, w_out[...].reshape(width, width)) + vectors[4:5, :]
    value = tokens[...].astype(jnp.float32) + branch
    middle[...] = value
    xhat, _ = norm_stats(value)
    normed[...] = (xhat * vectors[2:3, :] + vectors[3:4, :]).astype(jnp.bfloat16)


def forward_kernel(
    ids,
    normed_own,
    normed_came,
    grad_own,
    grad_came,
    up_a,
    up_b,
    down_a,
    down_b,
    vectors,
    act,
    grad_up,
    up_bias,
    result_own,
    result_came,
    back_own,
    back_came,
    result,
    back,
):
    step = pl.program_id(0)
    core = ids[CORE]
    frames, width = normed_own.shape

    @pl.when(step == 0)
    def _():
        result[...] = jnp.zeros_like(result)
        back[...] = jnp.zeros_like(back)

    def weave(first, second, axis):
        parts = []
        for k in range(2):
            for block in (first, second):
                at = [slice(None), slice(None)]
                at[axis] = slice(k * LANES, (k + 1) * LANES)
                parts.append(block[tuple(at)])
        return jnp.concatenate(parts, axis=axis)

    wide_step = 2 * LANES
    w_up = weave(up_a[...].reshape(width, wide_step), up_b[...].reshape(width, wide_step), 1)
    w_down = weave(down_a[...].reshape(wide_step, width), down_b[...].reshape(wide_step, width), 0)
    shift = jnp.where(
        core == 0,
        weave(vectors[6:7, :], vectors[7:8, :], 1),
        weave(vectors[8:9, :], vectors[9:10, :], 1),
    )
    sides = ((normed_own, grad_own), (normed_came, grad_came))
    values = [dot_nn(normed[...], w_up) + shift for normed, _ in sides]
    slopes = [dot_nt(grad[...], w_down) for _, grad in sides]
    bias = jnp.zeros((1, 4 * LANES), jnp.float32)
    for side, (value, slope) in enumerate(zip(values, slopes)):
        half = 0.5 + 0.5 * lax.erf(value * 0.7071067811865476)
        bell = jnp.exp(-0.5 * value * value) * 0.3989422804014327
        activated = (value * half).astype(jnp.bfloat16)
        change = (slope * (half + value * bell)).astype(jnp.bfloat16)
        act[side] = activated
        grad_up[side] = change
        bias = bias + jnp.sum(change.astype(jnp.float32), axis=0, keepdims=True)
        result[side] += dot_nn(activated, w_down)
        back[side] += dot_nt(change, w_up)
    for k in range(4):
        at = slice((k // 2) * LANES, (k // 2 + 1) * LANES)
        up_bias[k % 2 : k % 2 + 1, at] = bias[:, k * LANES : (k + 1) * LANES]

    @pl.when(step == 3)
    def _():
        result_own[...] = result[0]
        result_came[...] = result[1].astype(jnp.bfloat16)
        back_own[...] = back[0]
        back_came[...] = back[1].astype(jnp.bfloat16)


def middle_kernel(
    ids, back_own, back_came, middle, cotangent, w_out, vectors, grad_middle, grad_branch, out, sums
):
    step = pl.program_id(0)
    xhat, inverse = norm_stats(middle[...])
    grad = back_own[...] + back_came[...].astype(jnp.float32)
    value = cotangent[...].astype(jnp.float32) + norm_back(grad, xhat, inverse, vectors[2:3, :])
    grad_middle[...] = value
    low = value.astype(jnp.bfloat16)
    grad_branch[...] = low

    @pl.when(step == 0)
    def _():
        sums[...] = jnp.zeros_like(sums)

    sums[0:1, :] += jnp.sum(grad * xhat, axis=0, keepdims=True)
    sums[1:2, :] += jnp.sum(grad, axis=0, keepdims=True)
    sums[2:3, :] += jnp.sum(low.astype(jnp.float32), axis=0, keepdims=True)
    sums[3:4, :] += jnp.sum(cotangent[...].astype(jnp.float32), axis=0, keepdims=True)
    width = w_out.shape[-1]
    spread = dot_nt(low, w_out[...].reshape(width, width)).astype(jnp.bfloat16)
    for group in range(8):
        out[block_order(group)] = spread[:, group * LANES : (group + 1) * LANES]


def grad_out_kernel(ids, attended, grad_branch, kept, leaving):
    core = ids[CORE]
    grad = dot_tn(attended[...], grad_branch[...]).astype(jnp.bfloat16)
    half = grad.shape[1] // 2
    shape = kept.shape
    kept[...] = jnp.where(core == 0, grad[:, :half], grad[:, half:]).reshape(shape)
    leaving[...] = jnp.where(core == 0, grad[:, half:], grad[:, :half]).reshape(shape)


def grad_down_kernel(ids, act, grad_own, grad_came, out):
    grad = dot_tn(act[0], grad_own[...]) + dot_tn(act[1], grad_came[...])
    out[...] = grad.astype(jnp.bfloat16)


def grad_up_kernel(ids, normed_own, normed_came, grad_up, out_own, out_came, kept, leaving):
    chip_x = ids[CHIP_X]
    grad = (dot_tn(normed_own[...], grad_up[0]) + dot_tn(normed_came[...], grad_up[1])).astype(
        jnp.bfloat16
    )
    half = grad.shape[1] // 2
    shape = kept.shape[:2] + (half,)
    kept[:, :, :half] = jnp.where(chip_x == 0, grad[:, :half], grad[:, half:]).reshape(shape)
    leaving[:, :, :half] = jnp.where(chip_x == 0, grad[:, half:], grad[:, :half]).reshape(shape)
    more = (out_own[...].astype(jnp.float32) + out_came[...].astype(jnp.float32)).astype(
        jnp.bfloat16
    )
    cut = more.shape[2] // 2
    kept[:, :, half:] = jnp.where(chip_x == 0, more[:, :, :cut], more[:, :, cut:])
    leaving[:, :, half:] = jnp.where(chip_x == 0, more[:, :, cut:], more[:, :, :cut])


def back_project_kernel(
    ids,
    own,
    came,
    w_own,
    w_other,
    first,
    y_out,
    z_out,
    keep_left,
    keep_right,
    grads,
):
    square = ids[SQUARE]
    size, width = first.shape
    half = width // 2
    rows = 4 * size
    value = dot_nt(own[...].reshape(rows, 3 * LANES), w_own[...])
    value = value + dot_nt(came[...].reshape(rows, 3 * LANES), w_other[...])
    grads[...] = value.reshape(4, size, width)
    first[...] = grads[square]
    y_out[0] = grads[square ^ 1, :, :half].astype(jnp.bfloat16)
    keep_right[...] = grads[square ^ 1, :, half:]
    z_out[0] = grads[square ^ 2, :, half:].astype(jnp.bfloat16)
    keep_left[...] = grads[square ^ 2, :, :half]
    y_out[1] = grads[square ^ 3, :, :half].astype(jnp.bfloat16)
    z_out[1] = grads[square ^ 3, :, half:].astype(jnp.bfloat16)


def first_sums_kernel(
    ids, first, y_out, z_out, keep_left, keep_right, natural, vectors, sums
):
    square = ids[SQUARE]
    half = first.shape[1] // 2
    wide = jnp.float32
    parts = (
        (first[:, :half], first[:, half:]),
        (y_out[0].astype(wide), keep_right[...]),
        (keep_left[...], z_out[0].astype(wide)),
        (y_out[1].astype(wide), z_out[1].astype(wide)),
    )

    @pl.when(pl.program_id(0) == 0)
    def _():
        sums[...] = jnp.zeros_like(sums)

    for j in range(4):
        for side in range(2):
            lanes = slice(side * half, (side + 1) * half)
            value = parts[j][side]
            rows = natural[square ^ j, :, lanes].astype(wide)
            normed = (rows - vectors[1:2, lanes]) / vectors[0:1, lanes]
            sums[0:1, lanes] += jnp.sum(value * normed, axis=0, keepdims=True)
            sums[1:2, lanes] += jnp.sum(value, axis=0, keepdims=True)


def second_kernel(ids, keep_left, keep_right, y_came, z_came, z_out, y_out):
    z_out[...] = (keep_left[...] + y_came[1].astype(jnp.float32)).astype(jnp.bfloat16)
    y_out[...] = (keep_right[...] + z_came[1].astype(jnp.float32)).astype(jnp.bfloat16)


def last_kernel(ids, first, y_came, z_came, z_second, y_second, tokens, grad_middle, vectors, out):
    wide = jnp.float32
    left = y_came[0].astype(wide) + z_second[...].astype(wide)
    right = z_came[0].astype(wide) + y_second[...].astype(wide)
    grad = first[...] + jnp.concatenate([left, right], axis=1)
    xhat, inverse = norm_stats(tokens[...].astype(wide))
    out[...] = (grad_middle[...] + norm_back(grad, xhat, inverse, vectors[0:1, :])).astype(
        jnp.bfloat16
    )


def grad_heads_kernel(ids, normed, grads, out):
    out[...] = dot_tn(normed[...], grads[...]).astype(jnp.bfloat16)


def spread_kernel(
    ids,
    heads,
    heads_came,
    down,
    down_came,
    mixed,
    mixed_x,
    mixed_core,
    mixed_both,
    qkv_out,
    out_out,
    up_out,
    down_out,
):
    wide = jnp.float32
    core, chip_x = ids[CORE], ids[CHIP_X]

    def ordered(side, own, other):
        return jnp.where(side == 0, own, other), jnp.where(side == 0, other, own)

    for side, blocks in enumerate(ordered(core, heads[...], heads_came[...])):
        for j in range(4):
            for k in range(3):
                at = k * 8 * LANES + (4 * side + j) * LANES
                qkv_out[:, at : at + LANES] = blocks[j, :, k * LANES : (k + 1) * LANES].astype(wide)
    rows = down.shape[0]
    for side, block in enumerate(ordered(core, down[...], down_came[...])):
        down_out[side * rows : (side + 1) * rows, :] = block.astype(wide)
    own = ordered(chip_x, mixed[...], mixed_x[...])
    came = ordered(chip_x, mixed_core[...], mixed_both[...])
    width = out_out.shape[1]
    step = 2 * LANES
    for x in range(2):
        for side, block in enumerate(ordered(core, own[x], came[x])):
            for j in range(4):
                at = (4 * x + j) * 2 * step + side * step
                up_out[:, at : at + step] = block[:, j * step : (j + 1) * step].astype(wide)
            at = side * 2 * step + x * step
            out_out[:, at : at + step] = block[:, width:].astype(wide)


def hop_batch(block, bit):
    size = lax.axis_size("batch")
    return lax.ppermute(block, "batch", [(i, i ^ bit) for i in range(size)])


def hop_seq(block, bits):
    size = lax.axis_size("seq")
    return lax.ppermute(block, "seq", [(i, i ^ bits) for i in range(size)])


def swap_halves(block):
    batches, seqs = lax.axis_size("batch"), lax.axis_size("seq")
    route = []
    for b in range(batches):
        for s in range(seqs):
            target = ((b & ~1) | (s >> 2)) * seqs + ((s & 3) | ((b & 1) << 2))
            route.append((b * seqs + s, target))
    return lax.ppermute(block, ("batch", "seq"), route)


def after(value, *anchors):
    return lax.optimization_barrier((value,) + anchors)[0]


def trade(block, groups):
    return lax.all_to_all(block, "seq", 0, 0, tiled=True, axis_index_groups=groups)


IN_SQUARE = [[0, 1, 2, 3], [4, 5, 6, 7]]
ALONG_Z = [[0, 2, 4, 6], [1, 3, 5, 7]]


def square_shards(
    tokens,
    lengths,
    key_mask,
    cotangent,
    w_qkv,
    w_out,
    w_up,
    w_down,
    ln1_gain,
    ln1_bias,
    ln2_gain,
    ln2_bias,
    out_bias,
    up_bias,
    down_bias,
):
    low, wide = jnp.bfloat16, jnp.float32
    batch_index = lax.axis_index("batch")
    seq_index = lax.axis_index("seq")
    core = batch_index & 1
    chip_x = batch_index >> 1
    square = seq_index & 3
    y_bit = seq_index & 1
    ids = jnp.stack([core, chip_x, square, y_bit]).astype(jnp.int32)
    frames, width = tokens.shape[1], tokens.shape[2]
    rows = 8 * frames
    part = width // 8
    quarter = 2 * core + chip_x

    up_piece = lax.dynamic_index_in_dim(w_up.reshape(part, 8, 4, LANES), quarter, 2, False)
    down_piece = lax.dynamic_slice_in_dim(w_down, quarter * part, part, 0)
    out_piece = lax.dynamic_slice_in_dim(w_out, batch_index * (part // 4), part // 4, 0)
    bundle = jnp.concatenate([down_piece, up_piece.reshape(part, width), out_piece], axis=0)
    deep = bundle.shape[0]

    tokens_here = swap_halves(tokens[0])
    heads = lax.dynamic_slice_in_dim(w_qkv.reshape(part, 3, 8, LANES), 4 * core, 4, 2)
    heads = heads.transpose(2, 0, 1, 3).reshape(4, part, 3 * LANES)
    small = jnp.concatenate(
        [
            jnp.stack([ln1_gain, ln1_bias, ln2_gain, ln2_bias, out_bias, down_bias]),
            up_bias.reshape(4, part),
            jnp.zeros((6, part), low),
        ],
        axis=0,
    )
    small = jnp.broadcast_to(jnp.pad(small, ((0, 0), (0, 2 * part)))[None], (4, 16, 3 * part))
    heads = jnp.concatenate([heads, small], axis=1)
    came = lax.all_to_all(jnp.concatenate([heads, heads], axis=0), "seq", 0, 0, tiled=True)
    vectors = came[:, part:, :part].astype(wide).transpose(1, 0, 2).reshape(16, width)
    w_heads = came[:, :part].reshape(width, 3 * LANES)
    w_other = hop_batch(w_heads, 1)

    meta = jnp.concatenate([key_mask[0], jnp.pad(lengths[0], (0, LANES - lengths.shape[1]))])
    meta = meta.reshape(-1, LANES)
    meta = jnp.where(core == (seq_index >> 2), meta, hop_batch(meta, 1)).reshape(-1)
    ends = jnp.cumsum(meta[rows : rows + lengths.shape[1]])
    starts = ends - meta[rows : rows + lengths.shape[1]]
    positions = jnp.arange(rows, dtype=jnp.int32)
    start = jnp.max(
        jnp.where(starts[None, :] <= positions[:, None], starts[None, :], 0), axis=1
    ).astype(jnp.int32)
    bounds = attend_bounds(start, starts, rows)
    places = jnp.where(meta[:rows] == 1, positions, -1).astype(wide)[None, :]

    fourth = frames // 4
    slab = pl.BlockSpec((fourth, width), lambda i, *_: (i, 0))
    half = frames // 2
    wide_slab = pl.BlockSpec((half, width), lambda i, *_: (i, 0))
    normed_one = call(
        norm_kernel,
        "norm",
        2,
        [wide_slab, whole(16, width)],
        wide_slab,
        like((frames, width), low),
    )(ids, tokens_here, vectors)
    y_one = hop_seq(normed_one, 1)
    z_one = hop_seq(normed_one, 2)
    bundle = lax.all_gather(after(bundle, tokens_here, came), ("seq", "batch"), axis=0, tiled=True)
    bundle = bundle.reshape(8, 4, deep, width)
    half = frames // 2
    top, bottom = hop_seq(y_one[:half], 2), hop_seq(z_one[half:], 1)
    heads_shape = (4, frames, 3 * LANES)
    top_slab = pl.BlockSpec((fourth, width), lambda i, *_: (jnp.minimum(i, 1), 0))
    bottom_slab = pl.BlockSpec((fourth, width), lambda i, *_: (jnp.maximum(i, 2) - 2, 0))
    heads_slab = pl.BlockSpec((4, fourth, 3 * LANES), lambda i, *_: (0, i, 0))
    natural_slab = pl.BlockSpec((4, fourth, width), lambda i, *_: (0, i, 0))
    heads_like = like(heads_shape, low)
    qkv_own, leaving, natural = call(
        project_kernel,
        "project",
        4,
        [slab] * 3 + [top_slab, bottom_slab] + [whole(*w_heads.shape)] * 2,
        [heads_slab, heads_slab, natural_slab],
        (heads_like, heads_like, like((4, frames, width), low)),
        flops=2 * 4 * frames * width * 6 * LANES,
    )(ids, normed_one, y_one, z_one, top, bottom, w_heads, w_other)
    qkv_came = hop_batch(leaving, 1).reshape(4 * frames, 3 * LANES)
    qkv_own = qkv_own.reshape(4 * frames, 3 * LANES)
    natural = natural.reshape(4 * frames, width)
    cotangent_own = swap_halves(after(cotangent[0], leaving))

    attended_heads, lse = attend(ids, bounds, qkv_own, qkv_came, places)
    cotangent_came = hop_batch(cotangent_own, 1)

    mine = trade(attended_heads, IN_SQUARE)
    mine_came = hop_batch(mine, 1)
    blocks = pl.BlockSpec((8, half, LANES), lambda i, *_: (0, i, 0))
    w_out_spec = pl.BlockSpec(
        (8, 4, part // 4, width), lambda *_: (0, 0, (deep * 4) // part - 1, 0)
    )
    attended, middle, normed_two = call(
        out_kernel,
        "out_project",
        2,
        [blocks, blocks, wide_slab, w_out_spec, whole(16, width)],
        [wide_slab] * 3,
        (like((frames, width), low), like((frames, width), wide), like((frames, width), low)),
        flops=2 * frames * width * width,
    )(ids, mine, mine_came, tokens_here, bundle, vectors)
    normed_two_came = hop_batch(normed_two, 1)

    up_specs = [
        pl.BlockSpec((8, 1, part, 2 * LANES), lambda s, ids, k=k: (0, 2 * k + ids[CORE], 1, s))
        for k in range(2)
    ]
    down_specs = [
        pl.BlockSpec((2, 1, part, width), lambda s, ids, k=k: (s, 2 * k + ids[CORE], 0, 0))
        for k in range(2)
    ]
    hidden = pl.BlockSpec((2, frames, 4 * LANES), lambda s, *_: (0, 0, s))
    act, grad_up, up_sums, result_own, result_leaving, back_own, back_leaving = call(
        forward_kernel,
        "feed_forward",
        4,
        [whole(frames, width)] * 4
        + up_specs
        + down_specs
        + [pl.BlockSpec((16, 2 * LANES), lambda s, *_: (0, s))],
        [hidden, hidden, pl.BlockSpec((8, 2 * LANES), lambda s, *_: (0, s))]
        + [whole(frames, width)] * 4,
        (
            like((2, frames, 2 * width), low),
            like((2, frames, 2 * width), low),
            like((8, width), wide),
            like((frames, width), wide),
            like((frames, width), low),
            like((frames, width), wide),
            like((frames, width), low),
        ),
        scratch=[pltpu.VMEM((2, frames, width), wide)] * 2,
        flops=2 * 4 * 2 * frames * width * 2 * width,
    )(
        ids,
        normed_two,
        normed_two_came,
        cotangent_own,
        cotangent_came,
        bundle,
        bundle,
        bundle,
        bundle,
        vectors,
    )
    back_came = hop_batch(back_leaving, 1)

    hidden_pair = pl.BlockSpec((2, frames, 4 * LANES), lambda s, *_: (0, 0, s))
    down = call(
        grad_down_kernel,
        "grad_down",
        4,
        [hidden_pair, whole(frames, width), whole(frames, width)],
        pl.BlockSpec((4 * LANES, width), lambda s, *_: (s, 0)),
        like((2 * width, width), low),
        flops=2 * 2 * frames * width * 2 * width,
    )(ids, act, cotangent_own, cotangent_came)
    back_own = after(back_own, down)
    down = lax.psum_scatter(down, "seq", scatter_dimension=0, tiled=True)
    grad_middle, grad_branch, spread, middle_sums = call(
        middle_kernel,
        "middle_back",
        2,
        [wide_slab] * 4 + [w_out_spec, whole(16, width)],
        [wide_slab, wide_slab, blocks, whole(8, width)],
        (
            like((frames, width), wide),
            like((frames, width), low),
            like((8, frames, LANES), low),
            like((8, width), wide),
        ),
        flops=2 * frames * width * width,
    )(ids, back_own, back_came, middle, cotangent_own, bundle, vectors)
    grad_mine = trade(spread, IN_SQUARE)
    grad_mine_came = hop_batch(grad_mine, 1)

    split = like((8, part, width // 2), low)
    split_spec = pl.BlockSpec((4,) + split.shape[1:], lambda s, *_: (s, 0, 0))
    column = pl.BlockSpec((frames, 4 * part), lambda s, *_: (0, s))
    out_kept, out_leaving = call(
        grad_out_kernel,
        "grad_out",
        2,
        [column, whole(frames, width)],
        [split_spec, split_spec],
        (split, split),
        flops=frames * width,
    )(ids, attended, grad_branch)
    out_came = hop_batch(out_leaving, 1)
    broad = like((8, part, width + width // 4), low)
    broad_spec = pl.BlockSpec((4,) + broad.shape[1:], lambda s, *_: (s, 0, 0))
    up_kept, up_leaving = call(
        grad_up_kernel,
        "grad_up",
        2,
        [column, column, whole(2, frames, 2 * width), split_spec, split_spec],
        [broad_spec, broad_spec],
        (broad, broad),
        flops=frames * width,
    )(ids, normed_two, normed_two_came, grad_up, out_kept, out_came)
    up_came = hop_batch(up_leaving, 2)

    result = (
        middle
        + result_own
        + hop_batch(result_leaving, 1).astype(wide)
        + vectors[5:6]
    ).astype(low)
    result_home = swap_halves(result[None])

    grad_mine = after(grad_mine, result, up_leaving)
    grad_qkv, grad_leaving = attend_back(
        ids,
        bounds,
        qkv_own,
        qkv_came,
        grad_mine,
        grad_mine_came,
        attended_heads,
        places,
        lse,
    )
    grad_leaving = after(grad_leaving, up_came, result_home)
    mixed = (up_kept.astype(wide) + after(up_came, grad_leaving).astype(wide)).astype(low)
    mixed = lax.psum_scatter(
        mixed.reshape(width, width + width // 4), "seq", scatter_dimension=0, tiled=True
    )
    grad_qkv_came = hop_batch(grad_leaving, 1)

    pair = (2, frames, width // 2)
    wide_half = pl.BlockSpec((half, width // 2), lambda i, *_: (i, 0))
    wide_pair = pl.BlockSpec((2, half, width // 2), lambda i, *_: (0, i, 0))
    wide_heads = pl.BlockSpec((4, half, 3 * LANES), lambda i, *_: (0, i, 0))
    half_spec = pl.BlockSpec((fourth, width // 2), lambda i, *_: (i, 0))
    pair_spec = pl.BlockSpec((2, fourth, width // 2), lambda i, *_: (0, i, 0))
    first, y_out, z_out, keep_left, keep_right = call(
        back_project_kernel,
        "back_project",
        2,
        [wide_heads] * 2 + [whole(*w_heads.shape)] * 2,
        [wide_slab, wide_pair, wide_pair, wide_half, wide_half],
        (
            like((frames, width), wide),
            like(pair, low),
            like(pair, low),
            like(pair[1:], wide),
            like(pair[1:], wide),
        ),
        scratch=[pltpu.VMEM((4, half, width), wide)],
        flops=2 * 4 * frames * width * 6 * LANES,
    )(
        ids,
        grad_qkv.reshape(heads_shape),
        grad_qkv_came.reshape(heads_shape),
        w_heads,
        w_other,
    )
    y_came, z_came = hop_seq(y_out, 1), hop_seq(z_out, 2)

    first_sums = call(
        first_sums_kernel,
        "first_sums",
        4,
        [slab, pair_spec, pair_spec, half_spec, half_spec, natural_slab, whole(16, width)],
        whole(8, width),
        like((8, width), wide),
    )(
        ids,
        first,
        y_out,
        z_out,
        keep_left,
        keep_right,
        natural.reshape(4, frames, width),
        vectors,
    )
    y_came = after(y_came, first_sums)
    ups = jnp.zeros((4, width), wide)
    ups = lax.dynamic_update_slice(ups, up_sums[:2], (2 * core, 0))
    sums = jnp.concatenate([first_sums[:2], middle_sums[:4], ups, jnp.zeros((6, width), wide)])
    sums = sums.reshape(16, 8, 1, part).transpose(1, 2, 0, 3)
    sums = jnp.broadcast_to(sums, (8, 4, 16, part)).reshape(32, 16, part)

    heads_out = like((width, 3 * LANES), low)
    grad_heads = call(
        grad_heads_kernel,
        "grad_heads",
        2,
        [
            pl.BlockSpec((4 * frames, 4 * part), lambda i, *_: (0, i)),
            whole(4 * frames, 3 * LANES),
        ],
        pl.BlockSpec((4 * part, 3 * LANES), lambda i, *_: (i, 0)),
        like((width, 3 * LANES), low),
        flops=2 * 4 * frames * width * 3 * LANES,
    )
    heads_leaving = grad_heads(ids, after(natural, z_out), grad_qkv_came)
    heads_kept = grad_heads(ids, after(natural, z_out), grad_qkv)
    heads_came = hop_batch(heads_leaving, 1)
    heads_sum = (heads_kept.astype(wide) + heads_came.astype(wide)).astype(low)
    heads_came = hop_batch(heads_sum, 2)
    down = after(down, z_out)
    down_x = hop_batch(down, 2)
    down = (down.astype(wide) + down_x.astype(wide)).astype(low)
    y_came = after(y_came, heads_sum, down)
    down_came = hop_batch(down, 1)

    z_second, y_second = call(
        second_kernel,
        "second",
        1,
        [whole(*pair[1:])] * 2 + [whole(*pair)] * 2,
        [whole(*pair[1:])] * 2,
        (like(pair[1:], low), like(pair[1:], low)),
    )(ids, keep_left, keep_right, y_came, z_came)
    z_last, y_last = hop_seq(z_second, 2), hop_seq(y_second, 1)
    sums = lax.all_to_all(after(sums, z_second), ("seq", "batch"), 0, 0, tiled=True)
    sums = jnp.sum(sums, axis=0)
    grad_inputs = call(
        last_kernel,
        "last",
        2,
        [wide_slab, wide_pair, wide_pair, wide_half, wide_half]
        + [wide_slab, wide_slab, whole(16, width)],
        wide_slab,
        like((frames, width), low),
    )(ids, after(first, mixed, sums), y_came, z_came, z_last, y_last, tokens_here, grad_middle, vectors)
    mixed_x = hop_batch(mixed, 2)
    grad_inputs = swap_halves(grad_inputs[None])

    heads_sum = (
        after(heads_sum, z_last, y_last).astype(wide) + heads_came.astype(wide)
    ).astype(low)
    heads_sum = lax.all_to_all(
        heads_sum.reshape(8, part, 3 * LANES), "seq", 0, 0, tiled=True
    ).astype(wide)
    heads_sum = (heads_sum[:4] + heads_sum[4:]).astype(low)
    heads_came = hop_batch(heads_sum, 1)
    mixed_core, mixed_both = hop_batch(mixed, 1), hop_batch(mixed_x, 1)
    grad_qkv_w, grad_out_w, grad_up_w, grad_down_w = call(
        spread_kernel,
        "spread",
        1,
        [whole(4, part, 3 * LANES)] * 2
        + [whole(2 * part, width)] * 2
        + [whole(part, width + width // 4)] * 4,
        [
            whole(part, 3 * width),
            whole(part, width),
            whole(part, 4 * width),
            whole(4 * part, width),
        ],
        (
            like((part, 3 * width), wide),
            like((part, width), wide),
            like((part, 4 * width), wide),
            like((4 * part, width), wide),
        ),
    )(ids, heads_sum, heads_came, down, down_came, mixed, mixed_x, mixed_core, mixed_both)

    grad_inputs = after(grad_inputs, grad_qkv_w)
    return (
        result_home,
        grad_inputs,
        grad_qkv_w,
        grad_out_w,
        grad_up_w,
        grad_down_w,
        sums[0],
        sums[1],
        sums[2],
        sums[3],
        sums[4],
        sums[6:10].reshape(4 * LANES),
        sums[5],
    )


def solution(mesh):
    square = mesh.shape["seq"] == 8 and mesh.shape["batch"] == 4
    return jax.shard_map(
        square_shards if square else shards,
        mesh=mesh,
        in_specs=(
            P("batch", "seq", None),
            P("batch", None),
            P("batch", None),
            P("batch", "seq", None),
            P("seq", None),
            P("seq", None),
            P("seq", None),
            P("seq", None),
            P("seq"),
            P("seq"),
            P("seq"),
            P("seq"),
            P("seq"),
            P("seq"),
            P("seq"),
        ),
        out_specs=(
            P("batch", "seq", None),
            P("batch", "seq", None),
            P("seq", None),
            P("seq", None),
            P("seq", None),
            P("seq", None),
            P("seq"),
            P("seq"),
            P("seq"),
            P("seq"),
            P("seq"),
            P("seq"),
            P("seq"),
        ),
        check_vma=False,
    )
```
